32 devices in a mesh: slab: 2 (over x), blk: 16 (over z, y, core).
Axes of the slice: x: 2, y: 2, z: 4, core: 2. Of those that a mesh axis runs over, the one named last changes fastest.
Arguments:
- transmit: bfloat16 [2, 1024, 2048], P('slab', 'blk'), may hold values from -0.125 to 0.125
- reflect: bfloat16 [2, 2, 1024, 2048], P('slab', None, 'blk'), may hold values from -0.07910156 to 0.07910156
- source_amp: bfloat16 [512, 2048], P('blk'), may hold values from -6 to 6
- source_cell: int32 [512], P('blk'), may hold values from 0 to 1023
- source_slab: int32 [512], P('blk'), may hold values from 0 to 1
Outputs:
- sweep_out: float32 [2, 512, 2048], P('slab', 'blk')
The draws below stay inside these ranges and needn't reach their ends.
All inputs are finite; a program needn't handle non-finite values.
Results may differ from the reference program's by a relative error of at most 0.018.
Values may be sent and summed in bfloat16 or wider, within the bound.
A program may use at most 64 MiB of HBM per device.

```python
import jax
import jax.numpy as jnp
from jax import lax

N = 1024
SLABS = 2
SOURCES = 512
WIDTH = 256


def set_ends(entries, stream_key, least, top_value):
    longest = entries.shape.index(max(entries.shape))
    spots = []
    for shift in (0, 1):
        where = [jax.random.randint(jax.random.fold_in(stream_key, axis), (), 0, length) for axis, length in enumerate(entries.shape)]
        where[longest] = (where[longest] + shift) % entries.shape[longest]
        spots.append(tuple(where))
    return entries.at[spots[0]].set(least).at[spots[1]].set(top_value)


def level_of(stream_key, extent, cuts, smallest, high):
    loudness = 1.0
    for position, blocks in cuts:
        heights = jax.random.uniform(jax.random.fold_in(jax.random.fold_in(stream_key, 6), position), (blocks,), jnp.float32, smallest / len(cuts), high / len(cuts))
        loudness = loudness * jnp.repeat(jnp.exp(heights), extent[position] // blocks).reshape((-1,) + (1,) * (len(extent) - 1 - position))
    return loudness


def bell_draw(own_key, shape, scale, limit, cuts=(), kind=jnp.bfloat16):
    values = jax.random.normal(own_key, shape, jnp.float32) * scale
    if len(cuts) > 0:
        values = level_of(own_key, shape, cuts, -0.22, 0.18) * values
    return jnp.clip(values, min=-limit, max=limit).astype(kind)


def setup_inputs(seed: int = 0) -> dict:
    key_of = jax.random.split(jax.random.key(seed), 6)
    transmit = bell_draw(key_of[0], (SLABS, N, 2 * N), (2 * N) ** -0.5, 0.125, ((0, 2), (1, 16)))
    reflect = bell_draw(key_of[1], (SLABS, 2, N, 2 * N), (0.6 / (2 * N) ** 0.5), 0.07910156, ((0, 2), (2, 16)))
    source_amp = bell_draw(key_of[2], (SOURCES, 2 * N), 1.0, 6.0, ((0, 16),))
    source_cell = set_ends(jax.random.randint(key_of[3], (SOURCES,), 0, N), jax.random.fold_in(key_of[3], 1), 0, N - 1).astype(jnp.int32)
    source_slab = set_ends(jax.random.randint(key_of[4], (SOURCES,), 0, SLABS), jax.random.fold_in(key_of[4], 1), 0, SLABS - 1).astype(jnp.int32)
    return {"transmit": transmit, "reflect": reflect, "source_amp": source_amp, "source_cell": source_cell, "source_slab": source_slab}


def pair_form(matrix):
    half_width = matrix.shape[0]
    real_part = matrix[:, :half_width]
    imag_part = matrix[:, half_width:]
    return jnp.concatenate([matrix, jnp.concatenate([-imag_part, real_part], 1)], 0)


def transposed(matrix):
    half_width = matrix.shape[0]
    return jnp.concatenate([matrix[:, :half_width].T, matrix[:, half_width:].T], 1)


def complex_product(left_rows, right_matrix):
    return jnp.dot(left_rows, pair_form(right_matrix), preferred_element_type=jnp.float32)


def reference(transmit, reflect, source_amp, source_cell, source_slab):
    cell_index = jnp.arange(N, dtype=jnp.int32)
    offset = (cell_index[None, :] - source_cell[:, None].astype(jnp.int32)) % N
    inside = offset < WIDTH
    inside = jnp.concatenate([inside, inside], 1)
    slab_maps = []
    for slab_number in range(SLABS):
        coupling = complex_product(reflect[slab_number, 0], reflect[slab_number, 1]).astype(jnp.bfloat16)
        through = transmit[slab_number]
        slab_maps.append((through.astype(jnp.float32) + complex_product(coupling, through)).astype(jnp.bfloat16))
    forward = []
    carried = jnp.zeros((SOURCES, 2 * N), jnp.bfloat16)
    for slab_number in range(SLABS):
        keep = inside & (source_slab == slab_number)[:, None]
        forcing = jnp.where(keep, source_amp, jnp.zeros_like(source_amp))
        carried = (forcing.astype(jnp.float32) + jnp.dot(carried, pair_form(slab_maps[slab_number]), preferred_element_type=jnp.float32)).astype(jnp.bfloat16)
        forward.append(carried)
    current = forward[SLABS - 1].astype(jnp.float32)
    backward = [current]
    for slab_number in range(SLABS - 2, -1, -1):
        operand = current.astype(jnp.bfloat16)
        message = jnp.dot(operand, pair_form(transposed(slab_maps[slab_number + 1])), preferred_element_type=jnp.float32).astype(jnp.bfloat16)
        message = lax.optimization_barrier(message)
        current = forward[slab_number].astype(jnp.float32) + message.astype(jnp.float32)
        backward.append(current)
    return jnp.stack(backward[::-1])
```

```python
import functools

import jax
import jax.numpy as jnp
from jax import lax
from jax.experimental import pallas as pl
from jax.experimental.pallas import tpu as pltpu
from jax.sharding import PartitionSpec as P


def shifted(block, axis, distance):
    devices = range(lax.axis_size(axis))
    route = [(i - distance, i) for i in devices if i - distance in devices]
    return lax.ppermute(block, axis, route)


def transposed(matrix):
    half_width = matrix.shape[0]
    return jnp.concatenate([matrix[:, :half_width].T, matrix[:, half_width:].T], 1)


def complex_rows(left_rows, right_matrix):
    inner_width = right_matrix.shape[0]
    outer_width = right_matrix.shape[1] // 2
    row_count = left_rows.shape[0]
    stacked = jnp.concatenate([left_rows[:, :inner_width], left_rows[:, inner_width:]], 0)
    product = jnp.dot(stacked, right_matrix, preferred_element_type=jnp.float32)
    real_out = product[:row_count, :outer_width] - product[row_count:, outer_width:]
    imag_out = product[:row_count, outer_width:] + product[row_count:, :outer_width]
    return jnp.concatenate([real_out, imag_out], 1)


def body(transmit, reflect, source_amp, source_cell, source_slab):
    trans_local = transmit[0]
    refl_local = reflect[0]
    half_width = source_amp.shape[1] // 2
    refl_second = lax.all_gather(refl_local[1], "blk", axis=0, tiled=True)
    coupling = complex_rows(refl_local[0], refl_second).astype(jnp.bfloat16)
    start_rows = trans_local.astype(jnp.float32)
    piece_rows = lax.all_gather(trans_local, "blk", axis=0, tiled=True)
    piece_count = piece_rows.shape[0]
    real_cols = lax.slice_in_dim(coupling, 0, piece_count, axis=1)
    imag_cols = lax.dynamic_slice_in_dim(coupling, half_width, piece_count, 1)
    left_rows = jnp.concatenate([real_cols, imag_cols], 1)
    joined = (start_rows + complex_rows(left_rows, piece_rows)).astype(jnp.bfloat16)
    slab_matrix = lax.all_gather(joined, "blk", axis=0, tiled=True)
    back_matrix = transposed(slab_matrix)
    cell_index = lax.iota(jnp.int32, half_width)
    offset = (cell_index[None, :] - source_cell[:, None]) % half_width
    inside = offset < half_width // 4
    here = source_slab == lax.axis_index("slab")
    keep = inside & here[:, None]
    keep = jnp.concatenate([keep, keep], 1)
    forcing = jnp.where(keep, source_amp, jnp.zeros_like(source_amp))
    chain_length = lax.axis_size("slab")
    carried = forcing
    for sweep_step in range(chain_length - 1):
        arrived = shifted(carried, "slab", 1)
        carried = (forcing.astype(jnp.float32) + complex_rows(arrived, slab_matrix)).astype(
            jnp.bfloat16
        )
    current = carried.astype(jnp.float32)
    for sweep_step in range(chain_length - 1):
        message = complex_rows(current.astype(jnp.bfloat16), back_matrix).astype(jnp.bfloat16)
        arrived = shifted(message, "slab", -1)
        current = carried.astype(jnp.float32) + arrived.astype(jnp.float32)
    return current[None]


MESH = pl.DeviceIdType.MESH
Y = 2
CORE = 2
PLANES = 2


def pair_kernel(
    outer, t_hbm, r_hbm, amp_hbm, cell_hbm, slab_hbm, out_ref,
    amp_ref, cell_ref, slab_ref, g_ref, left_ref, coup_ref, x_ref, base_ref,
    f_ref, whole_ref, d_ref, far_ref,
    arg_sem, in_send, in_recv, left_send, left_recv, z_send, z_recv,
    c_send, c_recv, x_send, x_recv, f_send, f_recv, d_send, d_recv,
):
    plane = lax.axis_index("slab")
    me = lax.axis_index("blk")
    z, y, core = me // (Y * CORE), (me // CORE) % Y, me % CORE
    last = PLANES - 1
    depth = t_hbm.shape[1]
    width = t_hbm.shape[2] // 2
    part_width = width // (PLANES * Y)
    sources = amp_hbm.shape[0]
    y_peer, c_peer, x_peer = 1 - y, 1 - core, 1 - plane
    q = plane * Y + y
    f32, bf16 = jnp.float32, jnp.bfloat16

    def dev(p, zz, yy, cc):
        return (p, (zz * Y + yy) * CORE + cc)

    def cols(quarter, base=0):
        return pl.ds(pl.multiple_of(base + quarter * part_width, part_width), part_width)

    def remote(s, d, ss, rs, to):
        return pltpu.make_async_remote_copy(
            src_ref=s, dst_ref=d, send_sem=ss, recv_sem=rs, device_id=to, device_id_type=MESH)

    def piece(m, part, p, yy):
        s = r_hbm.at[0, 1] if m == 0 else t_hbm.at[0]
        return s.at[:, cols(p * Y + yy, part * width)]

    def slot(m, part, yy):
        return g_ref.at[m, part].at[z * Y + yy, core]

    def piece_local(m, part):
        return pltpu.make_async_copy(piece(m, part, last, y), slot(m, part, y), in_recv.at[(m * 2 + part) * Y + y])

    targets = ((0, y), (0, y_peer), (last, y_peer))

    def piece_send(m, part, k):
        p, yy = targets[k]
        return remote(piece(m, part, p, yy), slot(m, part, y), in_send.at[m, part, k],
                      in_recv.at[(m * 2 + part) * Y + y], dev(p, z, yy, core))

    def piece_recv(m, part, yy):
        return remote(slot(m, part, yy), slot(m, part, yy), in_send.at[m, part, 0],
                      in_recv.at[(m * 2 + part) * Y + yy], dev(plane, z, y_peer, core))

    def left_src(part):
        return r_hbm.at[0, 0, :, part * width:(part + 1) * width]

    def left_local(part):
        return pltpu.make_async_copy(left_src(part), left_ref.at[part].at[y], left_recv.at[part * Y + y])

    def left_push(part, k):
        to = dev(0, z, y, core) if k == 0 else dev(last, z, y_peer, core)
        return remote(left_src(part), left_ref.at[part].at[y], left_send.at[part, k],
                      left_recv.at[part * Y + y], to)

    def left_relay(part, yy):
        ref = left_ref.at[part].at[yy]
        return remote(ref, ref, left_send.at[part, 0], left_recv.at[part * Y + yy],
                      dev(plane, z, y_peer, core))

    args = [pltpu.make_async_copy(a, b, arg_sem.at[i]) for i, (a, b) in enumerate(
        ((amp_hbm, amp_ref), (cell_hbm, cell_ref), (slab_hbm, slab_ref)))]
    for copy in args:
        copy.start()

    @pl.when(plane == last)
    def _():
        for m in range(2):
            for part in range(2):
                piece_local(m, part).start()
        for part in range(2):
            left_local(part).start()

    barrier = pltpu.get_barrier_semaphore()
    peers = [dev(plane, (z + step) % outer, y, core) for step in range(1, outer)]
    peers += [dev(plane, z, y, c_peer), dev(plane, z, y_peer, core),
              dev(x_peer, z, y, core), dev(x_peer, z, y_peer, core)]
    for peer in peers:
        pl.semaphore_signal(barrier, inc=1, device_id=peer, device_id_type=MESH)
    pl.semaphore_wait(barrier, len(peers))

    @pl.when(plane == last)
    def _():
        for part in range(2):
            for k in range(3):
                piece_send(0, part, k).start()
        for part in range(2):
            for k in range(2):
                left_push(part, k).start()
        for part in range(2):
            for k in range(3):
                piece_send(1, part, k).start()

    def pieces_ready(m):
        for part in range(2):
            @pl.when(plane == last)
            def _():
                piece_local(m, part).wait()

            @pl.when(plane != last)
            def _():
                piece_recv(m, part, y).wait_recv()

            piece_recv(m, part, y_peer).wait_recv()

    pending = []
    always = plane >= 0
    steps = [s for d in range(1, outer) for s in (d, -d)]
    near = [s for s in steps if abs(s) <= 2]

    def chunk(m, zz, cc):
        return g_ref.at[m].at[:, pl.ds(zz * Y, Y), cc]

    def push(m, k, shift, to, ok):
        zz = z + shift
        ref = chunk(m, zz, core)
        copy = remote(ref, ref, z_send.at[m, k], z_recv.at[(m * outer + zz) * CORE + core], to)
        copy.start()
        pending.append((ok, m, k, shift))

    def landed(m, zz, cc):
        ref = chunk(m, zz, cc)
        remote(ref, ref, z_send.at[m, 0], z_recv.at[(m * outer + zz) * CORE + cc],
               dev(plane, z, y, c_peer)).wait_recv()

    def valid(zz):
        return (zz >= 0) & (zz < outer)

    def spread_own(m):
        for k, s in enumerate(sorted(near, key=lambda v: -abs(v))):
            ok = valid(z + s)

            @pl.when(ok)
            def _():
                push(m, k, 0, dev(plane, z + s, y, core), ok)
        push(m, 4, 0, dev(plane, z, y, c_peer), always)

    def spread(m, chosen):
        for s in chosen:
            i = steps.index(s)
            ok = valid(z + s)

            @pl.when(ok)
            def _():
                landed(m, z + s, core)
            if abs(s) >= 2:
                onward = 1 if s < 0 else -1
                both = ok & valid(z + onward)

                @pl.when(both)
                def _():
                    push(m, 5 + len(steps) + i, s, dev(plane, z + onward, y, core), both)

            @pl.when(ok)
            def _():
                push(m, 5 + i, s, dev(plane, z, y, c_peer), ok)

    def finish(m):
        for zz in range(outer):
            landed(m, zz, c_peer)

    def side(m, part):
        return g_ref[m, part].reshape(width, part_width)

    def complex_rows_here(lhs, m):
        n = lhs.shape[0] // 2
        pr = jnp.dot(lhs, side(m, 0), preferred_element_type=f32)
        pi = jnp.dot(lhs, side(m, 1), preferred_element_type=f32)
        return pr[:n] - pi[n:], pi[:n] + pr[n:]

    seconds = [s for s in steps if abs(s) == 2]
    firsts = [s for s in steps if abs(s) == 1]
    rest = [s for s in steps if abs(s) > 2]

    for copy in args:
        copy.wait()
    eye = (lax.broadcasted_iota(jnp.int32, (sources, sources), 0)
           == lax.broadcasted_iota(jnp.int32, (sources, sources), 1))
    cell = jnp.sum(jnp.where(eye, cell_ref[...], 0), axis=1, keepdims=True)
    slab = jnp.sum(jnp.where(eye, slab_ref[...], 0), axis=1, keepdims=True)
    offset = lax.broadcasted_iota(jnp.int32, (sources, width), 1) - cell
    offset = jnp.where(offset < 0, offset + width, offset)
    inside = offset < width // 4
    for part in range(2):
        amp = amp_ref[:, part * width:(part + 1) * width].astype(f32)
        x_ref[part, y] = jnp.where(inside & (slab == 0), amp, 0.0).astype(bf16)
        base_ref[part, y] = jnp.where(inside & (slab == 1), amp, 0.0).astype(bf16)

    pieces_ready(0)
    spread_own(0)

    def x_swap(yy):
        ref = x_ref.at[:, yy]
        return remote(ref, ref, x_send.at[0], x_recv.at[0], dev(plane, z, y_peer, core))

    def base_swap(yy, quarter):
        ref = base_ref.at[:, yy, :, cols(quarter)]
        return remote(ref, ref, x_send.at[1], x_recv.at[1], dev(plane, z, y_peer, core))

    x_swap(y).start()
    base_swap(y, plane * Y + y_peer).start()

    for part in range(2):
        @pl.when(plane == last)
        def _():
            left_local(part).wait()

        @pl.when(plane != last)
        def _():
            left_relay(part, y).wait_recv()
            left_relay(part, y).start()

    spread(0, seconds)
    pieces_ready(1)
    spread_own(1)
    spread(0, firsts + rest)
    finish(0)
    for part in range(2):
        left_relay(part, y_peer).wait_recv()

    re, im = complex_rows_here(left_ref[...].reshape(2 * Y * depth, width), 0)
    coup_ref[0:Y * depth, cols(q)] = re.astype(bf16)
    coup_ref[Y * depth:, cols(q)] = im.astype(bf16)
    others = ((x_peer, y), (plane, y_peer), (x_peer, y_peer))

    def coup_copy(k, quarter):
        p, yy = others[k]
        ref = coup_ref.at[:, cols(quarter)]
        return remote(ref, ref, c_send.at[k], c_recv.at[quarter], dev(p, z, yy, core))

    for k in range(3):
        coup_copy(k, q).start()
    spread(1, seconds + firsts + rest)
    finish(1)
    for k, (p, yy) in enumerate(others):
        coup_copy(k, p * Y + yy).wait_recv()

    re, im = complex_rows_here(coup_ref[...], 1)
    for part, value in ((0, re), (1, im)):
        start = g_ref[1, part, pl.ds(z * Y, Y), core].reshape(Y * depth, part_width)
        joined = (value + start.astype(f32)).astype(bf16)
        g_ref[2, part, pl.ds(z * Y, Y), core] = joined.reshape(Y, depth, part_width)
    spread_own(2)
    spread(2, seconds + firsts + rest)
    x_swap(y_peer).wait_recv()
    base_swap(y_peer, q).wait_recv()
    finish(2)

    re, im = complex_rows_here(x_ref[...].reshape(2 * Y * sources, width), 2)
    for part, value in ((0, re), (1, im)):
        start = base_ref[part, :, :, cols(q)].astype(f32)
        f_ref[part] = (value.reshape(Y, sources, part_width) + start).astype(bf16)

    lhs = f_ref[...].reshape(2 * Y * sources, part_width)
    n = Y * sources
    tile = Y * CORE * depth

    def d_copy(k, yy, quarter, j):
        spots = slice(j * tile, (j + 1) * tile)
        return remote(d_ref.at[:, yy, :, spots], far_ref.at[quarter].at[:, :, spots],
                      d_send.at[k, j], d_recv.at[quarter * outer + j], dev(0, z, yy, core))

    def f_copy(k, yy, quarter):
        return remote(f_ref.at[:, yy], whole_ref.at[:, :, cols(quarter)], f_send.at[k],
                      f_recv.at[quarter], dev(last, z, yy, core))

    for j in range(outer):
        spots = slice(j * tile, (j + 1) * tile)
        dims = (((1,), (1,)), ((), ()))
        right = [g_ref[2, part, j * Y:(j + 1) * Y].reshape(tile, part_width) for part in range(2)]
        pr = lax.dot_general(lhs, right[0], dims, preferred_element_type=f32)
        pi = lax.dot_general(lhs, right[1], dims, preferred_element_type=f32)
        d_ref[0, :, :, spots] = (pr[:n] - pi[n:]).astype(bf16).reshape(Y, sources, tile)
        d_ref[1, :, :, spots] = (pi[:n] + pr[n:]).astype(bf16).reshape(Y, sources, tile)
        d_copy(0, y_peer, q, j).start()

        @pl.when(plane == last)
        def _():
            d_copy(1, y, q, j).start()

    f_copy(0, y_peer, q).start()

    @pl.when(plane != last)
    def _():
        f_copy(1, y, q).start()

    @pl.when(plane == last)
    def _():
        for m in range(2):
            for part in range(2):
                for k in range(3):
                    piece_send(m, part, k).wait_send()
        for part in range(2):
            for k in range(2):
                left_push(part, k).wait_send()

    @pl.when(plane != last)
    def _():
        for part in range(2):
            left_relay(part, y).wait_send()

    x_swap(y).wait_send()
    base_swap(y, plane * Y + y_peer).wait_send()
    for k in range(3):
        coup_copy(k, q).wait_send()
    for ok, m, k, shift in pending:
        @pl.when(ok)
        def _():
            ref = chunk(m, z + shift, core)
            remote(ref, ref, z_send.at[m, k], z_recv.at[(m * outer + z + shift) * CORE + core],
                   dev(plane, z, y, c_peer)).wait_send()

    @pl.when(plane == last)
    def _():
        whole_ref[:, :, cols(q)] = f_ref[:, y]
        for p, yy in others:
            f_copy(0, y, p * Y + yy).wait_recv()
        for part in range(2):
            out_ref[:, part * width:(part + 1) * width] = whole_ref[part].astype(f32)

    @pl.when(plane != last)
    def _():
        for j in range(outer):
            spots = slice(j * tile, (j + 1) * tile)
            for p, yy in others:
                d_copy(0, y, p * Y + yy, j).wait_recv()
            for part in range(2):
                total = d_ref.at[part][y, :, spots].astype(f32)
                for p, yy in others:
                    total = total + far_ref.at[p * Y + yy][part, :, spots].astype(f32)
                out_ref[:, part * width + j * tile:part * width + (j + 1) * tile] = (
                    x_ref.at[part][y, :, spots].astype(f32) + total.astype(bf16).astype(f32))

    @pl.when(plane == last)
    def _():
        for j in range(outer):
            d_copy(1, y, q, j).wait_send()

    @pl.when(plane != last)
    def _():
        f_copy(1, y, q).wait_send()

    for j in range(outer):
        d_copy(0, y_peer, q, j).wait_send()
    f_copy(0, y_peer, q).wait_send()


def pair_body(transmit, reflect, source_amp, source_cell, source_slab):
    outer = lax.axis_size("blk") // (Y * CORE)
    sources, double = source_amp.shape
    depth = transmit.shape[1]
    width = double // 2
    quarter = width // (PLANES * Y)
    bf16 = jnp.bfloat16
    hbm = pl.BlockSpec(memory_space=pltpu.HBM)
    sem = pltpu.SemaphoreType.DMA
    out = pl.pallas_call(
        functools.partial(pair_kernel, outer),
        out_shape=pltpu.VMEM((sources, double), jnp.float32),
        in_specs=[hbm] * 5,
        out_specs=pl.BlockSpec(memory_space=pltpu.VMEM),
        scratch_shapes=[
            pltpu.VMEM((sources, double), bf16),
            pltpu.VMEM((1, sources), jnp.int32),
            pltpu.VMEM((1, sources), jnp.int32),
            pltpu.VMEM((3, 2, outer * Y, CORE, depth, quarter), bf16),
            pltpu.VMEM((2, Y, depth, width), bf16),
            pltpu.VMEM((2 * Y * depth, width), bf16),
            pltpu.VMEM((2, Y, sources, width), bf16),
            pltpu.VMEM((2, Y, sources, width), bf16),
            pltpu.VMEM((2, Y, sources, quarter), bf16),
            pltpu.VMEM((2, sources, width), bf16),
            pltpu.VMEM((2, Y, sources, width), bf16),
            pltpu.VMEM((PLANES * Y, 2, sources, width), bf16),
            sem((3,)),
            sem((2, 2, 3)),
            sem((2 * 2 * Y,)),
            sem((2, 2)),
            sem((2 * Y,)),
            sem((3, 5 + 4 * (outer - 1))),
            sem((3 * outer * CORE,)),
            sem((3,)),
            sem((PLANES * Y,)),
            sem((2,)),
            sem((2,)),
            sem((2,)),
            sem((PLANES * Y,)),
            sem((2, outer)),
            sem((PLANES * Y * outer,)),
        ],
        compiler_params=pltpu.CompilerParams(
            collective_id=0, has_side_effects=True, vmem_limit_bytes=32 << 20),
    )(*(pltpu.with_memory_space_constraint(a, pltpu.HBM) for a in (
        transmit, reflect, source_amp, source_cell[None], source_slab[None])))
    return out[None]


def solution(mesh):
    pair = mesh.shape["slab"] == PLANES and mesh.shape["blk"] % (Y * CORE) == 0
    return jax.shard_map(
        pair_body if pair else body,
        mesh=mesh,
        in_specs=(
            P("slab", "blk", None),
            P("slab", None, "blk", None),
            P("blk", None),
            P("blk"),
            P("blk"),
        ),
        out_specs=P("slab", "blk", None),
        check_vma=False,
    )
```

```python
import functools

import jax
import jax.numpy as jnp
from jax import lax
from jax.experimental import pallas as pl
from jax.experimental.pallas import tpu as pltpu
from jax.sharding import PartitionSpec as P


def shifted(block, axis, distance):
    devices = range(lax.axis_size(axis))
    route = [(i - distance, i) for i in devices if i - distance in devices]
    return lax.ppermute(block, axis, route)


def transposed(matrix):
    half_width = matrix.shape[0]
    return jnp.concatenate([matrix[:, :half_width].T, matrix[:, half_width:].T], 1)


def complex_rows(left_rows, right_matrix):
    inner_width = right_matrix.shape[0]
    outer_width = right_matrix.shape[1] // 2
    row_count = left_rows.shape[0]
    stacked = jnp.concatenate([left_rows[:, :inner_width], left_rows[:, inner_width:]], 0)
    product = jnp.dot(stacked, right_matrix, preferred_element_type=jnp.float32)
    real_out = product[:row_count, :outer_width] - product[row_count:, outer_width:]
    imag_out = product[:row_count, outer_width:] + product[row_count:, :outer_width]
    return jnp.concatenate([real_out, imag_out], 1)


def body(transmit, reflect, source_amp, source_cell, source_slab):
    trans_local = transmit[0]
    refl_local = reflect[0]
    half_width = source_amp.shape[1] // 2
    refl_second = lax.all_gather(refl_local[1], "blk", axis=0, tiled=True)
    coupling = complex_rows(refl_local[0], refl_second).astype(jnp.bfloat16)
    start_rows = trans_local.astype(jnp.float32)
    piece_rows = lax.all_gather(trans_local, "blk", axis=0, tiled=True)
    piece_count = piece_rows.shape[0]
    real_cols = lax.slice_in_dim(coupling, 0, piece_count, axis=1)
    imag_cols = lax.dynamic_slice_in_dim(coupling, half_width, piece_count, 1)
    left_rows = jnp.concatenate([real_cols, imag_cols], 1)
    joined = (start_rows + complex_rows(left_rows, piece_rows)).astype(jnp.bfloat16)
    slab_matrix = lax.all_gather(joined, "blk", axis=0, tiled=True)
    back_matrix = transposed(slab_matrix)
    cell_index = lax.iota(jnp.int32, half_width)
    offset = (cell_index[None, :] - source_cell[:, None]) % half_width
    inside = offset < half_width // 4
    here = source_slab == lax.axis_index("slab")
    keep = inside & here[:, None]
    keep = jnp.concatenate([keep, keep], 1)
    forcing = jnp.where(keep, source_amp, jnp.zeros_like(source_amp))
    chain_length = lax.axis_size("slab")
    carried = forcing
    for sweep_step in range(chain_length - 1):
        arrived = shifted(carried, "slab", 1)
        carried = (forcing.astype(jnp.float32) + complex_rows(arrived, slab_matrix)).astype(
            jnp.bfloat16
        )
    current = carried.astype(jnp.float32)
    for sweep_step in range(chain_length - 1):
        message = complex_rows(current.astype(jnp.bfloat16), back_matrix).astype(jnp.bfloat16)
        arrived = shifted(message, "slab", -1)
        current = carried.astype(jnp.float32) + arrived.astype(jnp.float32)
    return current[None]


MESH = pl.DeviceIdType.MESH
Y = 2
CORE = 2
PLANES = 2


def pair_kernel(
    outer, t_hbm, r_hbm, amp_hbm, cell_hbm, slab_hbm, out_ref,
    amp_ref, cell_ref, slab_ref, g_ref, left_ref, coup_ref, x_ref, base_ref,
    f_ref, whole_ref, d_ref, far_ref,
    ready, arg_sem, in_send, in_recv, left_send, left_recv, z_send, z_recv, relay_send,
    core_send, core_recv, c_send, c_recv, x_send, x_recv, f_send, f_recv, d_send, d_recv,
):
    plane = lax.axis_index("slab")
    me = lax.axis_index("blk")
    z, y, core = me // (Y * CORE), (me // CORE) % Y, me % CORE
    last = PLANES - 1
    depth = t_hbm.shape[1]
    half = depth // 2
    width = t_hbm.shape[2] // 2
    part_width = width // (PLANES * Y)
    sources = amp_hbm.shape[0]
    y_peer, c_peer, x_peer = 1 - y, 1 - core, 1 - plane
    q = plane * Y + y
    f32, bf16 = jnp.float32, jnp.bfloat16
    others = ((x_peer, y), (plane, y_peer), (x_peer, y_peer))
    order = (y, y_peer)

    def dev(p, zz, yy, cc):
        return (p, (zz * Y + yy) * CORE + cc)

    def cols(quarter, base=0):
        return pl.ds(pl.multiple_of(base + quarter * part_width, part_width), part_width)

    def remote(s, d, ss, rs, to):
        return pltpu.make_async_remote_copy(
            src_ref=s, dst_ref=d, send_sem=ss, recv_sem=rs, device_id=to, device_id_type=MESH)

    def valid(zz):
        return (zz >= 0) & (zz < outer)

    def unit(m, zz, yy):
        return g_ref.at[m].at[:, zz * Y + yy, core]

    def piece(m, part, p, yy):
        s = r_hbm.at[0, 1] if m == 0 else t_hbm.at[0]
        return s.at[:, cols(p * Y + yy, part * width)]

    def slot(m, part):
        return g_ref.at[m, part].at[z * Y + y, core]

    def piece_local(m, part):
        return pltpu.make_async_copy(piece(m, part, last, y), slot(m, part), in_recv.at[m * Y + y])

    def piece_send(m, part, p, yy):
        return remote(piece(m, part, p, yy), slot(m, part), in_send.at[m],
                      in_recv.at[m * Y + y], dev(p, z, yy, core))

    def piece_wait(m, yy):
        pltpu.make_async_copy(unit(m, z, yy), unit(m, z, yy), in_recv.at[m * Y + yy]).wait()

    left_units = [(part, h) for part in range(2) for h in range(2)]

    def left_rows(part, h, yy):
        return left_ref.at[part].at[yy, h * half:(h + 1) * half]

    def left_src(part, h):
        return r_hbm.at[0, 0, h * half:(h + 1) * half, part * width:(part + 1) * width]

    def left_local(part):
        return pltpu.make_async_copy(
            r_hbm.at[0, 0, :, part * width:(part + 1) * width], left_ref.at[part].at[y], left_recv.at[0])

    def left_push(u, part, h, k):
        to = dev(0, z, y, core) if k == 0 else dev(last, z, y_peer, core)
        return remote(left_src(part, h), left_rows(part, h, y), left_send.at[0],
                      left_recv.at[u if k == 0 else len(left_units)], to)

    def left_relay(u, part, h):
        ref = left_rows(part, h, y)
        return remote(ref, ref, left_send.at[0], left_recv.at[len(left_units)], dev(plane, z, y_peer, core))

    args = [pltpu.make_async_copy(a, b, arg_sem.at[i]) for i, (a, b) in enumerate(
        ((amp_hbm, amp_ref), (cell_hbm, cell_ref), (slab_hbm, slab_ref)))]

    barrier = pltpu.get_barrier_semaphore()
    for p, zz, yy, cc in ((plane, z, y, c_peer), (plane, z, y_peer, core), (x_peer, z, y, core),
                          (x_peer, z, y_peer, core)):
        pl.semaphore_signal(barrier, inc=1, device_id=dev(p, zz, yy, cc), device_id_type=MESH)
    for s in (1, 2):
        @pl.when(valid(z + s))
        def _():
            pl.semaphore_signal(barrier, inc=1, device_id=dev(plane, z + s, y, core), device_id_type=MESH)

    @pl.when(plane == last)
    def _():
        for m in range(2):
            for part in range(2):
                piece_local(m, part).start()
        for part in range(2):
            left_local(part).start()

    for copy in args:
        copy.start()
    pl.semaphore_wait(barrier, 4 + jnp.minimum(z, 2))
    for s in (1, 2):
        @pl.when(valid(z - s))
        def _():
            pl.semaphore_signal(ready.at[s - 1], inc=1, device_id=dev(plane, z - s, y, core),
                                device_id_type=MESH)

    @pl.when(plane == last)
    def _():
        for p, yy in ((0, y), (last, y_peer), (0, y_peer)):
            for part in range(2):
                piece_send(0, part, p, yy).start()
        for u, (part, h) in enumerate(left_units):
            for k in range(2):
                left_push(u, part, h, k).start()
        for p, yy in ((0, y), (last, y_peer), (0, y_peer)):
            for part in range(2):
                piece_send(1, part, p, yy).start()

    steps = [s for d in range(1, outer) for s in (d, -d)]
    relays = [(s, -1 if s > 0 else 1) for s in steps if abs(s) >= 2 and any(
        0 <= zz + s < outer and 0 <= zz + (-1 if s > 0 else 1) < outer for zz in range(outer))]

    def z_sem(m, shift, yy):
        return z_recv.at[(m * (outer - 1) + shift % outer - 1) * Y + yy]

    def near(m, i, yy, shifts):
        for s in shifts:
            @pl.when(valid(z + s))
            def _():
                remote(unit(m, z, yy), unit(m, z, yy), z_send.at[m * Y + i], z_sem(m, -s, yy),
                       dev(plane, z + s, y, core)).start()

    def relay(m, i, yy, r):
        s, onward = relays[r]
        return remote(unit(m, z + s, yy), unit(m, z + s, yy), relay_send.at[(m * Y + i) * len(relays) + r],
                      z_sem(m, s - onward, yy), dev(plane, z + onward, y, core))

    def relay_ok(r):
        s, onward = relays[r]
        return valid(z + s) & valid(z + onward)

    def landed(m, i, yy, d):
        for s in (d, -d):
            @pl.when(valid(z + s))
            def _():
                remote(unit(m, z + s, yy), unit(m, z + s, yy), z_send.at[0], z_sem(m, s, yy),
                       dev(plane, z, y, c_peer)).wait_recv()
        for r, (s, onward) in enumerate(relays):
            if abs(s) == d:
                @pl.when(relay_ok(r))
                def _():
                    relay(m, i, yy, r).start()

    def chunk(m, zz, cc):
        return g_ref.at[m].at[:, pl.ds(zz * Y, Y), cc]

    def core_copy(m, zz, cc):
        return remote(chunk(m, zz, cc), chunk(m, zz, cc), core_send.at[m], core_recv.at[m * outer + zz],
                      dev(plane, z, y, c_peer))

    def share(m, d):
        for s in ((d, -d) if d else (0,)):
            @pl.when(valid(z + s))
            def _():
                core_copy(m, z + s, core).start()

    def finish(m):
        for zz in range(outer):
            core_copy(m, zz, c_peer).wait_recv()

    def side(m, part):
        return g_ref[m, part].reshape(width, part_width)

    def complex_rows_here(lhs, m):
        n = lhs.shape[0] // 2
        pr = jnp.dot(lhs, side(m, 0), preferred_element_type=f32)
        pi = jnp.dot(lhs, side(m, 1), preferred_element_type=f32)
        return pr[:n] - pi[n:], pi[:n] + pr[n:]

    everyone = (-2, 2, -1, 1)

    def ready_wait(s):
        @pl.when(valid(z + s))
        def _():
            pl.semaphore_wait(ready.at[s - 1], 1)

    def first_push():
        near(0, 0, y, (-2, -1))
        ready_wait(1)
        near(0, 0, y, (1,))
        ready_wait(2)
        near(0, 0, y, (2,))

    @pl.when(plane == last)
    def _():
        piece_wait(0, y)
        first_push()
        piece_wait(0, y_peer)
        near(0, 1, y_peer, everyone)
        share(0, 0)
        piece_wait(1, y)
        near(1, 0, y, everyone)
        landed(0, 0, y, 2)
        landed(0, 0, y, 1)
        piece_wait(1, y_peer)
        near(1, 1, y_peer, everyone)
        share(1, 0)
        pltpu.make_async_copy(left_ref.at[:, y], left_ref.at[:, y], left_recv.at[0]).wait()

    for copy in args:
        copy.wait()
    eye = (lax.broadcasted_iota(jnp.int32, (sources, sources), 0)
           == lax.broadcasted_iota(jnp.int32, (sources, sources), 1))
    cell = jnp.sum(jnp.where(eye, cell_ref[...], 0), axis=1, keepdims=True)
    slab = jnp.sum(jnp.where(eye, slab_ref[...], 0), axis=1, keepdims=True)
    offset = lax.broadcasted_iota(jnp.int32, (sources, width), 1) - cell
    offset = jnp.where(offset < 0, offset + width, offset)
    inside = offset < width // 4
    for part in range(2):
        amp = amp_ref[:, part * width:(part + 1) * width].astype(f32)
        x_ref[part, y] = jnp.where(inside & (slab == 0), amp, 0.0).astype(bf16)
        base_ref[part, y] = jnp.where(inside & (slab == 1), amp, 0.0).astype(bf16)

    @pl.when(plane != last)
    def _():
        piece_wait(0, y)
        first_push()
        piece_wait(0, y_peer)
        near(0, 1, y_peer, everyone)
        share(0, 0)
        for u, (part, h) in enumerate(left_units):
            ref = left_rows(part, h, y)
            pltpu.make_async_copy(ref, ref, left_recv.at[u]).wait()
            left_relay(u, part, h).start()
            if u == 2:
                landed(0, 0, y, 2)
        landed(0, 0, y, 1)
        piece_wait(1, y)
        near(1, 0, y, everyone)
        piece_wait(1, y_peer)
        near(1, 1, y_peer, everyone)
        share(1, 0)

    far = range(3, outer)
    landed(0, 1, y_peer, 2)
    share(0, 2)
    landed(0, 1, y_peer, 1)
    share(0, 1)
    for d in far:
        landed(0, 0, y, d)
        landed(0, 1, y_peer, d)
        share(0, d)
    ref = left_ref.at[:, y_peer]
    pltpu.make_async_copy(ref, ref, left_recv.at[len(left_units)]).wait()
    finish(0)

    def x_swap(yy):
        ref = x_ref.at[:, yy]
        return remote(ref, ref, x_send.at[0], x_recv.at[0], dev(plane, z, y_peer, core))

    def base_swap(yy, quarter):
        ref = base_ref.at[:, yy, :, cols(quarter)]
        return remote(ref, ref, x_send.at[1], x_recv.at[1], dev(plane, z, y_peer, core))

    def coup_copy(yy, k, quarter):
        p, to_y = others[k]
        ref = coup_ref.at[yy].at[:, cols(quarter)]
        return remote(ref, ref, c_send.at[yy], c_recv.at[yy * len(others) + k], dev(p, z, to_y, core))

    re, im = complex_rows_here(left_ref[...].reshape(2 * Y * depth, width), 0)
    for yy in range(Y):
        coup_ref[yy, 0:depth, cols(q)] = re[yy * depth:(yy + 1) * depth].astype(bf16)
        coup_ref[yy, depth:, cols(q)] = im[yy * depth:(yy + 1) * depth].astype(bf16)
        for k in range(len(others)):
            coup_copy(yy, k, q).start()

    x_swap(y).start()
    base_swap(y, plane * Y + y_peer).start()
    landed(1, 0, y, 2)
    landed(1, 0, y, 1)
    landed(1, 1, y_peer, 2)
    share(1, 2)
    landed(1, 1, y_peer, 1)
    share(1, 1)
    for d in far:
        landed(1, 0, y, d)
        landed(1, 1, y_peer, d)
        share(1, d)
    finish(1)

    for yy in range(Y):
        for k, (p, from_y) in enumerate(others):
            coup_copy(yy, k, p * Y + from_y).wait_recv()
        re, im = complex_rows_here(coup_ref[yy], 1)
        for part, value in ((0, re), (1, im)):
            start = g_ref[1, part, z * Y + yy, core]
            g_ref[2, part, z * Y + yy, core] = (value + start.astype(f32)).astype(bf16)
        near(2, yy, yy, everyone)
    share(2, 0)
    for d in (2, 1, *far):
        for yy in range(Y):
            landed(2, yy, yy, d)
        share(2, d)
    x_swap(y_peer).wait_recv()
    base_swap(y_peer, q).wait_recv()
    finish(2)

    re, im = complex_rows_here(x_ref[...].reshape(2 * Y * sources, width), 2)
    for part, value in ((0, re), (1, im)):
        start = base_ref[part, :, :, cols(q)].astype(f32)
        f_ref[part] = (value.reshape(Y, sources, part_width) + start).astype(bf16)

    lhs = f_ref[...].reshape(2 * Y * sources, part_width)
    n = Y * sources
    tile = Y * CORE * depth

    def d_copy(to, k, yy, j):
        spots = slice(j * tile, (j + 1) * tile)
        return remote(d_ref.at[:, yy, :, spots], far_ref.at[k].at[:, :, spots],
                      d_send.at[to], d_recv.at[k * outer + j], dev(0, z, yy, core))

    def f_copy(to, k, yy, quarter):
        return remote(f_ref.at[:, yy], whole_ref.at[:, :, cols(quarter)], f_send.at[to],
                      f_recv.at[k], dev(last, z, yy, core))

    for j in range(outer):
        spots = slice(j * tile, (j + 1) * tile)
        dims = (((1,), (1,)), ((), ()))
        right = [g_ref[2, part, j * Y:(j + 1) * Y].reshape(tile, part_width) for part in range(2)]
        pr = lax.dot_general(lhs, right[0], dims, preferred_element_type=f32)
        pi = lax.dot_general(lhs, right[1], dims, preferred_element_type=f32)
        d_ref[0, :, :, spots] = (pr[:n] - pi[n:]).astype(bf16).reshape(Y, sources, tile)
        d_ref[1, :, :, spots] = (pi[:n] + pr[n:]).astype(bf16).reshape(Y, sources, tile)

        @pl.when(plane == last)
        def _():
            d_copy(0, 2, y_peer, j).start()
            d_copy(1, 0, y, j).start()

        @pl.when(plane != last)
        def _():
            d_copy(0, 1, y_peer, j).start()

    @pl.when(plane == last)
    def _():
        f_copy(0, 1, y_peer, q).start()

    @pl.when(plane != last)
    def _():
        f_copy(0, 2, y_peer, q).start()
        f_copy(1, 0, y, q).start()

    def sent(ref, sem):
        remote(ref, ref, sem, sem, dev(plane, z, y, c_peer)).wait_send()

    @pl.when(plane == last)
    def _():
        for m in range(2):
            sent(r_hbm.at[0, 0, :, 0:6 * part_width], in_send.at[m])
        sent(left_ref, left_send.at[0])

    @pl.when(plane != last)
    def _():
        sent(left_ref.at[:, 0], left_send.at[0])

    x_swap(y).wait_send()
    base_swap(y, plane * Y + y_peer).wait_send()
    for yy in range(Y):
        sent(coup_ref.at[yy, :, 0:len(others) * part_width], c_send.at[yy])
    count = sum(valid(z + s).astype(jnp.int32) for s in everyone)
    for m in range(3):
        sent(g_ref.at[m, :, :, 0], core_send.at[m])
        for i in range(Y):
            for total in range(1, 5):
                @pl.when(count == total)
                def _():
                    sent(g_ref.at[m, :, 0:total, 0], z_send.at[m * Y + i])
            for r in range(len(relays)):
                @pl.when(relay_ok(r))
                def _():
                    sent(g_ref.at[m, :, 0, 0], relay_send.at[(m * Y + i) * len(relays) + r])

    @pl.when(plane == last)
    def _():
        whole_ref[:, :, cols(q)] = f_ref[:, y]
        for k, (p, yy) in enumerate(others):
            f_copy(0, k, y, p * Y + yy).wait_recv()
        for part in range(2):
            out_ref[:, part * width:(part + 1) * width] = whole_ref[part].astype(f32)
        sent(d_ref.at[:, 0], d_send.at[0])
        sent(d_ref.at[:, 0], d_send.at[1])
        sent(f_ref.at[:, 0], f_send.at[0])

    @pl.when(plane != last)
    def _():
        for j in range(outer):
            spots = slice(j * tile, (j + 1) * tile)
            for k in range(len(others)):
                d_copy(0, k, y, j).wait_recv()
            for part in range(2):
                total = d_ref.at[part][y, :, spots].astype(f32)
                for k in range(len(others)):
                    total = total + far_ref[k, part, :, spots].astype(f32)
                out_ref[:, part * width + j * tile:part * width + (j + 1) * tile] = (
                    x_ref.at[part][y, :, spots].astype(f32) + total.astype(bf16).astype(f32))
        sent(d_ref.at[:, 0], d_send.at[0])
        sent(f_ref.at[:, 0], f_send.at[0])
        sent(f_ref.at[:, 0], f_send.at[1])


def pair_body(transmit, reflect, source_amp, source_cell, source_slab):
    outer = lax.axis_size("blk") // (Y * CORE)
    sources, double = source_amp.shape
    depth = transmit.shape[1]
    width = double // 2
    quarter = width // (PLANES * Y)
    bf16 = jnp.bfloat16
    hbm = pl.BlockSpec(memory_space=pltpu.HBM)
    sem = pltpu.SemaphoreType.DMA
    out = pl.pallas_call(
        functools.partial(pair_kernel, outer),
        out_shape=pltpu.VMEM((sources, double), jnp.float32),
        in_specs=[hbm] * 5,
        out_specs=pl.BlockSpec(memory_space=pltpu.VMEM),
        scratch_shapes=[
            pltpu.VMEM((sources, double), bf16),
            pltpu.VMEM((1, sources), jnp.int32),
            pltpu.VMEM((1, sources), jnp.int32),
            pltpu.VMEM((3, 2, outer * Y, CORE, depth, quarter), bf16),
            pltpu.VMEM((2, Y, depth, width), bf16),
            pltpu.VMEM((Y, 2 * depth, width), bf16),
            pltpu.VMEM((2, Y, sources, width), bf16),
            pltpu.VMEM((2, Y, sources, width), bf16),
            pltpu.VMEM((2, Y, sources, quarter), bf16),
            pltpu.VMEM((2, sources, width), bf16),
            pltpu.VMEM((2, Y, sources, width), bf16),
            pltpu.VMEM((PLANES * Y - 1, 2, sources, width), bf16),
            pltpu.SemaphoreType.REGULAR((2,)),
            sem((3,)),
            sem((2,)),
            sem((2 * Y,)),
            sem((1,)),
            sem((5,)),
            sem((3 * Y,)),
            sem((3 * (outer - 1) * Y,)),
            sem((3 * Y * 2 * max(outer - 3, 1),)),
            sem((3,)),
            sem((3 * outer,)),
            sem((Y,)),
            sem((3 * Y,)),
            sem((2,)),
            sem((2,)),
            sem((2,)),
            sem((3,)),
            sem((2,)),
            sem((3 * outer,)),
        ],
        compiler_params=pltpu.CompilerParams(
            collective_id=0, has_side_effects=True, vmem_limit_bytes=32 << 20),
    )(*(pltpu.with_memory_space_constraint(a, pltpu.HBM) for a in (
        transmit, reflect, source_amp, source_cell[None], source_slab[None])))
    return out[None]


def solution(mesh):
    pair = mesh.shape["slab"] == PLANES and mesh.shape["blk"] % (Y * CORE) == 0
    return jax.shard_map(
        pair_body if pair else body,
        mesh=mesh,
        in_specs=(
            P("slab", "blk", None),
            P("slab", None, "blk", None),
            P("blk", None),
            P("blk"),
            P("blk"),
        ),
        out_specs=P("slab", "blk", None),
        check_vma=False,
    )
```

```python
import functools

import jax
import jax.numpy as jnp
from jax import lax
from jax.experimental import pallas as pl
from jax.experimental.pallas import tpu as pltpu
from jax.sharding import PartitionSpec as P


def shifted(block, axis, distance):
    devices = range(lax.axis_size(axis))
    route = [(i - distance, i) for i in devices if i - distance in devices]
    return lax.ppermute(block, axis, route)


def transposed(matrix):
    half_width = matrix.shape[0]
    return jnp.concatenate([matrix[:, :half_width].T, matrix[:, half_width:].T], 1)


def complex_rows(left_rows, right_matrix):
    inner_width = right_matrix.shape[0]
    outer_width = right_matrix.shape[1] // 2
    row_count = left_rows.shape[0]
    stacked = jnp.concatenate([left_rows[:, :inner_width], left_rows[:, inner_width:]], 0)
    product = jnp.dot(stacked, right_matrix, preferred_element_type=jnp.float32)
    real_out = product[:row_count, :outer_width] - product[row_count:, outer_width:]
    imag_out = product[:row_count, outer_width:] + product[row_count:, :outer_width]
    return jnp.concatenate([real_out, imag_out], 1)


def body(transmit, reflect, source_amp, source_cell, source_slab):
    trans_local = transmit[0]
    refl_local = reflect[0]
    half_width = source_amp.shape[1] // 2
    refl_second = lax.all_gather(refl_local[1], "blk", axis=0, tiled=True)
    coupling = complex_rows(refl_local[0], refl_second).astype(jnp.bfloat16)
    start_rows = trans_local.astype(jnp.float32)
    piece_rows = lax.all_gather(trans_local, "blk", axis=0, tiled=True)
    piece_count = piece_rows.shape[0]
    real_cols = lax.slice_in_dim(coupling, 0, piece_count, axis=1)
    imag_cols = lax.dynamic_slice_in_dim(coupling, half_width, piece_count, 1)
    left_rows = jnp.concatenate([real_cols, imag_cols], 1)
    joined = (start_rows + complex_rows(left_rows, piece_rows)).astype(jnp.bfloat16)
    slab_matrix = lax.all_gather(joined, "blk", axis=0, tiled=True)
    back_matrix = transposed(slab_matrix)
    cell_index = lax.iota(jnp.int32, half_width)
    offset = (cell_index[None, :] - source_cell[:, None]) % half_width
    inside = offset < half_width // 4
    here = source_slab == lax.axis_index("slab")
    keep = inside & here[:, None]
    keep = jnp.concatenate([keep, keep], 1)
    forcing = jnp.where(keep, source_amp, jnp.zeros_like(source_amp))
    chain_length = lax.axis_size("slab")
    carried = forcing
    for sweep_step in range(chain_length - 1):
        arrived = shifted(carried, "slab", 1)
        carried = (forcing.astype(jnp.float32) + complex_rows(arrived, slab_matrix)).astype(
            jnp.bfloat16
        )
    current = carried.astype(jnp.float32)
    for sweep_step in range(chain_length - 1):
        message = complex_rows(current.astype(jnp.bfloat16), back_matrix).astype(jnp.bfloat16)
        arrived = shifted(message, "slab", -1)
        current = carried.astype(jnp.float32) + arrived.astype(jnp.float32)
    return current[None]


MESH = pl.DeviceIdType.MESH
Y = 2
CORE = 2
PLANES = 2


def pair_kernel(
    outer, t_hbm, r_hbm, amp_hbm, cell_hbm, slab_hbm, out_ref,
    amp_ref, cell_ref, slab_ref, g_ref, left_ref, coup_ref, x_ref, base_ref,
    f_ref, whole_ref, d_ref, far_ref,
    ready, arg_sem, in_send, in_recv, left_send, left_recv, z_send, z_recv, relay_send,
    core_send, core_recv, c_send, c_recv, x_send, x_recv, f_send, f_recv, d_send, d_recv,
):
    plane = lax.axis_index("slab")
    me = lax.axis_index("blk")
    z, y, core = me // (Y * CORE), (me // CORE) % Y, me % CORE
    last = PLANES - 1
    depth = t_hbm.shape[1]
    half = depth // 2
    width = t_hbm.shape[2] // 2
    part_width = width // (PLANES * Y)
    sources = amp_hbm.shape[0]
    y_peer, c_peer, x_peer = 1 - y, 1 - core, 1 - plane
    q = plane * Y + y
    f32, bf16 = jnp.float32, jnp.bfloat16
    others = ((x_peer, y), (plane, y_peer), (x_peer, y_peer))
    order = (y, y_peer)

    def dev(p, zz, yy, cc):
        return (p, (zz * Y + yy) * CORE + cc)

    def cols(quarter, base=0):
        return pl.ds(pl.multiple_of(base + quarter * part_width, part_width), part_width)

    def remote(s, d, ss, rs, to):
        return pltpu.make_async_remote_copy(
            src_ref=s, dst_ref=d, send_sem=ss, recv_sem=rs, device_id=to, device_id_type=MESH)

    def valid(zz):
        return (zz >= 0) & (zz < outer)

    def unit(m, zz, yy):
        return g_ref.at[m].at[:, zz * Y + yy, core]

    def piece(m, part, p, yy):
        s = r_hbm.at[0, 1] if m == 0 else t_hbm.at[0]
        return s.at[:, cols(p * Y + yy, part * width)]

    def slot(m, part):
        return g_ref.at[m, part].at[z * Y + y, core]

    def piece_local(m, part):
        return pltpu.make_async_copy(piece(m, part, last, y), slot(m, part), in_recv.at[m * Y + y])

    def piece_send(m, part, p, yy):
        return remote(piece(m, part, p, yy), slot(m, part), in_send.at[m],
                      in_recv.at[m * Y + y], dev(p, z, yy, core))

    def piece_wait(m, yy):
        pltpu.make_async_copy(unit(m, z, yy), unit(m, z, yy), in_recv.at[m * Y + yy]).wait()

    left_units = [(part, h) for part in range(2) for h in range(2)]

    def left_rows(part, h, yy):
        return left_ref.at[part].at[yy, h * half:(h + 1) * half]

    def left_src(part, h):
        return r_hbm.at[0, 0, h * half:(h + 1) * half, part * width:(part + 1) * width]

    def left_local(part):
        return pltpu.make_async_copy(
            r_hbm.at[0, 0, :, part * width:(part + 1) * width], left_ref.at[part].at[y], left_recv.at[0])

    def left_push(u, part, h, k):
        to = dev(0, z, y, core) if k == 0 else dev(last, z, y_peer, core)
        return remote(left_src(part, h), left_rows(part, h, y), left_send.at[0],
                      left_recv.at[u if k == 0 else len(left_units)], to)

    def left_relay(u, part, h):
        ref = left_rows(part, h, y)
        return remote(ref, ref, left_send.at[0], left_recv.at[len(left_units)], dev(plane, z, y_peer, core))

    args = [pltpu.make_async_copy(a, b, arg_sem.at[i]) for i, (a, b) in enumerate(
        ((amp_hbm, amp_ref), (cell_hbm, cell_ref), (slab_hbm, slab_ref)))]

    barrier = pltpu.get_barrier_semaphore()
    for p, zz, yy, cc in ((plane, z, y, c_peer), (plane, z, y_peer, core), (x_peer, z, y, core),
                          (x_peer, z, y_peer, core)):
        pl.semaphore_signal(barrier, inc=1, device_id=dev(p, zz, yy, cc), device_id_type=MESH)
    for s in (1, 2):
        @pl.when(valid(z + s))
        def _():
            pl.semaphore_signal(barrier, inc=1, device_id=dev(plane, z + s, y, core), device_id_type=MESH)

    @pl.when(plane == last)
    def _():
        for m in range(2):
            for part in range(2):
                piece_local(m, part).start()
        for part in range(2):
            left_local(part).start()

    for copy in args:
        copy.start()
    pl.semaphore_wait(barrier, 4 + jnp.minimum(z, 2))
    for s in (1, 2):
        @pl.when(valid(z - s))
        def _():
            pl.semaphore_signal(ready.at[s - 1], inc=1, device_id=dev(plane, z - s, y, core),
                                device_id_type=MESH)

    @pl.when(plane == last)
    def _():
        for p, yy in ((0, y), (last, y_peer), (0, y_peer)):
            for part in range(2):
                piece_send(0, part, p, yy).start()
        for u, (part, h) in enumerate(left_units):
            for k in range(2):
                left_push(u, part, h, k).start()
        for p, yy in ((0, y), (last, y_peer), (0, y_peer)):
            for part in range(2):
                piece_send(1, part, p, yy).start()

    steps = [s for d in range(1, outer) for s in (d, -d)]
    relays = [(s, -1 if s > 0 else 1) for s in steps if abs(s) >= 2 and any(
        0 <= zz + s < outer and 0 <= zz + (-1 if s > 0 else 1) < outer for zz in range(outer))]

    def z_sem(m, shift, yy):
        return z_recv.at[(m * (outer - 1) + shift % outer - 1) * Y + yy]

    def relays_to(s):
        return functools.reduce(jnp.logical_or, [relay_ok(r) for r in range(len(relays)) if relays[r][1] == s],
                                jnp.logical_and(z < 0, z > 0))

    def near(m, i, yy, shifts, when=lambda s: True):
        for s in shifts:
            @pl.when(valid(z + s) & when(s))
            def _():
                remote(unit(m, z, yy), unit(m, z, yy), z_send.at[m * Y + i], z_sem(m, -s, yy),
                       dev(plane, z + s, y, core)).start()

    def relay(m, i, yy, r):
        s, onward = relays[r]
        return remote(unit(m, z + s, yy), unit(m, z + s, yy), relay_send.at[(m * Y + i) * len(relays) + r],
                      z_sem(m, s - onward, yy), dev(plane, z + onward, y, core))

    def relay_ok(r):
        s, onward = relays[r]
        return valid(z + s) & valid(z + onward)

    def landed(m, i, yy, d):
        for s in (d, -d):
            @pl.when(valid(z + s))
            def _():
                remote(unit(m, z + s, yy), unit(m, z + s, yy), z_send.at[0], z_sem(m, s, yy),
                       dev(plane, z, y, c_peer)).wait_recv()
        for r, (s, onward) in enumerate(relays):
            if abs(s) == d:
                @pl.when(relay_ok(r))
                def _():
                    relay(m, i, yy, r).start()

    def chunk(m, zz, cc):
        return g_ref.at[m].at[:, pl.ds(zz * Y, Y), cc]

    def core_copy(m, zz, cc):
        return remote(chunk(m, zz, cc), chunk(m, zz, cc), core_send.at[m], core_recv.at[m * outer + zz],
                      dev(plane, z, y, c_peer))

    def share(m, d):
        for s in ((d, -d) if d else (0,)):
            @pl.when(valid(z + s))
            def _():
                core_copy(m, z + s, core).start()

    def finish(m):
        for zz in range(outer):
            core_copy(m, zz, c_peer).wait_recv()

    def side(m, part):
        return g_ref[m, part].reshape(width, part_width)

    def complex_rows_here(lhs, m):
        n = lhs.shape[0] // 2
        pr = jnp.dot(lhs, side(m, 0), preferred_element_type=f32)
        pi = jnp.dot(lhs, side(m, 1), preferred_element_type=f32)
        return pr[:n] - pi[n:], pi[:n] + pr[n:]

    everyone = (-2, 2, -1, 1)

    def ready_wait(s):
        @pl.when(valid(z + s))
        def _():
            pl.semaphore_wait(ready.at[s - 1], 1)

    def first_push():
        near(0, 0, y, (-2, -1))
        ready_wait(1)
        near(0, 0, y, (1,))
        ready_wait(2)
        near(0, 0, y, (2,))

    @pl.when(plane == last)
    def _():
        piece_wait(0, y)
        first_push()
        piece_wait(0, y_peer)
        near(0, 1, y_peer, everyone)
        share(0, 0)
        piece_wait(1, y)
        near(1, 0, y, everyone, lambda s: ~relays_to(s))
        landed(0, 0, y, 2)
        landed(0, 0, y, 1)
        piece_wait(1, y_peer)
        near(1, 1, y_peer, everyone, lambda s: ~relays_to(s))
        share(1, 0)
        landed(0, 1, y_peer, 2)
        near(1, 0, y, (-1, 1), relays_to)
        near(1, 1, y_peer, (-1, 1), relays_to)
        pltpu.make_async_copy(left_ref.at[:, y], left_ref.at[:, y], left_recv.at[0]).wait()

    for copy in args:
        copy.wait()
    eye = (lax.broadcasted_iota(jnp.int32, (sources, sources), 0)
           == lax.broadcasted_iota(jnp.int32, (sources, sources), 1))
    cell = jnp.sum(jnp.where(eye, cell_ref[...], 0), axis=1, keepdims=True)
    slab = jnp.sum(jnp.where(eye, slab_ref[...], 0), axis=1, keepdims=True)
    offset = lax.broadcasted_iota(jnp.int32, (sources, width), 1) - cell
    offset = jnp.where(offset < 0, offset + width, offset)
    inside = offset < width // 4
    for part in range(2):
        amp = amp_ref[:, part * width:(part + 1) * width].astype(f32)
        x_ref[part, y] = jnp.where(inside & (slab == 0), amp, 0.0).astype(bf16)
        base_ref[part, y] = jnp.where(inside & (slab == 1), amp, 0.0).astype(bf16)

    @pl.when(plane != last)
    def _():
        piece_wait(0, y)
        first_push()
        piece_wait(0, y_peer)
        near(0, 1, y_peer, everyone)
        share(0, 0)
        for u, (part, h) in enumerate(left_units):
            ref = left_rows(part, h, y)
            pltpu.make_async_copy(ref, ref, left_recv.at[u]).wait()
            left_relay(u, part, h).start()
            if u == 2:
                landed(0, 0, y, 2)
        landed(0, 0, y, 1)
        landed(0, 1, y_peer, 2)
        piece_wait(1, y)
        near(1, 0, y, everyone)
        piece_wait(1, y_peer)
        near(1, 1, y_peer, everyone)
        share(1, 0)

    far = range(3, outer)
    share(0, 2)
    landed(0, 1, y_peer, 1)
    share(0, 1)
    for d in far:
        landed(0, 0, y, d)
        landed(0, 1, y_peer, d)
        share(0, d)
    ref = left_ref.at[:, y_peer]
    pltpu.make_async_copy(ref, ref, left_recv.at[len(left_units)]).wait()
    finish(0)

    def x_swap(yy):
        ref = x_ref.at[:, yy]
        return remote(ref, ref, x_send.at[0], x_recv.at[0], dev(plane, z, y_peer, core))

    def base_swap(yy, quarter):
        ref = base_ref.at[:, yy, :, cols(quarter)]
        return remote(ref, ref, x_send.at[1], x_recv.at[1], dev(plane, z, y_peer, core))

    def coup_copy(yy, k, quarter):
        p, to_y = others[k]
        ref = coup_ref.at[yy].at[:, cols(quarter)]
        return remote(ref, ref, c_send.at[yy], c_recv.at[yy * len(others) + k], dev(p, z, to_y, core))

    re, im = complex_rows_here(left_ref[...].reshape(2 * Y * depth, width), 0)
    for yy in range(Y):
        coup_ref[yy, 0:depth, cols(q)] = re[yy * depth:(yy + 1) * depth].astype(bf16)
        coup_ref[yy, depth:, cols(q)] = im[yy * depth:(yy + 1) * depth].astype(bf16)
        for k in range(len(others)):
            coup_copy(yy, k, q).start()

    x_swap(y).start()
    base_swap(y, plane * Y + y_peer).start()
    landed(1, 0, y, 2)
    landed(1, 0, y, 1)
    landed(1, 1, y_peer, 2)
    share(1, 2)
    landed(1, 1, y_peer, 1)
    share(1, 1)
    for d in far:
        landed(1, 0, y, d)
        landed(1, 1, y_peer, d)
        share(1, d)
    finish(1)

    for yy in range(Y):
        for k, (p, from_y) in enumerate(others):
            coup_copy(yy, k, p * Y + from_y).wait_recv()
        re, im = complex_rows_here(coup_ref[yy], 1)
        for part, value in ((0, re), (1, im)):
            start = g_ref[1, part, z * Y + yy, core]
            g_ref[2, part, z * Y + yy, core] = (value + start.astype(f32)).astype(bf16)
        near(2, yy, yy, everyone)
    share(2, 0)
    for d in (2, 1, *far):
        for yy in range(Y):
            landed(2, yy, yy, d)
        share(2, d)
    x_swap(y_peer).wait_recv()
    base_swap(y_peer, q).wait_recv()
    finish(2)

    re, im = complex_rows_here(x_ref[...].reshape(2 * Y * sources, width), 2)
    for part, value in ((0, re), (1, im)):
        start = base_ref[part, :, :, cols(q)].astype(f32)
        f_ref[part] = (value.reshape(Y, sources, part_width) + start).astype(bf16)

    lhs = f_ref[...].reshape(2 * Y * sources, part_width)
    n = Y * sources
    tile = Y * CORE * depth

    def d_copy(to, k, yy, j):
        spots = slice(j * tile, (j + 1) * tile)
        return remote(d_ref.at[:, yy, :, spots], far_ref.at[k].at[:, :, spots],
                      d_send.at[to], d_recv.at[k * outer + j], dev(0, z, yy, core))

    def f_copy(to, k, yy, quarter):
        return remote(f_ref.at[:, yy], whole_ref.at[:, :, cols(quarter)], f_send.at[to],
                      f_recv.at[k], dev(last, z, yy, core))

    for j in range(outer):
        spots = slice(j * tile, (j + 1) * tile)
        dims = (((1,), (1,)), ((), ()))
        right = [g_ref[2, part, j * Y:(j + 1) * Y].reshape(tile, part_width) for part in range(2)]
        pr = lax.dot_general(lhs, right[0], dims, preferred_element_type=f32)
        pi = lax.dot_general(lhs, right[1], dims, preferred_element_type=f32)
        d_ref[0, :, :, spots] = (pr[:n] - pi[n:]).astype(bf16).reshape(Y, sources, tile)
        d_ref[1, :, :, spots] = (pi[:n] + pr[n:]).astype(bf16).reshape(Y, sources, tile)

        @pl.when(plane == last)
        def _():
            d_copy(0, 2, y_peer, j).start()
            d_copy(1, 0, y, j).start()

        @pl.when(plane != last)
        def _():
            d_copy(0, 1, y_peer, j).start()

    @pl.when(plane == last)
    def _():
        f_copy(0, 1, y_peer, q).start()

    @pl.when(plane != last)
    def _():
        f_copy(0, 2, y_peer, q).start()
        f_copy(1, 0, y, q).start()

    def sent(ref, sem):
        remote(ref, ref, sem, sem, dev(plane, z, y, c_peer)).wait_send()

    @pl.when(plane == last)
    def _():
        for m in range(2):
            sent(r_hbm.at[0, 0, :, 0:6 * part_width], in_send.at[m])
        sent(left_ref, left_send.at[0])

    @pl.when(plane != last)
    def _():
        sent(left_ref.at[:, 0], left_send.at[0])

    x_swap(y).wait_send()
    base_swap(y, plane * Y + y_peer).wait_send()
    for yy in range(Y):
        sent(coup_ref.at[yy, :, 0:len(others) * part_width], c_send.at[yy])
    count = sum(valid(z + s).astype(jnp.int32) for s in everyone)
    for m in range(3):
        sent(g_ref.at[m, :, :, 0], core_send.at[m])
        for i in range(Y):
            for total in range(1, 5):
                @pl.when(count == total)
                def _():
                    sent(g_ref.at[m, :, 0:total, 0], z_send.at[m * Y + i])
            for r in range(len(relays)):
                @pl.when(relay_ok(r))
                def _():
                    sent(g_ref.at[m, :, 0, 0], relay_send.at[(m * Y + i) * len(relays) + r])

    @pl.when(plane == last)
    def _():
        whole_ref[:, :, cols(q)] = f_ref[:, y]
        for k, (p, yy) in enumerate(others):
            f_copy(0, k, y, p * Y + yy).wait_recv()
        for part in range(2):
            out_ref[:, part * width:(part + 1) * width] = whole_ref[part].astype(f32)
        sent(d_ref.at[:, 0], d_send.at[0])
        sent(d_ref.at[:, 0], d_send.at[1])
        sent(f_ref.at[:, 0], f_send.at[0])

    @pl.when(plane != last)
    def _():
        for j in range(outer):
            spots = slice(j * tile, (j + 1) * tile)
            for k in range(len(others)):
                d_copy(0, k, y, j).wait_recv()
            for part in range(2):
                total = d_ref.at[part][y, :, spots].astype(f32)
                for k in range(len(others)):
                    total = total + far_ref[k, part, :, spots].astype(f32)
                out_ref[:, part * width + j * tile:part * width + (j + 1) * tile] = (
                    x_ref.at[part][y, :, spots].astype(f32) + total.astype(bf16).astype(f32))
        sent(d_ref.at[:, 0], d_send.at[0])
        sent(f_ref.at[:, 0], f_send.at[0])
        sent(f_ref.at[:, 0], f_send.at[1])


def pair_body(transmit, reflect, source_amp, source_cell, source_slab):
    outer = lax.axis_size("blk") // (Y * CORE)
    sources, double = source_amp.shape
    depth = transmit.shape[1]
    width = double // 2
    quarter = width // (PLANES * Y)
    bf16 = jnp.bfloat16
    hbm = pl.BlockSpec(memory_space=pltpu.HBM)
    sem = pltpu.SemaphoreType.DMA
    out = pl.pallas_call(
        functools.partial(pair_kernel, outer),
        out_shape=pltpu.VMEM((sources, double), jnp.float32),
        in_specs=[hbm] * 5,
        out_specs=pl.BlockSpec(memory_space=pltpu.VMEM),
        scratch_shapes=[
            pltpu.VMEM((sources, double), bf16),
            pltpu.VMEM((1, sources), jnp.int32),
            pltpu.VMEM((1, sources), jnp.int32),
            pltpu.VMEM((3, 2, outer * Y, CORE, depth, quarter), bf16),
            pltpu.VMEM((2, Y, depth, width), bf16),
            pltpu.VMEM((Y, 2 * depth, width), bf16),
            pltpu.VMEM((2, Y, sources, width), bf16),
            pltpu.VMEM((2, Y, sources, width), bf16),
            pltpu.VMEM((2, Y, sources, quarter), bf16),
            pltpu.VMEM((2, sources, width), bf16),
            pltpu.VMEM((2, Y, sources, width), bf16),
            pltpu.VMEM((PLANES * Y - 1, 2, sources, width), bf16),
            pltpu.SemaphoreType.REGULAR((2,)),
            sem((3,)),
            sem((2,)),
            sem((2 * Y,)),
            sem((1,)),
            sem((5,)),
            sem((3 * Y,)),
            sem((3 * (outer - 1) * Y,)),
            sem((3 * Y * 2 * max(outer - 3, 1),)),
            sem((3,)),
            sem((3 * outer,)),
            sem((Y,)),
            sem((3 * Y,)),
            sem((2,)),
            sem((2,)),
            sem((2,)),
            sem((3,)),
            sem((2,)),
            sem((3 * outer,)),
        ],
        compiler_params=pltpu.CompilerParams(
            collective_id=0, has_side_effects=True, vmem_limit_bytes=32 << 20),
    )(*(pltpu.with_memory_space_constraint(a, pltpu.HBM) for a in (
        transmit, reflect, source_amp, source_cell[None], source_slab[None])))
    return out[None]


def solution(mesh):
    pair = mesh.shape["slab"] == PLANES and mesh.shape["blk"] % (Y * CORE) == 0
    return jax.shard_map(
        pair_body if pair else body,
        mesh=mesh,
        in_specs=(
            P("slab", "blk", None),
            P("slab", None, "blk", None),
            P("blk", None),
            P("blk"),
            P("blk"),
        ),
        out_specs=P("slab", "blk", None),
        check_vma=False,
    )
```

```python
import functools

import jax
import jax.numpy as jnp
from jax import lax
from jax.experimental import pallas as pl
from jax.experimental.pallas import tpu as pltpu
from jax.sharding import PartitionSpec as P


def shifted(block, axis, distance):
    devices = range(lax.axis_size(axis))
    route = [(i - distance, i) for i in devices if i - distance in devices]
    return lax.ppermute(block, axis, route)


def transposed(matrix):
    half_width = matrix.shape[0]
    return jnp.concatenate([matrix[:, :half_width].T, matrix[:, half_width:].T], 1)


def complex_rows(left_rows, right_matrix):
    inner_width = right_matrix.shape[0]
    outer_width = right_matrix.shape[1] // 2
    row_count = left_rows.shape[0]
    stacked = jnp.concatenate([left_rows[:, :inner_width], left_rows[:, inner_width:]], 0)
    product = jnp.dot(stacked, right_matrix, preferred_element_type=jnp.float32)
    real_out = product[:row_count, :outer_width] - product[row_count:, outer_width:]
    imag_out = product[:row_count, outer_width:] + product[row_count:, :outer_width]
    return jnp.concatenate([real_out, imag_out], 1)


def body(transmit, reflect, source_amp, source_cell, source_slab):
    trans_local = transmit[0]
    refl_local = reflect[0]
    half_width = source_amp.shape[1] // 2
    refl_second = lax.all_gather(refl_local[1], "blk", axis=0, tiled=True)
    coupling = complex_rows(refl_local[0], refl_second).astype(jnp.bfloat16)
    start_rows = trans_local.astype(jnp.float32)
    piece_rows = lax.all_gather(trans_local, "blk", axis=0, tiled=True)
    piece_count = piece_rows.shape[0]
    real_cols = lax.slice_in_dim(coupling, 0, piece_count, axis=1)
    imag_cols = lax.dynamic_slice_in_dim(coupling, half_width, piece_count, 1)
    left_rows = jnp.concatenate([real_cols, imag_cols], 1)
    joined = (start_rows + complex_rows(left_rows, piece_rows)).astype(jnp.bfloat16)
    slab_matrix = lax.all_gather(joined, "blk", axis=0, tiled=True)
    back_matrix = transposed(slab_matrix)
    cell_index = lax.iota(jnp.int32, half_width)
    offset = (cell_index[None, :] - source_cell[:, None]) % half_width
    inside = offset < half_width // 4
    here = source_slab == lax.axis_index("slab")
    keep = inside & here[:, None]
    keep = jnp.concatenate([keep, keep], 1)
    forcing = jnp.where(keep, source_amp, jnp.zeros_like(source_amp))
    chain_length = lax.axis_size("slab")
    carried = forcing
    for sweep_step in range(chain_length - 1):
        arrived = shifted(carried, "slab", 1)
        carried = (forcing.astype(jnp.float32) + complex_rows(arrived, slab_matrix)).astype(
            jnp.bfloat16
        )
    current = carried.astype(jnp.float32)
    for sweep_step in range(chain_length - 1):
        message = complex_rows(current.astype(jnp.bfloat16), back_matrix).astype(jnp.bfloat16)
        arrived = shifted(message, "slab", -1)
        current = carried.astype(jnp.float32) + arrived.astype(jnp.float32)
    return current[None]


MESH = pl.DeviceIdType.MESH
Y = 2
CORE = 2
PLANES = 2


def pair_kernel(
    outer, t_hbm, r_hbm, amp_hbm, cell_hbm, slab_hbm, out_ref,
    amp_ref, cell_ref, slab_ref, g_ref, left_ref, coup_ref, x_ref, base_ref,
    f_ref, whole_ref, d_ref, far_ref,
    ready, arg_sem, in_send, in_recv, left_send, left_recv, z_send, z_recv, relay_send,
    core_send, core_recv, c_send, c_recv, x_send, x_recv, f_send, f_recv, d_send, d_recv,
):
    plane = lax.axis_index("slab")
    me = lax.axis_index("blk")
    z, y, core = me // (Y * CORE), (me // CORE) % Y, me % CORE
    last = PLANES - 1
    depth = t_hbm.shape[1]
    half = depth // 2
    width = t_hbm.shape[2] // 2
    part_width = width // (PLANES * Y)
    sources = amp_hbm.shape[0]
    y_peer, c_peer, x_peer = 1 - y, 1 - core, 1 - plane
    q = plane * Y + y
    f32, bf16 = jnp.float32, jnp.bfloat16
    others = ((x_peer, y), (plane, y_peer), (x_peer, y_peer))
    order = (y, y_peer)

    def dev(p, zz, yy, cc):
        return (p, (zz * Y + yy) * CORE + cc)

    def cols(quarter, base=0):
        return pl.ds(pl.multiple_of(base + quarter * part_width, part_width), part_width)

    def remote(s, d, ss, rs, to):
        return pltpu.make_async_remote_copy(
            src_ref=s, dst_ref=d, send_sem=ss, recv_sem=rs, device_id=to, device_id_type=MESH)

    def got(ref, sem):
        pltpu.make_async_copy(ref, ref, sem).wait()

    def sent(ref, sem):
        remote(ref, ref, sem, sem, dev(plane, z, y, c_peer)).wait_send()

    def valid(zz):
        return (zz >= 0) & (zz < outer)

    def unit(m, zz, yy):
        return g_ref.at[m].at[:, zz * Y + yy, core]

    def piece(m, part, p, yy):
        s = r_hbm.at[0, 1] if m == 0 else t_hbm.at[0]
        return s.at[:, cols(p * Y + yy, part * width)]

    def slot(m, part):
        return g_ref.at[m, part].at[z * Y + y, core]

    def piece_local(m, part):
        return pltpu.make_async_copy(piece(m, part, last, y), slot(m, part), in_recv.at[m * Y + y])

    def piece_send(m, part, p, yy):
        split = m == 0 and part == 1 and p != last and yy is y
        return remote(piece(m, part, p, yy), slot(m, part), in_send.at[0],
                      in_recv.at[2 * Y] if split else in_recv.at[m * Y + y], dev(p, z, yy, core))

    def piece_wait(m, yy):
        got(unit(m, z, yy), in_recv.at[m * Y + yy])

    left_units = [(part, h) for part in range(2) for h in range(2)]

    def left_rows(part, h, yy):
        return left_ref.at[part].at[yy, h * half:(h + 1) * half]

    def left_src(part, h):
        return r_hbm.at[0, 0, h * half:(h + 1) * half, part * width:(part + 1) * width]

    def left_local(part):
        return pltpu.make_async_copy(
            r_hbm.at[0, 0, :, part * width:(part + 1) * width], left_ref.at[part].at[y], left_recv.at[0])

    def left_push(u, part, h, k):
        to = dev(0, z, y, core) if k == 0 else dev(last, z, y_peer, core)
        return remote(left_src(part, h), left_rows(part, h, y), left_send.at[0],
                      left_recv.at[u if k == 0 else len(left_units)], to)

    def left_relay(u, part, h):
        ref = left_rows(part, h, y)
        return remote(ref, ref, left_send.at[0], left_recv.at[len(left_units)], dev(plane, z, y_peer, core))

    args = [pltpu.make_async_copy(a, b, arg_sem.at[i]) for i, (a, b) in enumerate(
        ((amp_hbm, amp_ref), (cell_hbm, cell_ref), (slab_hbm, slab_ref)))]

    barrier = pltpu.get_barrier_semaphore()

    def tell(sem, to, when=None):
        def send():
            pl.semaphore_signal(sem, inc=1, device_id=to, device_id_type=MESH)
        send() if when is None else pl.when(when)(send)

    for p, yy, cc in ((plane, y, c_peer), (plane, y_peer, core), (x_peer, y, core), (x_peer, y_peer, core)):
        tell(barrier, dev(p, z, yy, cc))
    for s in (1, 2):
        tell(barrier, dev(plane, z + s, y, core), valid(z + s))

    @pl.when(plane == last)
    def _():
        for m in range(2):
            for part in range(2):
                piece_local(m, part).start()
        for part in range(2):
            left_local(part).start()

    for copy in args:
        copy.start()
    pl.semaphore_wait(barrier, 4 + jnp.minimum(z, 2))
    for s in (1, 2):
        tell(ready.at[s - 1], dev(plane, z - s, y, core), valid(z - s))

    @pl.when(plane == last)
    def _():
        for p, yy in ((0, y), (last, y_peer), (0, y_peer)):
            for part in range(2):
                piece_send(0, part, p, yy).start()
        for u, (part, h) in enumerate(left_units):
            for k in range(2):
                left_push(u, part, h, k).start()
        for p, yy in ((0, y), (last, y_peer), (0, y_peer)):
            for part in range(2):
                piece_send(1, part, p, yy).start()

    def z_sem(m, shift, yy):
        return z_recv.at[(m * (outer - 1) + shift % outer - 1) * Y + yy]

    reach = (-2, 2, -1, 1)

    def near(m, yy, when=lambda s: True, part=None, shifts=reach):
        for s in shifts:
            @pl.when(valid(z + s) & when(s))
            def _():
                ref = unit(m, z, yy) if part is None else slot(m, part)
                remote(ref, ref, z_send.at[0], z_sem(m, -s, yy), dev(plane, z + s, y, core)).start()

    def ready_wait(s):
        @pl.when(valid(z + s))
        def _():
            pl.semaphore_wait(ready.at[s - 1], 1)

    def relays_to(s):
        return {1: (z >= 2) & valid(z + 1), -1: (z <= outer - 3) & valid(z - 1)}.get(s, z < 0)

    def onward_ok(s):
        return valid(z + s) & valid(z + (-1 if s > 0 else 1)) & (abs(s) > 1)

    def hop(m, yy, d):
        for s in (d, -d) if d > 1 else ():
            @pl.when(onward_ok(s))
            def _():
                onward = -1 if s > 0 else 1
                ref = unit(m, z + s, yy)
                got(ref, z_sem(m, s, yy))
                remote(ref, ref, relay_send.at[0], z_sem(m, s - onward, yy),
                       dev(plane, z + onward, y, core)).start()

    def rest(m, d):
        for s in (d, -d):
            @pl.when(valid(z + s) & ~onward_ok(s))
            def _():
                for yy in range(Y):
                    got(unit(m, z + s, yy), z_sem(m, s, yy))

    def chunk(m, zz, cc):
        return g_ref.at[m].at[:, pl.ds(zz * Y, Y), cc]

    def core_copy(m, zz, cc):
        return remote(chunk(m, zz, cc), chunk(m, zz, cc), core_send.at[0], core_recv.at[m],
                      dev(plane, z, y, c_peer))

    def share(m, d):
        for s in ((d, -d) if d else (0,)):
            @pl.when(valid(z + s))
            def _():
                core_copy(m, z + s, core).start()

    def finish(m):
        got(g_ref.at[m].at[:, :, c_peer], core_recv.at[m])

    def collect(m):
        for d in range(1, outer):
            rest(m, d)
            share(m, d)
        finish(m)

    def side(m, part):
        return g_ref[m, part].reshape(width, part_width)

    def complex_rows_here(lhs, m):
        n = lhs.shape[0] // 2
        pr = jnp.dot(lhs, side(m, 0), preferred_element_type=f32)
        pi = jnp.dot(lhs, side(m, 1), preferred_element_type=f32)
        return pr[:n] - pi[n:], pi[:n] + pr[n:]

    @pl.when(plane == last)
    def _():
        piece_wait(0, y)
        near(0, y, shifts=(-2, -1))
        ready_wait(1)
        near(0, y, shifts=(1,))
        ready_wait(2)
        near(0, y, shifts=(2,))
        piece_wait(0, y_peer)
        near(0, y_peer)
        share(0, 0)
        piece_wait(1, y)
        near(1, y, lambda s: ~relays_to(s))
        hop(0, y, 2)
        hop(0, y_peer, 2)
        for yy in order:
            for d in range(3, outer):
                hop(0, yy, d)
        near(1, y, relays_to)
        piece_wait(1, y_peer)
        near(1, y_peer)
        share(1, 0)
        got(left_ref.at[:, y], left_recv.at[0])

    for copy in args:
        copy.wait()
    eye = (lax.broadcasted_iota(jnp.int32, (sources, sources), 0)
           == lax.broadcasted_iota(jnp.int32, (sources, sources), 1))
    cell = jnp.sum(jnp.where(eye, cell_ref[...], 0), axis=1, keepdims=True)
    slab = jnp.sum(jnp.where(eye, slab_ref[...], 0), axis=1, keepdims=True)
    offset = lax.broadcasted_iota(jnp.int32, (sources, width), 1) - cell
    offset = jnp.where(offset < 0, offset + width, offset)
    inside = offset < width // 4
    for part in range(2):
        amp = amp_ref[:, part * width:(part + 1) * width].astype(f32)
        x_ref[part, y] = jnp.where(inside & (slab == 0), amp, 0.0).astype(bf16)
        base_ref[part, y] = jnp.where(inside & (slab == 1), amp, 0.0).astype(bf16)

    @pl.when(plane != last)
    def _():
        ready_wait(1)
        ready_wait(2)
        for part in range(2):
            got(slot(0, part), in_recv.at[y] if part == 0 else in_recv.at[2 * Y])
            near(0, y, part=part)
        piece_wait(0, y_peer)
        near(0, y_peer)
        share(0, 0)
        hops = [(y, 1), (y, 2), (y_peer, 1), (y_peer, 2)]
        for u, (part, h) in enumerate(left_units):
            got(left_rows(part, h, y), left_recv.at[u])
            left_relay(u, part, h).start()
            hop(0, *hops[u])
        for yy in order:
            for d in range(3, outer):
                hop(0, yy, d)
        for yy in order:
            piece_wait(1, yy)
            near(1, yy)
        share(1, 0)

    for d in range(1, outer):
        rest(0, d)
        share(0, d)
    got(left_ref.at[:, y_peer], left_recv.at[len(left_units)])
    finish(0)

    def x_swap(yy):
        ref = x_ref.at[:, yy]
        return remote(ref, ref, x_send.at[0], x_recv.at[0], dev(plane, z, y_peer, core))

    def base_swap(yy, quarter):
        ref = base_ref.at[:, yy, :, cols(quarter)]
        return remote(ref, ref, x_send.at[1], x_recv.at[1], dev(plane, z, y_peer, core))

    def coup_copy(yy, k, quarter):
        p, to_y = others[k]
        ref = coup_ref.at[yy].at[:, cols(quarter)]
        return remote(ref, ref, c_send.at[0], c_recv.at[yy], dev(p, z, to_y, core))

    re, im = complex_rows_here(left_ref[...].reshape(2 * Y * depth, width), 0)
    for yy in range(Y):
        coup_ref[yy, 0:depth, cols(q)] = re[yy * depth:(yy + 1) * depth].astype(bf16)
        coup_ref[yy, depth:, cols(q)] = im[yy * depth:(yy + 1) * depth].astype(bf16)
        for k in range(len(others)):
            coup_copy(yy, k, q).start()

    x_swap(y).start()
    base_swap(y, plane * Y + y_peer).start()

    for yy in order:
        for d in range(2, outer):
            hop(1, yy, d)
    collect(1)
    trio = len(others) * part_width
    for yy in range(Y):
        got(coup_ref.at[yy, :, 0:trio], c_recv.at[yy])
        re, im = complex_rows_here(coup_ref[yy], 1)
        for part, value in ((0, re), (1, im)):
            start = g_ref[1, part, z * Y + yy, core]
            g_ref[2, part, z * Y + yy, core] = (value + start.astype(f32)).astype(bf16)
        near(2, yy)
    share(2, 0)
    for d in range(1, outer):
        for yy in range(Y):
            hop(2, yy, d)
    for d in range(1, outer):
        rest(2, d)
        share(2, d)
    x_swap(y_peer).wait_recv()
    base_swap(y_peer, q).wait_recv()
    finish(2)

    re, im = complex_rows_here(x_ref[...].reshape(2 * Y * sources, width), 2)
    for part, value in ((0, re), (1, im)):
        start = base_ref[part, :, :, cols(q)].astype(f32)
        f_ref[part] = (value.reshape(Y, sources, part_width) + start).astype(bf16)

    lhs = f_ref[...].reshape(2 * Y * sources, part_width)
    n = Y * sources
    tile = Y * CORE * depth

    def d_copy(k, yy, j):
        spots = slice(j * tile, (j + 1) * tile)
        return remote(d_ref.at[:, yy, :, spots], far_ref.at[k].at[:, :, spots],
                      d_send.at[0], d_recv.at[j], dev(0, z, yy, core))

    def f_copy(yy):
        return remote(f_ref.at[:, yy], whole_ref.at[:, :, cols(q)], f_send.at[0],
                      f_recv.at[0], dev(last, z, yy, core))

    for j in range(outer):
        spots = slice(j * tile, (j + 1) * tile)
        dims = (((1,), (1,)), ((), ()))
        right = [g_ref[2, part, j * Y:(j + 1) * Y].reshape(tile, part_width) for part in range(2)]
        pr = lax.dot_general(lhs, right[0], dims, preferred_element_type=f32)
        pi = lax.dot_general(lhs, right[1], dims, preferred_element_type=f32)
        d_ref[0, :, :, spots] = (pr[:n] - pi[n:]).astype(bf16).reshape(Y, sources, tile)
        d_ref[1, :, :, spots] = (pi[:n] + pr[n:]).astype(bf16).reshape(Y, sources, tile)

        @pl.when(plane == last)
        def _():
            d_copy(2, y_peer, j).start()
            d_copy(0, y, j).start()

        @pl.when(plane != last)
        def _():
            d_copy(1, y_peer, j).start()

    @pl.when(plane == last)
    def _():
        f_copy(y_peer).start()

    @pl.when(plane != last)
    def _():
        f_copy(y_peer).start()
        f_copy(y).start()

    @pl.when(plane == last)
    def _():
        sent(r_hbm.at[0, :, :, 0:6 * part_width], in_send.at[0])
        sent(left_ref, left_send.at[0])

    @pl.when(plane != last)
    def _():
        sent(left_ref.at[:, 0], left_send.at[0])

    x_swap(y).wait_send()
    base_swap(y, plane * Y + y_peer).wait_send()
    sent(coup_ref.at[:, :, 0:trio], c_send.at[0])
    sent(g_ref.at[:, :, :, 0], core_send.at[0])
    for zz in range(outer):
        count = sum(0 <= zz + s < outer for s in reach)
        hops = (max(zz - 1, 0) + max(outer - 2 - zz, 0)) * (0 < zz < outer - 1)

        @pl.when(z == zz)
        def _():
            sent(g_ref.at[:, :, 0:Y * count, 0], z_send.at[0])
            if hops:
                sent(g_ref.at[:, :, 0:Y * hops, 0], relay_send.at[0])

    @pl.when(plane == last)
    def _():
        whole_ref[:, :, cols(q)] = f_ref[:, y]
        got(whole_ref.at[:, :, 0:trio], f_recv.at[0])
        for part in range(2):
            out_ref[:, part * width:(part + 1) * width] = whole_ref[part].astype(f32)
        sent(d_ref, d_send.at[0])
        sent(f_ref.at[:, 0], f_send.at[0])

    @pl.when(plane != last)
    def _():
        for j in range(outer):
            spots = slice(j * tile, (j + 1) * tile)
            got(far_ref.at[:, :, :, spots], d_recv.at[j])
            for part in range(2):
                total = d_ref.at[part][y, :, spots].astype(f32)
                for k in range(len(others)):
                    total = total + far_ref[k, part, :, spots].astype(f32)
                out_ref[:, part * width + j * tile:part * width + (j + 1) * tile] = (
                    x_ref.at[part][y, :, spots].astype(f32) + total.astype(bf16).astype(f32))
        sent(d_ref.at[:, 0], d_send.at[0])
        sent(f_ref, f_send.at[0])


def pair_body(transmit, reflect, source_amp, source_cell, source_slab):
    outer = lax.axis_size("blk") // (Y * CORE)
    sources, double = source_amp.shape
    depth = transmit.shape[1]
    width = double // 2
    quarter = width // (PLANES * Y)
    bf16 = jnp.bfloat16
    hbm = pl.BlockSpec(memory_space=pltpu.HBM)
    sem = pltpu.SemaphoreType.DMA
    out = pl.pallas_call(
        functools.partial(pair_kernel, outer),
        out_shape=pltpu.VMEM((sources, double), jnp.float32),
        in_specs=[hbm] * 5,
        out_specs=pl.BlockSpec(memory_space=pltpu.VMEM),
        scratch_shapes=[
            pltpu.VMEM((sources, double), bf16),
            pltpu.VMEM((1, sources), jnp.int32),
            pltpu.VMEM((1, sources), jnp.int32),
            pltpu.VMEM((3, 2, outer * Y, CORE, depth, quarter), bf16),
            pltpu.VMEM((2, Y, depth, width), bf16),
            pltpu.VMEM((Y, 2 * depth, width), bf16),
            pltpu.VMEM((2, Y, sources, width), bf16),
            pltpu.VMEM((2, Y, sources, width), bf16),
            pltpu.VMEM((2, Y, sources, quarter), bf16),
            pltpu.VMEM((2, sources, width), bf16),
            pltpu.VMEM((2, Y, sources, width), bf16),
            pltpu.VMEM((PLANES * Y - 1, 2, sources, width), bf16),
            pltpu.SemaphoreType.REGULAR((2,)),
            sem((3,)),
            sem((1,)),
            sem((2 * Y + 1,)),
            sem((1,)),
            sem((5,)),
            sem((1,)),
            sem((3 * (outer - 1) * Y,)),
            sem((1,)),
            sem((1,)),
            sem((3,)),
            sem((1,)),
            sem((Y,)),
            sem((2,)),
            sem((2,)),
            sem((1,)),
            sem((1,)),
            sem((1,)),
            sem((outer,)),
        ],
        compiler_params=pltpu.CompilerParams(
            collective_id=0, has_side_effects=True, vmem_limit_bytes=32 << 20),
    )(*(pltpu.with_memory_space_constraint(a, pltpu.HBM) for a in (
        transmit, reflect, source_amp, source_cell[None], source_slab[None])))
    return out[None]


def solution(mesh):
    pair = mesh.shape["slab"] == PLANES and mesh.shape["blk"] % (Y * CORE) == 0 and mesh.shape["blk"] > 2 * Y * CORE
    return jax.shard_map(
        pair_body if pair else body,
        mesh=mesh,
        in_specs=(
            P("slab", "blk", None),
            P("slab", None, "blk", None),
            P("blk", None),
            P("blk"),
            P("blk"),
        ),
        out_specs=P("slab", "blk", None),
        check_vma=False,
    )
```

```python
import functools

import jax
import jax.numpy as jnp
from jax import lax
from jax.experimental import pallas as pl
from jax.experimental.pallas import tpu as pltpu
from jax.sharding import PartitionSpec as P


def shifted(block, axis, distance):
    devices = range(lax.axis_size(axis))
    route = [(i - distance, i) for i in devices if i - distance in devices]
    return lax.ppermute(block, axis, route)


def transposed(matrix):
    half_width = matrix.shape[0]
    return jnp.concatenate([matrix[:, :half_width].T, matrix[:, half_width:].T], 1)


def complex_rows(left_rows, right_matrix):
    inner_width = right_matrix.shape[0]
    outer_width = right_matrix.shape[1] // 2
    row_count = left_rows.shape[0]
    stacked = jnp.concatenate([left_rows[:, :inner_width], left_rows[:, inner_width:]], 0)
    product = jnp.dot(stacked, right_matrix, preferred_element_type=jnp.float32)
    real_out = product[:row_count, :outer_width] - product[row_count:, outer_width:]
    imag_out = product[:row_count, outer_width:] + product[row_count:, :outer_width]
    return jnp.concatenate([real_out, imag_out], 1)


def body(transmit, reflect, source_amp, source_cell, source_slab):
    trans_local = transmit[0]
    refl_local = reflect[0]
    half_width = source_amp.shape[1] // 2
    refl_second = lax.all_gather(refl_local[1], "blk", axis=0, tiled=True)
    coupling = complex_rows(refl_local[0], refl_second).astype(jnp.bfloat16)
    start_rows = trans_local.astype(jnp.float32)
    piece_rows = lax.all_gather(trans_local, "blk", axis=0, tiled=True)
    piece_count = piece_rows.shape[0]
    real_cols = lax.slice_in_dim(coupling, 0, piece_count, axis=1)
    imag_cols = lax.dynamic_slice_in_dim(coupling, half_width, piece_count, 1)
    left_rows = jnp.concatenate([real_cols, imag_cols], 1)
    joined = (start_rows + complex_rows(left_rows, piece_rows)).astype(jnp.bfloat16)
    slab_matrix = lax.all_gather(joined, "blk", axis=0, tiled=True)
    back_matrix = transposed(slab_matrix)
    cell_index = lax.iota(jnp.int32, half_width)
    offset = (cell_index[None, :] - source_cell[:, None]) % half_width
    inside = offset < half_width // 4
    here = source_slab == lax.axis_index("slab")
    keep = inside & here[:, None]
    keep = jnp.concatenate([keep, keep], 1)
    forcing = jnp.where(keep, source_amp, jnp.zeros_like(source_amp))
    chain_length = lax.axis_size("slab")
    carried = forcing
    for sweep_step in range(chain_length - 1):
        arrived = shifted(carried, "slab", 1)
        carried = (forcing.astype(jnp.float32) + complex_rows(arrived, slab_matrix)).astype(
            jnp.bfloat16
        )
    current = carried.astype(jnp.float32)
    for sweep_step in range(chain_length - 1):
        message = complex_rows(current.astype(jnp.bfloat16), back_matrix).astype(jnp.bfloat16)
        arrived = shifted(message, "slab", -1)
        current = carried.astype(jnp.float32) + arrived.astype(jnp.float32)
    return current[None]


MESH = pl.DeviceIdType.MESH
Y = 2
CORE = 2
PLANES = 2
SPLIT = 4


def pair_kernel(
    outer, t_hbm, r_hbm, amp_hbm, cell_hbm, slab_hbm, out_ref,
    amp_ref, cell_ref, slab_ref, g_ref, left_ref, coup_ref, x_ref, base_ref,
    f_ref, whole_ref, d_ref, far_ref, hand_ref,
    ready, arg_sem, in_send, in_recv, left_send, left_recv, z_send, z_recv, relay_send,
    core_send, core_recv, c_send, c_recv, x_send, x_recv, f_send, f_recv, d_send, d_recv, hand_recv,
):
    plane = lax.axis_index("slab")
    me = lax.axis_index("blk")
    z, y, core = me // (Y * CORE), (me // CORE) % Y, me % CORE
    last = PLANES - 1
    depth = t_hbm.shape[1]
    half = depth // 2
    width = t_hbm.shape[2] // 2
    part_width = width // (PLANES * Y)
    sources = amp_hbm.shape[0]
    y_peer, c_peer, x_peer = 1 - y, 1 - core, 1 - plane
    q = plane * Y + y
    f32, bf16 = jnp.float32, jnp.bfloat16
    others = ((x_peer, y), (plane, y_peer), (x_peer, y_peer))
    order = (y, y_peer)
    rows = coup_ref.shape[1] // 2
    per = depth // rows
    parts = range(Y * per)

    def dev(p, zz, yy, cc):
        return (p, (zz * Y + yy) * CORE + cc)

    def cols(quarter, base=0):
        return pl.ds(pl.multiple_of(base + quarter * part_width, part_width), part_width)

    def remote(s, d, ss, rs, to):
        return pltpu.make_async_remote_copy(
            src_ref=s, dst_ref=d, send_sem=ss, recv_sem=rs, device_id=to, device_id_type=MESH)

    def got(ref, sem):
        pltpu.make_async_copy(ref, ref, sem).wait()

    def sent(ref, sem):
        remote(ref, ref, sem, sem, dev(plane, z, y, c_peer)).wait_send()

    def valid(zz):
        return (zz >= 0) & (zz < outer)

    def unit(m, zz, u):
        if m < 2:
            return g_ref.at[m].at[:, zz * Y + u, core]
        return g_ref.at[m].at[:, zz * Y + u // per, core, u % per * rows:(u % per + 1) * rows]

    def piece(m, part, p, yy):
        s = r_hbm.at[0, 1] if m == 0 else t_hbm.at[0]
        return s.at[:, cols(p * Y + yy, part * width)]

    def slot(m, part):
        return g_ref.at[m, part].at[z * Y + y, core]

    def piece_local(m, part):
        return pltpu.make_async_copy(piece(m, part, last, y), slot(m, part), in_recv.at[m * Y + y])

    def piece_send(m, part, p, yy):
        split = m == 0 and part == 1 and p != last and yy is y
        return remote(piece(m, part, p, yy), slot(m, part), in_send.at[0],
                      in_recv.at[2 * Y] if split else in_recv.at[m * Y + y], dev(p, z, yy, core))

    def piece_wait(m, yy):
        got(unit(m, z, yy), in_recv.at[m * Y + yy])

    left_units = [(part, h) for part in range(2) for h in range(2)]

    def left_rows(part, h, yy):
        return left_ref.at[part].at[yy, h * half:(h + 1) * half]

    def left_src(part, h):
        return r_hbm.at[0, 0, h * half:(h + 1) * half, part * width:(part + 1) * width]

    def left_local(part):
        return pltpu.make_async_copy(
            r_hbm.at[0, 0, :, part * width:(part + 1) * width], left_ref.at[part].at[y], left_recv.at[0])

    def left_push(u, part, h, k):
        to = dev(0, z, y, core) if k == 0 else dev(last, z, y_peer, core)
        return remote(left_src(part, h), left_rows(part, h, y), left_send.at[0],
                      left_recv.at[u if k == 0 else len(left_units)], to)

    def left_relay(u, part, h):
        ref = left_rows(part, h, y)
        return remote(ref, ref, left_send.at[0], left_recv.at[len(left_units)], dev(plane, z, y_peer, core))

    args = [pltpu.make_async_copy(a, b, arg_sem.at[i]) for i, (a, b) in enumerate(
        ((amp_hbm, amp_ref), (cell_hbm, cell_ref), (slab_hbm, slab_ref)))]

    barrier = pltpu.get_barrier_semaphore()

    def tell(sem, to, when=None):
        def send():
            pl.semaphore_signal(sem, inc=1, device_id=to, device_id_type=MESH)
        send() if when is None else pl.when(when)(send)

    for p, yy, cc in ((plane, y, c_peer), (plane, y_peer, core), (x_peer, y, core), (x_peer, y_peer, core)):
        tell(barrier, dev(p, z, yy, cc))
    for s in (1, 2):
        tell(barrier, dev(plane, z + s, y, core), valid(z + s))

    @pl.when(plane == last)
    def _():
        for m in range(2):
            for part in range(2):
                piece_local(m, part).start()
        for part in range(2):
            left_local(part).start()

    for copy in args:
        copy.start()
    pl.semaphore_wait(barrier, 4 + jnp.minimum(z, 2))
    for s in (1, 2):
        tell(ready.at[s - 1], dev(plane, z - s, y, core), valid(z - s))

    @pl.when(plane == last)
    def _():
        for p, yy in ((0, y), (last, y_peer), (0, y_peer)):
            for part in range(2):
                piece_send(0, part, p, yy).start()
        for u, (part, h) in enumerate(left_units):
            for k in range(2):
                left_push(u, part, h, k).start()
        for p, yy in ((0, y), (last, y_peer), (0, y_peer)):
            for part in range(2):
                piece_send(1, part, p, yy).start()

    def z_sem(m, shift, yy):
        k = shift % outer - 1
        return z_recv.at[(m * (outer - 1) + k) * Y + yy if m < 2 else (2 * (outer - 1) + k * per) * Y + yy]

    reach = (-2, 2, -1, 1)

    def near(m, yy, when=lambda s: True, part=None, shifts=reach):
        for s in shifts:
            @pl.when(valid(z + s) & when(s))
            def _():
                ref = unit(m, z, yy) if part is None else slot(m, part)
                remote(ref, ref, z_send.at[0], z_sem(m, -s, yy), dev(plane, z + s, y, core)).start()

    def inner(s):
        return (z + s > 0) & (z + s < outer - 1) if abs(s) == 1 else z < 0

    def outward(s):
        return ~inner(s)

    def ready_wait(s):
        @pl.when(valid(z + s))
        def _():
            pl.semaphore_wait(ready.at[s - 1], 1)

    def relays_to(s):
        return {1: (z >= 2) & valid(z + 1), -1: (z <= outer - 3) & valid(z - 1)}.get(s, z < 0)

    def onward_ok(s):
        return valid(z + s) & valid(z + (-1 if s > 0 else 1)) & (abs(s) > 1)

    def hop(m, yy, d):
        for s in (d, -d) if d > 1 else ():
            @pl.when(onward_ok(s))
            def _():
                onward = -1 if s > 0 else 1
                ref = unit(m, z + s, yy)
                got(ref, z_sem(m, s, yy))
                remote(ref, ref, relay_send.at[0], z_sem(m, s - onward, yy),
                       dev(plane, z + onward, y, core)).start()

    def rest(m, d):
        for s in (d, -d):
            @pl.when(valid(z + s) & ~onward_ok(s))
            def _():
                for yy in range(Y) if m < 2 else parts:
                    got(unit(m, z + s, yy), z_sem(m, s, yy))

    def chunk(m, zz, cc):
        return g_ref.at[m].at[:, pl.ds(zz * Y, Y), cc]

    def core_copy(m, zz, cc):
        return remote(chunk(m, zz, cc), chunk(m, zz, cc), core_send.at[0], core_recv.at[m],
                      dev(plane, z, y, c_peer))

    def share(m, d):
        for s in ((d, -d) if d else (0,)):
            @pl.when(valid(z + s))
            def _():
                core_copy(m, z + s, core).start()

    def finish(m):
        got(g_ref.at[m].at[:, :, c_peer], core_recv.at[m])

    def collect(m):
        for d in range(1, outer):
            rest(m, d)
            share(m, d)
        finish(m)

    def side(m, part):
        return g_ref[m, part].reshape(width, part_width)

    def complex_rows_here(lhs, m):
        n = lhs.shape[0] // 2
        pr = jnp.dot(lhs, side(m, 0), preferred_element_type=f32)
        pi = jnp.dot(lhs, side(m, 1), preferred_element_type=f32)
        return pr[:n] - pi[n:], pi[:n] + pr[n:]

    @pl.when(plane == last)
    def _():
        piece_wait(0, y)
        near(0, y, shifts=(-2, -1))
        ready_wait(1)
        near(0, y, shifts=(1,))
        ready_wait(2)
        near(0, y, shifts=(2,))
        piece_wait(0, y_peer)
        near(0, y_peer)
        share(0, 0)
        piece_wait(1, y)
        near(1, y, lambda s: ~relays_to(s))
        hop(0, y, 2)
        hop(0, y_peer, 2)
        for yy in order:
            for d in range(3, outer):
                hop(0, yy, d)
        near(1, y, relays_to)
        piece_wait(1, y_peer)
        near(1, y_peer)
        share(1, 0)
        got(left_ref.at[:, y], left_recv.at[0])

    for copy in args:
        copy.wait()
    eye = (lax.broadcasted_iota(jnp.int32, (sources, sources), 0)
           == lax.broadcasted_iota(jnp.int32, (sources, sources), 1))
    cell = jnp.sum(jnp.where(eye, cell_ref[...], 0), axis=1, keepdims=True)
    slab = jnp.sum(jnp.where(eye, slab_ref[...], 0), axis=1, keepdims=True)
    offset = lax.broadcasted_iota(jnp.int32, (sources, width), 1) - cell
    offset = jnp.where(offset < 0, offset + width, offset)
    inside = offset < width // 4
    for part in range(2):
        amp = amp_ref[:, part * width:(part + 1) * width].astype(f32)
        x_ref[part, y] = jnp.where(inside & (slab == 0), amp, 0.0).astype(bf16)
        base_ref[part, y] = jnp.where(inside & (slab == 1), amp, 0.0).astype(bf16)

    @pl.when(plane != last)
    def _():
        ready_wait(1)
        ready_wait(2)
        for part in range(2):
            got(slot(0, part), in_recv.at[y] if part == 0 else in_recv.at[2 * Y])
            near(0, y, part=part)
        piece_wait(0, y_peer)
        near(0, y_peer)
        share(0, 0)
        hops = [(y, 1), (y, 2), (y_peer, 1), (y_peer, 2)]
        for u, (part, h) in enumerate(left_units):
            got(left_rows(part, h, y), left_recv.at[u])
            left_relay(u, part, h).start()
            hop(0, *hops[u])
        for yy in order:
            for d in range(3, outer):
                hop(0, yy, d)
        for yy in order:
            piece_wait(1, yy)
            near(1, yy)
        share(1, 0)

    for d in range(1, outer):
        rest(0, d)
        share(0, d)
    got(left_ref.at[:, y_peer], left_recv.at[len(left_units)])
    finish(0)

    def x_swap(yy):
        ref = x_ref.at[:, yy]
        return remote(ref, ref, x_send.at[0], x_recv.at[0], dev(plane, z, y_peer, core))

    def base_swap(yy, quarter):
        ref = base_ref.at[:, yy, :, cols(quarter)]
        return remote(ref, ref, x_send.at[1], x_recv.at[1], dev(plane, z, y_peer, core))

    def coup_copy(yy, k, quarter):
        p, to_y = others[k]
        ref = coup_ref.at[yy].at[:, cols(quarter)]
        return remote(ref, ref, c_send.at[0], c_recv.at[yy], dev(p, z, to_y, core))

    re, im = complex_rows_here(left_ref[...].reshape(2 * Y * depth, width), 0)
    for u in parts:
        coup_ref[u, 0:rows, cols(q)] = re[u * rows:(u + 1) * rows].astype(bf16)
        coup_ref[u, rows:, cols(q)] = im[u * rows:(u + 1) * rows].astype(bf16)
        for k in range(len(others)):
            coup_copy(u, k, q).start()

    x_swap(y).start()
    base_swap(y, plane * Y + y_peer).start()

    for yy in order:
        for d in range(2, outer):
            hop(1, yy, d)
    collect(1)
    trio = len(others) * part_width
    for u in parts:
        got(coup_ref.at[u, :, 0:trio], c_recv.at[u])
        re, im = complex_rows_here(coup_ref[u], 1)
        here = slice(u % per * rows, (u % per + 1) * rows)
        for part, value in ((0, re), (1, im)):
            start = g_ref[1, part, z * Y + u // per, core, here]
            g_ref[2, part, z * Y + u // per, core, here] = (value + start.astype(f32)).astype(bf16)
        near(2, u, outward)
    for u in parts:
        near(2, u, inner)
    share(2, 0)
    for u in parts:
        for d in range(2, outer):
            hop(2, u, d)
    for d in range(1, outer):
        rest(2, d)
        share(2, d)
    x_swap(y_peer).wait_recv()
    base_swap(y_peer, q).wait_recv()
    finish(2)

    re, im = complex_rows_here(x_ref[...].reshape(2 * Y * sources, width), 2)
    for part, value in ((0, re), (1, im)):
        start = base_ref[part, :, :, cols(q)].astype(f32)
        f_ref[part] = (value.reshape(Y, sources, part_width) + start).astype(bf16)

    lhs = f_ref[...].reshape(2 * Y * sources, part_width)
    n = Y * sources
    tile = Y * CORE * depth

    def d_copy(k, yy, j):
        spots = slice(j * tile, (j + 1) * tile)
        return remote(d_ref.at[:, yy, :, spots], far_ref.at[k].at[:, :, spots],
                      d_send.at[0], d_recv.at[j], dev(0, z, yy, core))

    def f_copy(yy):
        return remote(f_ref.at[:, yy], whole_ref.at[:, :, cols(q)], f_send.at[0],
                      f_recv.at[0], dev(last, z, yy, core))

    handed, direct = range(outer // 2), range(outer // 2, outer)

    def hand_copy(j):
        spots = slice(j * tile, (j + 1) * tile)
        return remote(d_ref.at[:, y_peer, :, spots], hand_ref.at[:, :, spots], d_send.at[0], hand_recv.at[j],
                      dev(plane, z, y_peer, core))

    for j in (direct[0], *handed, *direct[1:]):
        spots = slice(j * tile, (j + 1) * tile)
        dims = (((1,), (1,)), ((), ()))
        right = [g_ref[2, part, j * Y:(j + 1) * Y].reshape(tile, part_width) for part in range(2)]
        pr = lax.dot_general(lhs, right[0], dims, preferred_element_type=f32)
        pi = lax.dot_general(lhs, right[1], dims, preferred_element_type=f32)
        d_ref[0, :, :, spots] = (pr[:n] - pi[n:]).astype(bf16).reshape(Y, sources, tile)
        d_ref[1, :, :, spots] = (pi[:n] + pr[n:]).astype(bf16).reshape(Y, sources, tile)

        @pl.when(plane == last)
        def _():
            if j in handed:
                hand_copy(j).start()
            else:
                d_copy(2, y_peer, j).start()
                d_copy(0, y, j).start()

        @pl.when(plane != last)
        def _():
            d_copy(1, y_peer, j).start()

    @pl.when(plane == last)
    def _():
        f_copy(y_peer).start()
        for j in handed:
            spots = slice(j * tile, (j + 1) * tile)
            got(hand_ref.at[:, :, spots], hand_recv.at[j])
            for part in range(2):
                d_ref[part, y, :, spots] = (d_ref[part, y, :, spots].astype(f32)
                                            + hand_ref[part, :, spots].astype(f32)).astype(bf16)
            d_copy(0, y, j).start()

    @pl.when(plane != last)
    def _():
        f_copy(y_peer).start()
        f_copy(y).start()

    @pl.when(plane == last)
    def _():
        sent(r_hbm.at[0, :, :, 0:6 * part_width], in_send.at[0])
        sent(left_ref, left_send.at[0])

    @pl.when(plane != last)
    def _():
        sent(left_ref.at[:, 0], left_send.at[0])

    x_swap(y).wait_send()
    base_swap(y, plane * Y + y_peer).wait_send()
    sent(coup_ref.at[:, :, 0:trio], c_send.at[0])
    sent(g_ref.at[:, :, :, 0], core_send.at[0])
    for zz in range(outer):
        count = sum(0 <= zz + s < outer for s in reach)
        hops = (max(zz - 1, 0) + max(outer - 2 - zz, 0)) * (0 < zz < outer - 1)

        @pl.when(z == zz)
        def _():
            sent(g_ref.at[:, :, 0:Y * count, 0], z_send.at[0])
            if hops:
                sent(g_ref.at[:, :, 0:Y * hops, 0], relay_send.at[0])

    @pl.when(plane == last)
    def _():
        whole_ref[:, :, cols(q)] = f_ref[:, y]
        got(whole_ref.at[:, :, 0:trio], f_recv.at[0])
        for part in range(2):
            out_ref[:, part * width:(part + 1) * width] = whole_ref[part].astype(f32)
        sent(d_ref, d_send.at[0])
        sent(f_ref.at[:, 0], f_send.at[0])

    @pl.when(plane != last)
    def _():
        for j in (*direct, *handed):
            spots = slice(j * tile, (j + 1) * tile)
            count = len(others) - (j in handed)
            got(far_ref.at[0:count, :, :, spots], d_recv.at[j])
            for part in range(2):
                total = d_ref.at[part][y, :, spots].astype(f32)
                for k in range(count):
                    total = total + far_ref[k, part, :, spots].astype(f32)
                out_ref[:, part * width + j * tile:part * width + (j + 1) * tile] = (
                    x_ref.at[part][y, :, spots].astype(f32) + total.astype(bf16).astype(f32))
        sent(d_ref.at[:, 0], d_send.at[0])
        sent(f_ref, f_send.at[0])


def pair_body(transmit, reflect, source_amp, source_cell, source_slab):
    outer = lax.axis_size("blk") // (Y * CORE)
    sources, double = source_amp.shape
    depth = transmit.shape[1]
    width = double // 2
    quarter = width // (PLANES * Y)
    bf16 = jnp.bfloat16
    hbm = pl.BlockSpec(memory_space=pltpu.HBM)
    sem = pltpu.SemaphoreType.DMA
    out = pl.pallas_call(
        functools.partial(pair_kernel, outer),
        out_shape=pltpu.VMEM((sources, double), jnp.float32),
        in_specs=[hbm] * 5,
        out_specs=pl.BlockSpec(memory_space=pltpu.VMEM),
        scratch_shapes=[
            pltpu.VMEM((sources, double), bf16),
            pltpu.VMEM((1, sources), jnp.int32),
            pltpu.VMEM((1, sources), jnp.int32),
            pltpu.VMEM((3, 2, outer * Y, CORE, depth, quarter), bf16),
            pltpu.VMEM((2, Y, depth, width), bf16),
            pltpu.VMEM((SPLIT, 2 * Y * depth // SPLIT, width), bf16),
            pltpu.VMEM((2, Y, sources, width), bf16),
            pltpu.VMEM((2, Y, sources, width), bf16),
            pltpu.VMEM((2, Y, sources, quarter), bf16),
            pltpu.VMEM((2, sources, width), bf16),
            pltpu.VMEM((2, Y, sources, width), bf16),
            pltpu.VMEM((PLANES * Y - 1, 2, sources, width), bf16),
            pltpu.VMEM((2, sources, width), bf16),
            pltpu.SemaphoreType.REGULAR((2,)),
            sem((3,)),
            sem((1,)),
            sem((2 * Y + 1,)),
            sem((1,)),
            sem((5,)),
            sem((1,)),
            sem(((outer - 1) * (2 * Y + SPLIT),)),
            sem((1,)),
            sem((1,)),
            sem((3,)),
            sem((1,)),
            sem((SPLIT,)),
            sem((2,)),
            sem((2,)),
            sem((1,)),
            sem((1,)),
            sem((1,)),
            sem((outer,)),
            sem((outer // 2,)),
        ],
        compiler_params=pltpu.CompilerParams(
            collective_id=0, has_side_effects=True, vmem_limit_bytes=32 << 20),
    )(*(pltpu.with_memory_space_constraint(a, pltpu.HBM) for a in (
        transmit, reflect, source_amp, source_cell[None], source_slab[None])))
    return out[None]


def solution(mesh):
    pair = mesh.shape["slab"] == PLANES and mesh.shape["blk"] % (Y * CORE) == 0 and mesh.shape["blk"] > 2 * Y * CORE
    return jax.shard_map(
        pair_body if pair else body,
        mesh=mesh,
        in_specs=(
            P("slab", "blk", None),
            P("slab", None, "blk", None),
            P("blk", None),
            P("blk"),
            P("blk"),
        ),
        out_specs=P("slab", "blk", None),
        check_vma=False,
    )
```

```python
import functools

import jax
import jax.numpy as jnp
from jax import lax
from jax.experimental import pallas as pl
from jax.experimental.pallas import tpu as pltpu
from jax.sharding import PartitionSpec as P


def shifted(block, axis, distance):
    devices = range(lax.axis_size(axis))
    route = [(i - distance, i) for i in devices if i - distance in devices]
    return lax.ppermute(block, axis, route)


def transposed(matrix):
    half_width = matrix.shape[0]
    return jnp.concatenate([matrix[:, :half_width].T, matrix[:, half_width:].T], 1)


def complex_rows(left_rows, right_matrix):
    inner_width = right_matrix.shape[0]
    outer_width = right_matrix.shape[1] // 2
    row_count = left_rows.shape[0]
    stacked = jnp.concatenate([left_rows[:, :inner_width], left_rows[:, inner_width:]], 0)
    product = jnp.dot(stacked, right_matrix, preferred_element_type=jnp.float32)
    real_out = product[:row_count, :outer_width] - product[row_count:, outer_width:]
    imag_out = product[:row_count, outer_width:] + product[row_count:, :outer_width]
    return jnp.concatenate([real_out, imag_out], 1)


def body(transmit, reflect, source_amp, source_cell, source_slab):
    trans_local = transmit[0]
    refl_local = reflect[0]
    half_width = source_amp.shape[1] // 2
    refl_second = lax.all_gather(refl_local[1], "blk", axis=0, tiled=True)
    coupling = complex_rows(refl_local[0], refl_second).astype(jnp.bfloat16)
    start_rows = trans_local.astype(jnp.float32)
    piece_rows = lax.all_gather(trans_local, "blk", axis=0, tiled=True)
    piece_count = piece_rows.shape[0]
    real_cols = lax.slice_in_dim(coupling, 0, piece_count, axis=1)
    imag_cols = lax.dynamic_slice_in_dim(coupling, half_width, piece_count, 1)
    left_rows = jnp.concatenate([real_cols, imag_cols], 1)
    joined = (start_rows + complex_rows(left_rows, piece_rows)).astype(jnp.bfloat16)
    slab_matrix = lax.all_gather(joined, "blk", axis=0, tiled=True)
    back_matrix = transposed(slab_matrix)
    cell_index = lax.iota(jnp.int32, half_width)
    offset = (cell_index[None, :] - source_cell[:, None]) % half_width
    inside = offset < half_width // 4
    here = source_slab == lax.axis_index("slab")
    keep = inside & here[:, None]
    keep = jnp.concatenate([keep, keep], 1)
    forcing = jnp.where(keep, source_amp, jnp.zeros_like(source_amp))
    chain_length = lax.axis_size("slab")
    carried = forcing
    for sweep_step in range(chain_length - 1):
        arrived = shifted(carried, "slab", 1)
        carried = (forcing.astype(jnp.float32) + complex_rows(arrived, slab_matrix)).astype(
            jnp.bfloat16
        )
    current = carried.astype(jnp.float32)
    for sweep_step in range(chain_length - 1):
        message = complex_rows(current.astype(jnp.bfloat16), back_matrix).astype(jnp.bfloat16)
        arrived = shifted(message, "slab", -1)
        current = carried.astype(jnp.float32) + arrived.astype(jnp.float32)
    return current[None]


MESH = pl.DeviceIdType.MESH
Y = 2
CORE = 2
PLANES = 2
SPLIT = 4


def pair_kernel(
    outer, t_hbm, r_hbm, amp_hbm, cell_hbm, slab_hbm, out_ref,
    amp_ref, cell_ref, slab_ref, g_ref, left_ref, coup_ref, x_ref, base_ref,
    f_ref, whole_ref, d_ref, far_ref, hand_ref,
    ready, arg_sem, in_send, in_recv, left_send, left_recv, z_send, z_recv, relay_send,
    core_send, core_recv, c_send, c_recv, x_send, x_recv, f_send, f_recv, d_send, d_recv, hand_recv,
):
    plane = lax.axis_index("slab")
    me = lax.axis_index("blk")
    z, y, core = me // (Y * CORE), (me // CORE) % Y, me % CORE
    last = PLANES - 1
    depth = t_hbm.shape[1]
    half = depth // 2
    width = t_hbm.shape[2] // 2
    part_width = width // (PLANES * Y)
    sources = amp_hbm.shape[0]
    y_peer, c_peer, x_peer = 1 - y, 1 - core, 1 - plane
    q = plane * Y + y
    f32, bf16 = jnp.float32, jnp.bfloat16
    others = ((x_peer, y), (plane, y_peer), (x_peer, y_peer))
    order = (y, y_peer)
    rows = coup_ref.shape[1] // 2
    per = depth // rows
    parts = range(Y * per)

    def dev(p, zz, yy, cc):
        return (p, (zz * Y + yy) * CORE + cc)

    def cols(quarter, base=0):
        return pl.ds(pl.multiple_of(base + quarter * part_width, part_width), part_width)

    def remote(s, d, ss, rs, to):
        return pltpu.make_async_remote_copy(
            src_ref=s, dst_ref=d, send_sem=ss, recv_sem=rs, device_id=to, device_id_type=MESH)

    def got(ref, sem):
        pltpu.make_async_copy(ref, ref, sem).wait()

    def sent(ref, sem):
        remote(ref, ref, sem, sem, dev(plane, z, y, c_peer)).wait_send()

    def valid(zz):
        return (zz >= 0) & (zz < outer)

    def unit(m, zz, u):
        if m < 2:
            return g_ref.at[m].at[:, zz * Y + u, core]
        return g_ref.at[m].at[:, zz * Y + u // per, core, u % per * rows:(u % per + 1) * rows]

    def piece(m, part, p, yy):
        s = r_hbm.at[0, 1] if m == 0 else t_hbm.at[0]
        return s.at[:, cols(p * Y + yy, part * width)]

    def slot(m, part):
        return g_ref.at[m, part].at[z * Y + y, core]

    def piece_local(m, part):
        return pltpu.make_async_copy(piece(m, part, last, y), slot(m, part), in_recv.at[m * Y + y])

    def piece_send(m, part, p, yy):
        split = m == 0 and part == 1 and p != last and yy is y
        return remote(piece(m, part, p, yy), slot(m, part), in_send.at[0],
                      in_recv.at[2 * Y] if split else in_recv.at[m * Y + y], dev(p, z, yy, core))

    def piece_wait(m, yy):
        got(unit(m, z, yy), in_recv.at[m * Y + yy])

    left_units = [(part, h) for part in range(2) for h in range(2)]

    def left_rows(part, h, yy):
        return left_ref.at[part].at[yy, h * half:(h + 1) * half]

    def left_src(part, h):
        return r_hbm.at[0, 0, h * half:(h + 1) * half, part * width:(part + 1) * width]

    def left_local(part):
        return pltpu.make_async_copy(
            r_hbm.at[0, 0, :, part * width:(part + 1) * width], left_ref.at[part].at[y], left_recv.at[0])

    def left_push(u, part, h, k):
        to = dev(0, z, y, core) if k == 0 else dev(last, z, y_peer, core)
        return remote(left_src(part, h), left_rows(part, h, y), left_send.at[0],
                      left_recv.at[u if k == 0 else len(left_units)], to)

    def left_relay(u, part, h):
        ref = left_rows(part, h, y)
        return remote(ref, ref, left_send.at[0], left_recv.at[len(left_units)], dev(plane, z, y_peer, core))

    args = [pltpu.make_async_copy(a, b, arg_sem.at[i]) for i, (a, b) in enumerate(
        ((amp_hbm, amp_ref), (cell_hbm, cell_ref), (slab_hbm, slab_ref)))]

    barrier = pltpu.get_barrier_semaphore()

    def tell(sem, to, when=None):
        def send():
            pl.semaphore_signal(sem, inc=1, device_id=to, device_id_type=MESH)
        send() if when is None else pl.when(when)(send)

    for p, yy, cc in ((plane, y, c_peer), (plane, y_peer, core), (x_peer, y, core), (x_peer, y_peer, core)):
        tell(barrier, dev(p, z, yy, cc))
    for s in (1, 2):
        tell(barrier, dev(plane, z + s, y, core), valid(z + s))

    @pl.when(plane == last)
    def _():
        for m in range(2):
            for part in range(2):
                piece_local(m, part).start()
        for part in range(2):
            left_local(part).start()

    for copy in args:
        copy.start()
    pl.semaphore_wait(barrier, 4 + jnp.minimum(z, 2))
    for s in (1, 2):
        tell(ready.at[s - 1], dev(plane, z - s, y, core), valid(z - s))

    @pl.when(plane == last)
    def _():
        for p, yy in ((0, y), (last, y_peer), (0, y_peer)):
            for part in range(2):
                piece_send(0, part, p, yy).start()
        for u, (part, h) in enumerate(left_units):
            for k in range(2):
                left_push(u, part, h, k).start()
        for p, yy in ((0, y), (last, y_peer), (0, y_peer)):
            for part in range(2):
                piece_send(1, part, p, yy).start()

    def z_sem(m, shift, yy):
        k = shift % outer - 1
        return z_recv.at[(m * (outer - 1) + k) * Y + yy if m < 2 else (2 * (outer - 1) + k * per) * Y + yy]

    reach = (-2, 2, -1, 1)

    def near(m, yy, when=lambda s: True, part=None, shifts=reach):
        for s in shifts:
            @pl.when(valid(z + s) & when(s))
            def _():
                ref = unit(m, z, yy) if part is None else slot(m, part)
                remote(ref, ref, z_send.at[0], z_sem(m, -s, yy), dev(plane, z + s, y, core)).start()

    def inner(s):
        return (z + s > 0) & (z + s < outer - 1) if abs(s) == 1 else z < 0

    def outward(s):
        return ~inner(s)

    def ready_wait(s):
        @pl.when(valid(z + s))
        def _():
            pl.semaphore_wait(ready.at[s - 1], 1)

    def relays_to(s):
        return {1: (z >= 2) & valid(z + 1), -1: (z <= outer - 3) & valid(z - 1)}.get(s, z < 0)

    def onward_ok(s):
        return valid(z + s) & valid(z + (-1 if s > 0 else 1)) & (abs(s) > 1)

    def hop(m, yy, d):
        for s in (d, -d) if d > 1 else ():
            @pl.when(onward_ok(s))
            def _():
                onward = -1 if s > 0 else 1
                ref = unit(m, z + s, yy)
                got(ref, z_sem(m, s, yy))
                remote(ref, ref, relay_send.at[0], z_sem(m, s - onward, yy),
                       dev(plane, z + onward, y, core)).start()

    def rest(m, d):
        for s in (d, -d):
            @pl.when(valid(z + s) & ~onward_ok(s))
            def _():
                for yy in range(Y) if m < 2 else parts:
                    got(unit(m, z + s, yy), z_sem(m, s, yy))

    def chunk(m, zz, cc):
        return g_ref.at[m].at[:, pl.ds(zz * Y, Y), cc]

    def core_copy(m, zz, cc):
        return remote(chunk(m, zz, cc), chunk(m, zz, cc), core_send.at[0], core_recv.at[m],
                      dev(plane, z, y, c_peer))

    def share(m, d):
        for s in ((d, -d) if d else (0,)):
            @pl.when(valid(z + s))
            def _():
                core_copy(m, z + s, core).start()

    def finish(m):
        got(g_ref.at[m].at[:, :, c_peer], core_recv.at[m])

    def collect(m):
        for d in range(1, outer):
            rest(m, d)
            share(m, d)
        finish(m)

    def side(m, part):
        return g_ref[m, part].reshape(width, part_width)

    def complex_rows_here(lhs, m):
        n = lhs.shape[0] // 2
        pr = jnp.dot(lhs, side(m, 0), preferred_element_type=f32)
        pi = jnp.dot(lhs, side(m, 1), preferred_element_type=f32)
        return pr[:n] - pi[n:], pi[:n] + pr[n:]

    @pl.when(plane == last)
    def _():
        piece_wait(0, y)
        near(0, y, shifts=(-2, -1))
        ready_wait(1)
        near(0, y, shifts=(1,))
        ready_wait(2)
        near(0, y, shifts=(2,))
        piece_wait(0, y_peer)
        near(0, y_peer)
        share(0, 0)
        piece_wait(1, y)
        near(1, y, lambda s: ~relays_to(s))
        hop(0, y, 2)
        hop(0, y_peer, 2)
        for yy in order:
            for d in range(3, outer):
                hop(0, yy, d)
        near(1, y, relays_to)
        piece_wait(1, y_peer)
        near(1, y_peer)
        share(1, 0)
        got(left_ref.at[:, y], left_recv.at[0])

    for copy in args:
        copy.wait()
    eye = (lax.broadcasted_iota(jnp.int32, (sources, sources), 0)
           == lax.broadcasted_iota(jnp.int32, (sources, sources), 1))
    cell = jnp.sum(jnp.where(eye, cell_ref[...], 0), axis=1, keepdims=True)
    slab = jnp.sum(jnp.where(eye, slab_ref[...], 0), axis=1, keepdims=True)
    offset = lax.broadcasted_iota(jnp.int32, (sources, width), 1) - cell
    offset = jnp.where(offset < 0, offset + width, offset)
    inside = offset < width // 4
    for part in range(2):
        amp = amp_ref[:, part * width:(part + 1) * width].astype(f32)
        x_ref[part, y] = jnp.where(inside & (slab == 0), amp, 0.0).astype(bf16)
        base_ref[part, y] = jnp.where(inside & (slab == 1), amp, 0.0).astype(bf16)

    @pl.when(plane != last)
    def _():
        ready_wait(1)
        ready_wait(2)
        for part in range(2):
            got(slot(0, part), in_recv.at[y] if part == 0 else in_recv.at[2 * Y])
            near(0, y, part=part)
        piece_wait(0, y_peer)
        near(0, y_peer)
        share(0, 0)
        hops = [(y, 1), (y, 2), (y_peer, 1), (y_peer, 2)]
        for u, (part, h) in enumerate(left_units):
            got(left_rows(part, h, y), left_recv.at[u])
            left_relay(u, part, h).start()
            hop(0, *hops[u])
        for yy in order:
            for d in range(3, outer):
                hop(0, yy, d)
        for yy in order:
            piece_wait(1, yy)
            near(1, yy)
        share(1, 0)

    for d in range(1, outer):
        rest(0, d)
        share(0, d)
    got(left_ref.at[:, y_peer], left_recv.at[len(left_units)])
    finish(0)

    def x_swap(yy):
        ref = x_ref.at[:, yy]
        return remote(ref, ref, x_send.at[0], x_recv.at[0], dev(plane, z, y_peer, core))

    def base_swap(yy, quarter):
        ref = base_ref.at[:, yy, :, cols(quarter)]
        return remote(ref, ref, x_send.at[1], x_recv.at[1], dev(plane, z, y_peer, core))

    def coup_copy(yy, k, quarter):
        p, to_y = others[k]
        ref = coup_ref.at[yy].at[:, cols(quarter)]
        return remote(ref, ref, c_send.at[0], c_recv.at[yy], dev(p, z, to_y, core))

    for yy in range(Y):
        re, im = complex_rows_here(left_ref[:, yy].reshape(2 * depth, width), 0)
        for u in range(yy * per, (yy + 1) * per):
            here = slice(u % per * rows, (u % per + 1) * rows)
            coup_ref[u, 0:rows, cols(q)] = re[here].astype(bf16)
            coup_ref[u, rows:, cols(q)] = im[here].astype(bf16)
            for k in range(len(others)):
                coup_copy(u, k, q).start()


    for yy in order:
        for d in range(2, outer):
            hop(1, yy, d)
    collect(1)
    trio = len(others) * part_width
    for u in parts:
        got(coup_ref.at[u, :, 0:trio], c_recv.at[u])
        re, im = complex_rows_here(coup_ref[u], 1)
        here = slice(u % per * rows, (u % per + 1) * rows)
        for part, value in ((0, re), (1, im)):
            start = g_ref[1, part, z * Y + u // per, core, here]
            g_ref[2, part, z * Y + u // per, core, here] = (value + start.astype(f32)).astype(bf16)
        near(2, u, outward)
    x_swap(y).start()
    base_swap(y, plane * Y + y_peer).start()
    share(2, 0)
    for u in parts[:len(parts) // 2]:
        near(2, u, inner)
    for u in parts:
        for d in range(2, outer):
            hop(2, u, d)
        if u >= len(parts) // 2:
            near(2, u, inner)
    for d in range(1, outer):
        rest(2, d)
        share(2, d)
    x_swap(y_peer).wait_recv()
    base_swap(y_peer, q).wait_recv()
    finish(2)

    re, im = complex_rows_here(x_ref[...].reshape(2 * Y * sources, width), 2)
    for part, value in ((0, re), (1, im)):
        start = base_ref[part, :, :, cols(q)].astype(f32)
        f_ref[part] = (value.reshape(Y, sources, part_width) + start).astype(bf16)

    lhs = f_ref[...].reshape(2 * Y * sources, part_width)
    n = Y * sources
    tile = Y * CORE * depth

    def d_copy(k, yy, j):
        spots = slice(j * tile, (j + 1) * tile)
        return remote(d_ref.at[:, yy, :, spots], far_ref.at[k].at[:, :, spots],
                      d_send.at[0], d_recv.at[j], dev(0, z, yy, core))

    def f_copy(yy):
        return remote(f_ref.at[:, yy], whole_ref.at[:, :, cols(q)], f_send.at[0],
                      f_recv.at[0], dev(last, z, yy, core))

    handed, direct = range(outer // 2), range(outer // 2, outer)

    def hand_copy(j):
        spots = slice(j * tile, (j + 1) * tile)
        return remote(d_ref.at[:, y_peer, :, spots], hand_ref.at[:, :, spots], d_send.at[0], hand_recv.at[j],
                      dev(plane, z, y_peer, core))

    for j in (direct[0], *handed, *direct[1:]):
        spots = slice(j * tile, (j + 1) * tile)
        dims = (((1,), (1,)), ((), ()))
        right = [g_ref[2, part, j * Y:(j + 1) * Y].reshape(tile, part_width) for part in range(2)]
        pr = lax.dot_general(lhs, right[0], dims, preferred_element_type=f32)
        pi = lax.dot_general(lhs, right[1], dims, preferred_element_type=f32)
        d_ref[0, :, :, spots] = (pr[:n] - pi[n:]).astype(bf16).reshape(Y, sources, tile)
        d_ref[1, :, :, spots] = (pi[:n] + pr[n:]).astype(bf16).reshape(Y, sources, tile)

        @pl.when(plane == last)
        def _():
            if j in handed:
                hand_copy(j).start()
            else:
                d_copy(2, y_peer, j).start()
                d_copy(0, y, j).start()

        @pl.when(plane != last)
        def _():
            d_copy(1, y_peer, j).start()

    @pl.when(plane == last)
    def _():
        f_copy(y_peer).start()
        for j in handed:
            spots = slice(j * tile, (j + 1) * tile)
            got(hand_ref.at[:, :, spots], hand_recv.at[j])
            for part in range(2):
                d_ref[part, y, :, spots] = (d_ref[part, y, :, spots].astype(f32)
                                            + hand_ref[part, :, spots].astype(f32)).astype(bf16)
            d_copy(0, y, j).start()

    @pl.when(plane != last)
    def _():
        f_copy(y_peer).start()
        f_copy(y).start()

    @pl.when(plane == last)
    def _():
        sent(r_hbm.at[0, :, :, 0:6 * part_width], in_send.at[0])
        sent(left_ref, left_send.at[0])

    @pl.when(plane != last)
    def _():
        sent(left_ref.at[:, 0], left_send.at[0])

    x_swap(y).wait_send()
    base_swap(y, plane * Y + y_peer).wait_send()
    sent(coup_ref.at[:, :, 0:trio], c_send.at[0])
    sent(g_ref.at[:, :, :, 0], core_send.at[0])
    for zz in range(outer):
        count = sum(0 <= zz + s < outer for s in reach)
        hops = (max(zz - 1, 0) + max(outer - 2 - zz, 0)) * (0 < zz < outer - 1)

        @pl.when(z == zz)
        def _():
            sent(g_ref.at[:, :, 0:Y * count, 0], z_send.at[0])
            if hops:
                sent(g_ref.at[:, :, 0:Y * hops, 0], relay_send.at[0])

    @pl.when(plane == last)
    def _():
        whole_ref[:, :, cols(q)] = f_ref[:, y]
        got(whole_ref.at[:, :, 0:trio], f_recv.at[0])
        for part in range(2):
            out_ref[:, part * width:(part + 1) * width] = whole_ref[part].astype(f32)
        sent(d_ref, d_send.at[0])
        sent(f_ref.at[:, 0], f_send.at[0])

    @pl.when(plane != last)
    def _():
        for j in (*direct, *handed):
            spots = slice(j * tile, (j + 1) * tile)
            count = len(others) - (j in handed)
            got(far_ref.at[0:count, :, :, spots], d_recv.at[j])
            for part in range(2):
                total = d_ref.at[part][y, :, spots].astype(f32)
                for k in range(count):
                    total = total + far_ref[k, part, :, spots].astype(f32)
                out_ref[:, part * width + j * tile:part * width + (j + 1) * tile] = (
                    x_ref.at[part][y, :, spots].astype(f32) + total.astype(bf16).astype(f32))
        sent(d_ref.at[:, 0], d_send.at[0])
        sent(f_ref, f_send.at[0])


def pair_body(transmit, reflect, source_amp, source_cell, source_slab):
    outer = lax.axis_size("blk") // (Y * CORE)
    sources, double = source_amp.shape
    depth = transmit.shape[1]
    width = double // 2
    quarter = width // (PLANES * Y)
    bf16 = jnp.bfloat16
    hbm = pl.BlockSpec(memory_space=pltpu.HBM)
    sem = pltpu.SemaphoreType.DMA
    out = pl.pallas_call(
        functools.partial(pair_kernel, outer),
        out_shape=pltpu.VMEM((sources, double), jnp.float32),
        in_specs=[hbm] * 5,
        out_specs=pl.BlockSpec(memory_space=pltpu.VMEM),
        scratch_shapes=[
            pltpu.VMEM((sources, double), bf16),
            pltpu.VMEM((1, sources), jnp.int32),
            pltpu.VMEM((1, sources), jnp.int32),
            pltpu.VMEM((3, 2, outer * Y, CORE, depth, quarter), bf16),
            pltpu.VMEM((2, Y, depth, width), bf16),
            pltpu.VMEM((SPLIT, 2 * Y * depth // SPLIT, width), bf16),
            pltpu.VMEM((2, Y, sources, width), bf16),
            pltpu.VMEM((2, Y, sources, width), bf16),
            pltpu.VMEM((2, Y, sources, quarter), bf16),
            pltpu.VMEM((2, sources, width), bf16),
            pltpu.VMEM((2, Y, sources, width), bf16),
            pltpu.VMEM((PLANES * Y - 1, 2, sources, width), bf16),
            pltpu.VMEM((2, sources, width), bf16),
            pltpu.SemaphoreType.REGULAR((2,)),
            sem((3,)),
            sem((1,)),
            sem((2 * Y + 1,)),
            sem((1,)),
            sem((5,)),
            sem((1,)),
            sem(((outer - 1) * (2 * Y + SPLIT),)),
            sem((1,)),
            sem((1,)),
            sem((3,)),
            sem((1,)),
            sem((SPLIT,)),
            sem((2,)),
            sem((2,)),
            sem((1,)),
            sem((1,)),
            sem((1,)),
            sem((outer,)),
            sem((outer // 2,)),
        ],
        compiler_params=pltpu.CompilerParams(
            collective_id=0, has_side_effects=True, vmem_limit_bytes=32 << 20),
    )(*(pltpu.with_memory_space_constraint(a, pltpu.HBM) for a in (
        transmit, reflect, source_amp, source_cell[None], source_slab[None])))
    return out[None]


def solution(mesh):
    pair = mesh.shape["slab"] == PLANES and mesh.shape["blk"] % (Y * CORE) == 0 and mesh.shape["blk"] > 2 * Y * CORE
    return jax.shard_map(
        pair_body if pair else body,
        mesh=mesh,
        in_specs=(
            P("slab", "blk", None),
            P("slab", None, "blk", None),
            P("blk", None),
            P("blk"),
            P("blk"),
        ),
        out_specs=P("slab", "blk", None),
        check_vma=False,
    )
```

```python
import functools

import jax
import jax.numpy as jnp
from jax import lax
from jax.experimental import pallas as pl
from jax.experimental.pallas import tpu as pltpu
from jax.sharding import PartitionSpec as P


def shifted(block, axis, distance):
    devices = range(lax.axis_size(axis))
    route = [(i - distance, i) for i in devices if i - distance in devices]
    return lax.ppermute(block, axis, route)


def transposed(matrix):
    half_width = matrix.shape[0]
    return jnp.concatenate([matrix[:, :half_width].T, matrix[:, half_width:].T], 1)


def complex_rows(left_rows, right_matrix):
    inner_width = right_matrix.shape[0]
    outer_width = right_matrix.shape[1] // 2
    row_count = left_rows.shape[0]
    stacked = jnp.concatenate([left_rows[:, :inner_width], left_rows[:, inner_width:]], 0)
    product = jnp.dot(stacked, right_matrix, preferred_element_type=jnp.float32)
    real_out = product[:row_count, :outer_width] - product[row_count:, outer_width:]
    imag_out = product[:row_count, outer_width:] + product[row_count:, :outer_width]
    return jnp.concatenate([real_out, imag_out], 1)


def body(transmit, reflect, source_amp, source_cell, source_slab):
    trans_local = transmit[0]
    refl_local = reflect[0]
    half_width = source_amp.shape[1] // 2
    refl_second = lax.all_gather(refl_local[1], "blk", axis=0, tiled=True)
    coupling = complex_rows(refl_local[0], refl_second).astype(jnp.bfloat16)
    start_rows = trans_local.astype(jnp.float32)
    piece_rows = lax.all_gather(trans_local, "blk", axis=0, tiled=True)
    piece_count = piece_rows.shape[0]
    real_cols = lax.slice_in_dim(coupling, 0, piece_count, axis=1)
    imag_cols = lax.dynamic_slice_in_dim(coupling, half_width, piece_count, 1)
    left_rows = jnp.concatenate([real_cols, imag_cols], 1)
    joined = (start_rows + complex_rows(left_rows, piece_rows)).astype(jnp.bfloat16)
    slab_matrix = lax.all_gather(joined, "blk", axis=0, tiled=True)
    back_matrix = transposed(slab_matrix)
    cell_index = lax.iota(jnp.int32, half_width)
    offset = (cell_index[None, :] - source_cell[:, None]) % half_width
    inside = offset < half_width // 4
    here = source_slab == lax.axis_index("slab")
    keep = inside & here[:, None]
    keep = jnp.concatenate([keep, keep], 1)
    forcing = jnp.where(keep, source_amp, jnp.zeros_like(source_amp))
    chain_length = lax.axis_size("slab")
    carried = forcing
    for sweep_step in range(chain_length - 1):
        arrived = shifted(carried, "slab", 1)
        carried = (forcing.astype(jnp.float32) + complex_rows(arrived, slab_matrix)).astype(
            jnp.bfloat16
        )
    current = carried.astype(jnp.float32)
    for sweep_step in range(chain_length - 1):
        message = complex_rows(current.astype(jnp.bfloat16), back_matrix).astype(jnp.bfloat16)
        arrived = shifted(message, "slab", -1)
        current = carried.astype(jnp.float32) + arrived.astype(jnp.float32)
    return current[None]


MESH = pl.DeviceIdType.MESH
Y = 2
CORE = 2
PLANES = 2
SPLIT = 4


def pair_kernel(
    outer, t_hbm, r_hbm, amp_hbm, cell_hbm, slab_hbm, out_ref,
    amp_ref, cell_ref, slab_ref, g_ref, left_ref, coup_ref, x_ref, base_ref,
    f_ref, whole_ref, d_ref, far_ref, hand_ref,
    ready, arg_sem, in_send, in_recv, left_send, left_recv, z_send, z_recv, relay_send,
    core_send, core_recv, c_send, c_recv, x_send, x_recv, f_send, f_recv, d_send, d_recv, hand_recv,
):
    plane = lax.axis_index("slab")
    me = lax.axis_index("blk")
    z, y, core = me // (Y * CORE), (me // CORE) % Y, me % CORE
    last = PLANES - 1
    depth = t_hbm.shape[1]
    half = depth // 2
    width = t_hbm.shape[2] // 2
    part_width = width // (PLANES * Y)
    sources = amp_hbm.shape[0]
    y_peer, c_peer, x_peer = 1 - y, 1 - core, 1 - plane
    q = plane * Y + y
    f32, bf16 = jnp.float32, jnp.bfloat16
    others = ((x_peer, y), (plane, y_peer), (x_peer, y_peer))
    order = (y, y_peer)
    rows = coup_ref.shape[1] // 2
    per = depth // rows
    parts = range(Y * per)

    def dev(p, zz, yy, cc):
        return (p, (zz * Y + yy) * CORE + cc)

    def cols(quarter, base=0):
        return pl.ds(pl.multiple_of(base + quarter * part_width, part_width), part_width)

    def remote(s, d, ss, rs, to):
        return pltpu.make_async_remote_copy(
            src_ref=s, dst_ref=d, send_sem=ss, recv_sem=rs, device_id=to, device_id_type=MESH)

    def got(ref, sem):
        pltpu.make_async_copy(ref, ref, sem).wait()

    def sent(ref, sem):
        remote(ref, ref, sem, sem, dev(plane, z, y, c_peer)).wait_send()

    def valid(zz):
        return (zz >= 0) & (zz < outer)

    def unit(m, zz, u):
        if m < 2:
            return g_ref.at[m].at[:, zz * Y + u, core]
        return g_ref.at[m].at[:, zz * Y + u // per, core, u % per * rows:(u % per + 1) * rows]

    def piece(m, part, p, yy):
        s = r_hbm.at[0, 1] if m == 0 else t_hbm.at[0]
        return s.at[:, cols(p * Y + yy, part * width)]

    def slot(m, part):
        return g_ref.at[m, part].at[z * Y + y, core]

    def piece_local(m, part):
        return pltpu.make_async_copy(piece(m, part, last, y), slot(m, part), in_recv.at[m * Y + y])

    def piece_send(m, part, p, yy):
        split = m == 0 and part == 1 and p != last and yy is y
        return remote(piece(m, part, p, yy), slot(m, part), in_send.at[0],
                      in_recv.at[2 * Y] if split else in_recv.at[m * Y + y], dev(p, z, yy, core))

    def piece_wait(m, yy):
        got(unit(m, z, yy), in_recv.at[m * Y + yy])

    left_units = [(part, h) for part in range(2) for h in range(2)]

    def left_rows(part, h, yy):
        return left_ref.at[part].at[yy, h * half:(h + 1) * half]

    def left_src(part, h):
        return r_hbm.at[0, 0, h * half:(h + 1) * half, part * width:(part + 1) * width]

    def left_local(part):
        return pltpu.make_async_copy(
            r_hbm.at[0, 0, :, part * width:(part + 1) * width], left_ref.at[part].at[y], left_recv.at[0])

    def left_push(u, part, h, k):
        to = dev(0, z, y, core) if k == 0 else dev(last, z, y_peer, core)
        return remote(left_src(part, h), left_rows(part, h, y), left_send.at[0],
                      left_recv.at[u if k == 0 else len(left_units)], to)

    def left_relay(u, part, h):
        ref = left_rows(part, h, y)
        return remote(ref, ref, left_send.at[0], left_recv.at[len(left_units)], dev(plane, z, y_peer, core))

    args = [pltpu.make_async_copy(a, b, arg_sem.at[i]) for i, (a, b) in enumerate(
        ((amp_hbm, amp_ref), (cell_hbm, cell_ref), (slab_hbm, slab_ref)))]

    barrier = pltpu.get_barrier_semaphore()

    def tell(sem, to, when=None):
        def send():
            pl.semaphore_signal(sem, inc=1, device_id=to, device_id_type=MESH)
        send() if when is None else pl.when(when)(send)

    for p, yy, cc in ((plane, y, c_peer), (plane, y_peer, core), (x_peer, y, core), (x_peer, y_peer, core)):
        tell(barrier, dev(p, z, yy, cc))
    for s in (1, 2):
        tell(barrier, dev(plane, z + s, y, core), valid(z + s))

    @pl.when(plane == last)
    def _():
        for m in range(2):
            for part in range(2):
                piece_local(m, part).start()
        for part in range(2):
            left_local(part).start()

    for copy in args:
        copy.start()
    pl.semaphore_wait(barrier, 4 + jnp.minimum(z, 2))
    for s in (1, 2):
        tell(ready.at[s - 1], dev(plane, z - s, y, core), valid(z - s))

    @pl.when(plane == last)
    def _():
        for p, yy in ((0, y), (last, y_peer), (0, y_peer)):
            for part in range(2):
                piece_send(0, part, p, yy).start()
        for u, (part, h) in enumerate(left_units):
            for k in range(2):
                left_push(u, part, h, k).start()
        for p, yy in ((0, y), (last, y_peer), (0, y_peer)):
            for part in range(2):
                piece_send(1, part, p, yy).start()

    def z_sem(m, shift, yy):
        k = shift % outer - 1
        return z_recv.at[(m * (outer - 1) + k) * Y + yy if m < 2 else (2 * (outer - 1) + k * per) * Y + yy]

    reach = (-2, 2, -1, 1)

    def near(m, yy, when=lambda s: True, part=None, shifts=reach):
        for s in shifts:
            @pl.when(valid(z + s) & when(s))
            def _():
                ref = unit(m, z, yy) if part is None else slot(m, part)
                remote(ref, ref, z_send.at[0], z_sem(m, -s, yy), dev(plane, z + s, y, core)).start()

    def inner(s):
        return (z + s > 0) & (z + s < outer - 1) if abs(s) == 1 else z < 0

    def outward(s):
        return ~inner(s)

    def ready_wait(s):
        @pl.when(valid(z + s))
        def _():
            pl.semaphore_wait(ready.at[s - 1], 1)

    def relays_to(s):
        return {1: (z >= 2) & valid(z + 1), -1: (z <= outer - 3) & valid(z - 1)}.get(s, z < 0)

    def onward_ok(s):
        return valid(z + s) & valid(z + (-1 if s > 0 else 1)) & (abs(s) > 1)

    def hop(m, yy, d):
        for s in (d, -d) if d > 1 else ():
            @pl.when(onward_ok(s))
            def _():
                onward = -1 if s > 0 else 1
                ref = unit(m, z + s, yy)
                got(ref, z_sem(m, s, yy))
                remote(ref, ref, relay_send.at[0], z_sem(m, s - onward, yy),
                       dev(plane, z + onward, y, core)).start()

    def units(m):
        return order if m < 2 else parts

    def share(m, d, only=None):
        for s in ((d, -d) if d else (0,)):
            @pl.when(valid(z + s))
            def _():
                for u in units(m) if only is None else (only,):
                    ref = unit(m, z + s, u)
                    remote(ref, ref, core_send.at[0], core_recv.at[m], dev(plane, z, y, c_peer)).start()

    def rest(m, d):
        for u in units(m):
            for s in (d, -d):
                @pl.when(valid(z + s) & ~onward_ok(s))
                def _():
                    got(unit(m, z + s, u), z_sem(m, s, u))
            share(m, d, u)

    def finish(m):
        got(g_ref.at[m].at[:, :, c_peer], core_recv.at[m])

    def collect(m):
        for d in range(1, outer):
            rest(m, d)
        finish(m)

    def side(m, part):
        return g_ref[m, part].reshape(width, part_width)

    def complex_rows_here(lhs, m):
        n = lhs.shape[0] // 2
        pr = jnp.dot(lhs, side(m, 0), preferred_element_type=f32)
        pi = jnp.dot(lhs, side(m, 1), preferred_element_type=f32)
        return pr[:n] - pi[n:], pi[:n] + pr[n:]

    @pl.when(plane == last)
    def _():
        piece_wait(0, y)
        near(0, y, shifts=(-2, -1))
        ready_wait(1)
        near(0, y, shifts=(1,))
        ready_wait(2)
        near(0, y, shifts=(2,))
        piece_wait(0, y_peer)
        near(0, y_peer)
        share(0, 0)
        piece_wait(1, y)
        near(1, y, lambda s: ~relays_to(s))
        hop(0, y, 2)
        hop(0, y_peer, 2)
        for yy in order:
            for d in range(3, outer):
                hop(0, yy, d)
        near(1, y, relays_to)
        piece_wait(1, y_peer)
        near(1, y_peer)
        share(1, 0)
        got(left_ref.at[:, y], left_recv.at[0])

    for copy in args:
        copy.wait()
    eye = (lax.broadcasted_iota(jnp.int32, (sources, sources), 0)
           == lax.broadcasted_iota(jnp.int32, (sources, sources), 1))
    cell = jnp.sum(jnp.where(eye, cell_ref[...], 0), axis=1, keepdims=True)
    slab = jnp.sum(jnp.where(eye, slab_ref[...], 0), axis=1, keepdims=True)
    offset = lax.broadcasted_iota(jnp.int32, (sources, width), 1) - cell
    offset = jnp.where(offset < 0, offset + width, offset)
    inside = offset < width // 4
    for part in range(2):
        amp = amp_ref[:, part * width:(part + 1) * width].astype(f32)
        x_ref[part, y] = jnp.where(inside & (slab == 0), amp, 0.0).astype(bf16)
        base_ref[part, y] = jnp.where(inside & (slab == 1), amp, 0.0).astype(bf16)

    @pl.when(plane != last)
    def _():
        ready_wait(1)
        ready_wait(2)
        for part in range(2):
            got(slot(0, part), in_recv.at[y] if part == 0 else in_recv.at[2 * Y])
            near(0, y, part=part)
        piece_wait(0, y_peer)
        near(0, y_peer)
        share(0, 0)
        hops = [(y, 1), (y, 2), (y_peer, 1), (y_peer, 2)]
        for u, (part, h) in enumerate(left_units):
            got(left_rows(part, h, y), left_recv.at[u])
            left_relay(u, part, h).start()
            hop(0, *hops[u])
        for yy in order:
            for d in range(3, outer):
                hop(0, yy, d)
        for yy in order:
            piece_wait(1, yy)
            near(1, yy)
        share(1, 0)

    for d in range(1, outer):
        rest(0, d)
    got(left_ref.at[:, y_peer], left_recv.at[len(left_units)])
    finish(0)

    def x_swap(yy):
        ref = x_ref.at[:, yy]
        return remote(ref, ref, x_send.at[0], x_recv.at[0], dev(plane, z, y_peer, core))

    def base_swap(yy, quarter):
        ref = base_ref.at[:, yy, :, cols(quarter)]
        return remote(ref, ref, x_send.at[1], x_recv.at[1], dev(plane, z, y_peer, core))

    def coup_copy(yy, k, quarter):
        p, to_y = others[k]
        ref = coup_ref.at[yy].at[:, cols(quarter)]
        return remote(ref, ref, c_send.at[0], c_recv.at[yy], dev(p, z, to_y, core))

    for yy in range(Y):
        re, im = complex_rows_here(left_ref[:, yy].reshape(2 * depth, width), 0)
        for u in range(yy * per, (yy + 1) * per):
            here = slice(u % per * rows, (u % per + 1) * rows)
            coup_ref[u, 0:rows, cols(q)] = re[here].astype(bf16)
            coup_ref[u, rows:, cols(q)] = im[here].astype(bf16)
            for k in range(len(others)):
                coup_copy(u, k, q).start()


    for yy in order:
        for d in range(2, outer):
            hop(1, yy, d)
    collect(1)
    trio = len(others) * part_width
    for u in parts:
        got(coup_ref.at[u, :, 0:trio], c_recv.at[u])
        re, im = complex_rows_here(coup_ref[u], 1)
        here = slice(u % per * rows, (u % per + 1) * rows)
        for part, value in ((0, re), (1, im)):
            start = g_ref[1, part, z * Y + u // per, core, here]
            g_ref[2, part, z * Y + u // per, core, here] = (value + start.astype(f32)).astype(bf16)
        near(2, u, outward)
    x_swap(y).start()
    base_swap(y, plane * Y + y_peer).start()
    share(2, 0)
    for u in parts[:len(parts) // 2]:
        near(2, u, inner)
    for u in parts:
        for d in range(2, outer):
            hop(2, u, d)
        if u >= len(parts) // 2:
            near(2, u, inner)
    for d in range(1, outer):
        rest(2, d)
    x_swap(y_peer).wait_recv()
    base_swap(y_peer, q).wait_recv()
    finish(2)

    re, im = complex_rows_here(x_ref[...].reshape(2 * Y * sources, width), 2)
    for part, value in ((0, re), (1, im)):
        start = base_ref[part, :, :, cols(q)].astype(f32)
        f_ref[part] = (value.reshape(Y, sources, part_width) + start).astype(bf16)

    lhs = f_ref[...].reshape(2 * Y * sources, part_width)
    n = Y * sources
    tile = Y * CORE * depth

    def d_copy(k, yy, j):
        spots = slice(j * tile, (j + 1) * tile)
        return remote(d_ref.at[:, yy, :, spots], far_ref.at[k].at[:, :, spots],
                      d_send.at[0], d_recv.at[j], dev(0, z, yy, core))

    def f_copy(yy):
        return remote(f_ref.at[:, yy], whole_ref.at[:, :, cols(q)], f_send.at[0],
                      f_recv.at[0], dev(last, z, yy, core))

    handed, direct = range(outer // 2), range(outer // 2, outer)

    def hand_copy(j):
        spots = slice(j * tile, (j + 1) * tile)
        return remote(d_ref.at[:, y_peer, :, spots], hand_ref.at[:, :, spots], d_send.at[0], hand_recv.at[j],
                      dev(plane, z, y_peer, core))

    for j in (direct[0], *handed, *direct[1:]):
        spots = slice(j * tile, (j + 1) * tile)
        dims = (((1,), (1,)), ((), ()))
        right = [g_ref[2, part, j * Y:(j + 1) * Y].reshape(tile, part_width) for part in range(2)]
        pr = lax.dot_general(lhs, right[0], dims, preferred_element_type=f32)
        pi = lax.dot_general(lhs, right[1], dims, preferred_element_type=f32)
        d_ref[0, :, :, spots] = (pr[:n] - pi[n:]).astype(bf16).reshape(Y, sources, tile)
        d_ref[1, :, :, spots] = (pi[:n] + pr[n:]).astype(bf16).reshape(Y, sources, tile)

        @pl.when(plane == last)
        def _():
            if j in handed:
                hand_copy(j).start()
            else:
                d_copy(2, y_peer, j).start()
                d_copy(0, y, j).start()

        @pl.when(plane != last)
        def _():
            d_copy(1, y_peer, j).start()

    @pl.when(plane == last)
    def _():
        f_copy(y_peer).start()
        for j in handed:
            spots = slice(j * tile, (j + 1) * tile)
            got(hand_ref.at[:, :, spots], hand_recv.at[j])
            for part in range(2):
                d_ref[part, y, :, spots] = (d_ref[part, y, :, spots].astype(f32)
                                            + hand_ref[part, :, spots].astype(f32)).astype(bf16)
            d_copy(0, y, j).start()

    @pl.when(plane != last)
    def _():
        f_copy(y_peer).start()
        f_copy(y).start()

    @pl.when(plane == last)
    def _():
        sent(r_hbm.at[0, :, :, 0:6 * part_width], in_send.at[0])
        sent(left_ref, left_send.at[0])

    @pl.when(plane != last)
    def _():
        sent(left_ref.at[:, 0], left_send.at[0])

    x_swap(y).wait_send()
    base_swap(y, plane * Y + y_peer).wait_send()
    sent(coup_ref.at[:, :, 0:trio], c_send.at[0])
    sent(g_ref.at[:, :, :, 0], core_send.at[0])
    for zz in range(outer):
        count = sum(0 <= zz + s < outer for s in reach)
        hops = (max(zz - 1, 0) + max(outer - 2 - zz, 0)) * (0 < zz < outer - 1)

        @pl.when(z == zz)
        def _():
            sent(g_ref.at[:, :, 0:Y * count, 0], z_send.at[0])
            if hops:
                sent(g_ref.at[:, :, 0:Y * hops, 0], relay_send.at[0])

    @pl.when(plane == last)
    def _():
        whole_ref[:, :, cols(q)] = f_ref[:, y]
        got(whole_ref.at[:, :, 0:trio], f_recv.at[0])
        for part in range(2):
            out_ref[:, part * width:(part + 1) * width] = whole_ref[part].astype(f32)
        sent(d_ref, d_send.at[0])
        sent(f_ref.at[:, 0], f_send.at[0])

    @pl.when(plane != last)
    def _():
        for j in (*direct, *handed):
            spots = slice(j * tile, (j + 1) * tile)
            count = len(others) - (j in handed)
            got(far_ref.at[0:count, :, :, spots], d_recv.at[j])
            for part in range(2):
                total = d_ref.at[part][y, :, spots].astype(f32)
                for k in range(count):
                    total = total + far_ref[k, part, :, spots].astype(f32)
                out_ref[:, part * width + j * tile:part * width + (j + 1) * tile] = (
                    x_ref.at[part][y, :, spots].astype(f32) + total.astype(bf16).astype(f32))
        sent(d_ref.at[:, 0], d_send.at[0])
        sent(f_ref, f_send.at[0])


def pair_body(transmit, reflect, source_amp, source_cell, source_slab):
    outer = lax.axis_size("blk") // (Y * CORE)
    sources, double = source_amp.shape
    depth = transmit.shape[1]
    width = double // 2
    quarter = width // (PLANES * Y)
    bf16 = jnp.bfloat16
    hbm = pl.BlockSpec(memory_space=pltpu.HBM)
    sem = pltpu.SemaphoreType.DMA
    out = pl.pallas_call(
        functools.partial(pair_kernel, outer),
        out_shape=pltpu.VMEM((sources, double), jnp.float32),
        in_specs=[hbm] * 5,
        out_specs=pl.BlockSpec(memory_space=pltpu.VMEM),
        scratch_shapes=[
            pltpu.VMEM((sources, double), bf16),
            pltpu.VMEM((1, sources), jnp.int32),
            pltpu.VMEM((1, sources), jnp.int32),
            pltpu.VMEM((3, 2, outer * Y, CORE, depth, quarter), bf16),
            pltpu.VMEM((2, Y, depth, width), bf16),
            pltpu.VMEM((SPLIT, 2 * Y * depth // SPLIT, width), bf16),
            pltpu.VMEM((2, Y, sources, width), bf16),
            pltpu.VMEM((2, Y, sources, width), bf16),
            pltpu.VMEM((2, Y, sources, quarter), bf16),
            pltpu.VMEM((2, sources, width), bf16),
            pltpu.VMEM((2, Y, sources, width), bf16),
            pltpu.VMEM((PLANES * Y - 1, 2, sources, width), bf16),
            pltpu.VMEM((2, sources, width), bf16),
            pltpu.SemaphoreType.REGULAR((2,)),
            sem((3,)),
            sem((1,)),
            sem((2 * Y + 1,)),
            sem((1,)),
            sem((5,)),
            sem((1,)),
            sem(((outer - 1) * (2 * Y + SPLIT),)),
            sem((1,)),
            sem((1,)),
            sem((3,)),
            sem((1,)),
            sem((SPLIT,)),
            sem((2,)),
            sem((2,)),
            sem((1,)),
            sem((1,)),
            sem((1,)),
            sem((outer,)),
            sem((outer // 2,)),
        ],
        compiler_params=pltpu.CompilerParams(
            collective_id=0, has_side_effects=True, vmem_limit_bytes=32 << 20),
    )(*(pltpu.with_memory_space_constraint(a, pltpu.HBM) for a in (
        transmit, reflect, source_amp, source_cell[None], source_slab[None])))
    return out[None]


def solution(mesh):
    pair = mesh.shape["slab"] == PLANES and mesh.shape["blk"] % (Y * CORE) == 0 and mesh.shape["blk"] > 2 * Y * CORE
    return jax.shard_map(
        pair_body if pair else body,
        mesh=mesh,
        in_specs=(
            P("slab", "blk", None),
            P("slab", None, "blk", None),
            P("blk", None),
            P("blk"),
            P("blk"),
        ),
        out_specs=P("slab", "blk", None),
        check_vma=False,
    )
```

```python
import functools

import jax
import jax.numpy as jnp
from jax import lax
from jax.experimental import pallas as pl
from jax.experimental.pallas import tpu as pltpu
from jax.sharding import PartitionSpec as P


def shifted(block, axis, distance):
    devices = range(lax.axis_size(axis))
    route = [(i - distance, i) for i in devices if i - distance in devices]
    return lax.ppermute(block, axis, route)


def transposed(matrix):
    half_width = matrix.shape[0]
    return jnp.concatenate([matrix[:, :half_width].T, matrix[:, half_width:].T], 1)


def complex_rows(left_rows, right_matrix):
    inner_width = right_matrix.shape[0]
    outer_width = right_matrix.shape[1] // 2
    row_count = left_rows.shape[0]
    stacked = jnp.concatenate([left_rows[:, :inner_width], left_rows[:, inner_width:]], 0)
    product = jnp.dot(stacked, right_matrix, preferred_element_type=jnp.float32)
    real_out = product[:row_count, :outer_width] - product[row_count:, outer_width:]
    imag_out = product[:row_count, outer_width:] + product[row_count:, :outer_width]
    return jnp.concatenate([real_out, imag_out], 1)


def body(transmit, reflect, source_amp, source_cell, source_slab):
    trans_local = transmit[0]
    refl_local = reflect[0]
    half_width = source_amp.shape[1] // 2
    refl_second = lax.all_gather(refl_local[1], "blk", axis=0, tiled=True)
    coupling = complex_rows(refl_local[0], refl_second).astype(jnp.bfloat16)
    start_rows = trans_local.astype(jnp.float32)
    piece_rows = lax.all_gather(trans_local, "blk", axis=0, tiled=True)
    piece_count = piece_rows.shape[0]
    real_cols = lax.slice_in_dim(coupling, 0, piece_count, axis=1)
    imag_cols = lax.dynamic_slice_in_dim(coupling, half_width, piece_count, 1)
    left_rows = jnp.concatenate([real_cols, imag_cols], 1)
    joined = (start_rows + complex_rows(left_rows, piece_rows)).astype(jnp.bfloat16)
    slab_matrix = lax.all_gather(joined, "blk", axis=0, tiled=True)
    back_matrix = transposed(slab_matrix)
    cell_index = lax.iota(jnp.int32, half_width)
    offset = (cell_index[None, :] - source_cell[:, None]) % half_width
    inside = offset < half_width // 4
    here = source_slab == lax.axis_index("slab")
    keep = inside & here[:, None]
    keep = jnp.concatenate([keep, keep], 1)
    forcing = jnp.where(keep, source_amp, jnp.zeros_like(source_amp))
    chain_length = lax.axis_size("slab")
    carried = forcing
    for sweep_step in range(chain_length - 1):
        arrived = shifted(carried, "slab", 1)
        carried = (forcing.astype(jnp.float32) + complex_rows(arrived, slab_matrix)).astype(
            jnp.bfloat16
        )
    current = carried.astype(jnp.float32)
    for sweep_step in range(chain_length - 1):
        message = complex_rows(current.astype(jnp.bfloat16), back_matrix).astype(jnp.bfloat16)
        arrived = shifted(message, "slab", -1)
        current = carried.astype(jnp.float32) + arrived.astype(jnp.float32)
    return current[None]


MESH = pl.DeviceIdType.MESH
Y = 2
CORE = 2
PLANES = 2
SPLIT = 4


def pair_kernel(
    outer, t_hbm, r_hbm, amp_hbm, cell_hbm, slab_hbm, out_ref,
    amp_ref, cell_ref, slab_ref, g_ref, left_ref, coup_ref, x_ref, base_ref,
    f_ref, whole_ref, d_ref, far_ref, hand_ref,
    ready, arg_sem, in_send, in_recv, left_send, left_recv, z_send, z_recv, relay_send,
    core_send, core_recv, c_send, c_recv, x_send, x_recv, f_send, f_recv, d_send, d_recv, hand_recv,
):
    plane = lax.axis_index("slab")
    me = lax.axis_index("blk")
    z, y, core = me // (Y * CORE), (me // CORE) % Y, me % CORE
    last = PLANES - 1
    depth = t_hbm.shape[1]
    half = depth // 4
    width = t_hbm.shape[2] // 2
    part_width = width // (PLANES * Y)
    sources = amp_hbm.shape[0]
    y_peer, c_peer, x_peer = 1 - y, 1 - core, 1 - plane
    q = plane * Y + y
    f32, bf16 = jnp.float32, jnp.bfloat16
    others = ((x_peer, y), (plane, y_peer), (x_peer, y_peer))
    order = (y, y_peer)
    rows = coup_ref.shape[1] // 2
    per = depth // rows
    parts = range(Y * per)

    def dev(p, zz, yy, cc):
        return (p, (zz * Y + yy) * CORE + cc)

    def cols(quarter, base=0):
        return pl.ds(pl.multiple_of(base + quarter * part_width, part_width), part_width)

    def remote(s, d, ss, rs, to):
        return pltpu.make_async_remote_copy(
            src_ref=s, dst_ref=d, send_sem=ss, recv_sem=rs, device_id=to, device_id_type=MESH)

    def got(ref, sem):
        pltpu.make_async_copy(ref, ref, sem).wait()

    def sent(ref, sem):
        remote(ref, ref, sem, sem, dev(plane, z, y, c_peer)).wait_send()

    def valid(zz):
        return (zz >= 0) & (zz < outer)

    def unit(m, zz, u):
        if m < 2:
            return g_ref.at[m].at[:, zz * Y + u, core]
        return g_ref.at[m].at[:, zz * Y + u // per, core, u % per * rows:(u % per + 1) * rows]

    def piece(m, part, p, yy):
        s = r_hbm.at[0, 1] if m == 0 else t_hbm.at[0]
        return s.at[:, cols(p * Y + yy, part * width)]

    def slot(m, part):
        return g_ref.at[m, part].at[z * Y + y, core]

    def piece_local(m, part):
        return pltpu.make_async_copy(piece(m, part, last, y), slot(m, part), in_recv.at[m * Y + y])

    def piece_send(m, part, p, yy):
        split = m == 0 and part == 1 and p != last and yy is y
        return remote(piece(m, part, p, yy), slot(m, part), in_send.at[0],
                      in_recv.at[2 * Y] if split else in_recv.at[m * Y + y], dev(p, z, yy, core))

    def piece_wait(m, yy):
        got(unit(m, z, yy), in_recv.at[m * Y + yy])

    left_units = [(part, h) for part in range(2) for h in range(4)]

    def left_rows(part, h, yy):
        return left_ref.at[part].at[yy, h * half:(h + 1) * half]

    def left_src(part, h):
        return r_hbm.at[0, 0, h * half:(h + 1) * half, part * width:(part + 1) * width]

    def left_local(part):
        return pltpu.make_async_copy(
            r_hbm.at[0, 0, :, part * width:(part + 1) * width], left_ref.at[part].at[y], left_recv.at[0])

    def left_push(u, part, h, k):
        to = dev(0, z, y, core) if k == 0 else dev(last, z, y_peer, core)
        return remote(left_src(part, h), left_rows(part, h, y), left_send.at[0],
                      left_recv.at[u if k == 0 else len(left_units)], to)

    def left_relay(u, part, h):
        ref = left_rows(part, h, y)
        return remote(ref, ref, left_send.at[0], left_recv.at[len(left_units)], dev(plane, z, y_peer, core))

    args = [pltpu.make_async_copy(a, b, arg_sem.at[i]) for i, (a, b) in enumerate(
        ((amp_hbm, amp_ref), (cell_hbm, cell_ref), (slab_hbm, slab_ref)))]

    barrier = pltpu.get_barrier_semaphore()

    def tell(sem, to, when=None):
        def send():
            pl.semaphore_signal(sem, inc=1, device_id=to, device_id_type=MESH)
        send() if when is None else pl.when(when)(send)

    for p, yy, cc in ((plane, y, c_peer), (plane, y_peer, core), (x_peer, y, core), (x_peer, y_peer, core)):
        tell(barrier, dev(p, z, yy, cc))
    for s in (1, 2):
        tell(barrier, dev(plane, z + s, y, core), valid(z + s))

    @pl.when(plane == last)
    def _():
        for m in range(2):
            for part in range(2):
                piece_local(m, part).start()
        for part in range(2):
            left_local(part).start()

    for copy in args:
        copy.start()
    pl.semaphore_wait(barrier, 4 + jnp.minimum(z, 2))
    for s in (1, 2):
        tell(ready.at[s - 1], dev(plane, z - s, y, core), valid(z - s))

    @pl.when(plane == last)
    def _():
        for p, yy in ((0, y), (last, y_peer), (0, y_peer)):
            for part in range(2):
                piece_send(0, part, p, yy).start()
        for u, (part, h) in enumerate(left_units):
            for k in range(2):
                left_push(u, part, h, k).start()
        for p, yy in ((0, y), (last, y_peer), (0, y_peer)):
            for part in range(2):
                piece_send(1, part, p, yy).start()

    def z_sem(m, shift, yy):
        k = shift % outer - 1
        return z_recv.at[(m * (outer - 1) + k) * Y + yy if m < 2 else (2 * (outer - 1) + k * per) * Y + yy]

    reach = (-2, 2, -1, 1)

    def near(m, yy, when=lambda s: True, part=None, shifts=reach):
        for s in shifts:
            @pl.when(valid(z + s) & when(s))
            def _():
                ref = unit(m, z, yy) if part is None else slot(m, part)
                remote(ref, ref, z_send.at[0], z_sem(m, -s, yy), dev(plane, z + s, y, core)).start()

    def inner(s):
        return (z + s > 0) & (z + s < outer - 1) if abs(s) == 1 else z < 0

    def outward(s):
        return ~inner(s)

    def ready_wait(s):
        @pl.when(valid(z + s))
        def _():
            pl.semaphore_wait(ready.at[s - 1], 1)

    def relays_to(s):
        return {1: (z >= 2) & valid(z + 1), -1: (z <= outer - 3) & valid(z - 1)}.get(s, z < 0)

    def onward_ok(s):
        return valid(z + s) & valid(z + (-1 if s > 0 else 1)) & (abs(s) > 1)

    def hop(m, yy, d):
        for s in (d, -d) if d > 1 else ():
            @pl.when(onward_ok(s))
            def _():
                onward = -1 if s > 0 else 1
                ref = unit(m, z + s, yy)
                got(ref, z_sem(m, s, yy))
                remote(ref, ref, relay_send.at[0], z_sem(m, s - onward, yy),
                       dev(plane, z + onward, y, core)).start()

    def units(m):
        return order if m < 2 else parts

    def share(m, d, only=None):
        for s in ((d, -d) if d else (0,)):
            @pl.when(valid(z + s))
            def _():
                for u in units(m) if only is None else (only,):
                    ref = unit(m, z + s, u)
                    remote(ref, ref, core_send.at[0], core_recv.at[m], dev(plane, z, y, c_peer)).start()

    def rest(m, d):
        for u in units(m):
            for s in (d, -d):
                @pl.when(valid(z + s) & ~onward_ok(s))
                def _():
                    got(unit(m, z + s, u), z_sem(m, s, u))
            share(m, d, u)

    def finish(m):
        got(g_ref.at[m].at[:, :, c_peer], core_recv.at[m])

    def collect(m):
        for d in range(1, outer):
            rest(m, d)
        finish(m)

    def side(m, part):
        return g_ref[m, part].reshape(width, part_width)

    def complex_rows_here(lhs, m):
        n = lhs.shape[0] // 2
        pr = jnp.dot(lhs, side(m, 0), preferred_element_type=f32)
        pi = jnp.dot(lhs, side(m, 1), preferred_element_type=f32)
        return pr[:n] - pi[n:], pi[:n] + pr[n:]

    @pl.when(plane == last)
    def _():
        piece_wait(0, y)
        near(0, y, shifts=(-2, -1))
        ready_wait(1)
        near(0, y, shifts=(1,))
        ready_wait(2)
        near(0, y, shifts=(2,))
        piece_wait(0, y_peer)
        near(0, y_peer)
        share(0, 0)
        hop(0, y, 2)
        hop(0, y_peer, 2)
        for yy in order:
            for d in range(3, outer):
                hop(0, yy, d)
        piece_wait(1, y)
        near(1, y)
        piece_wait(1, y_peer)
        near(1, y_peer)
        share(1, 0)
        got(left_ref.at[:, y], left_recv.at[0])

    for copy in args:
        copy.wait()
    eye = (lax.broadcasted_iota(jnp.int32, (sources, sources), 0)
           == lax.broadcasted_iota(jnp.int32, (sources, sources), 1))
    cell = jnp.sum(jnp.where(eye, cell_ref[...], 0), axis=1, keepdims=True)
    slab = jnp.sum(jnp.where(eye, slab_ref[...], 0), axis=1, keepdims=True)
    offset = lax.broadcasted_iota(jnp.int32, (sources, width), 1) - cell
    offset = jnp.where(offset < 0, offset + width, offset)
    inside = offset < width // 4
    for part in range(2):
        amp = amp_ref[:, part * width:(part + 1) * width].astype(f32)
        x_ref[part, y] = jnp.where(inside & (slab == 0), amp, 0.0).astype(bf16)
        base_ref[part, y] = jnp.where(inside & (slab == 1), amp, 0.0).astype(bf16)

    @pl.when(plane != last)
    def _():
        ready_wait(1)
        ready_wait(2)
        for part in range(2):
            got(slot(0, part), in_recv.at[y] if part == 0 else in_recv.at[2 * Y])
            near(0, y, part=part)
        piece_wait(0, y_peer)
        near(0, y_peer)
        share(0, 0)
        hops = [(y, 1), (y, 2), (y_peer, 1), (y_peer, 2)]
        for u, (part, h) in enumerate(left_units):
            got(left_rows(part, h, y), left_recv.at[u])
            left_relay(u, part, h).start()
            if u % 2:
                hop(0, *hops[u // 2])
        for yy in order:
            for d in range(3, outer):
                hop(0, yy, d)
        for yy in order:
            piece_wait(1, yy)
            near(1, yy)
        share(1, 0)

    for d in range(1, outer):
        rest(0, d)
    got(left_ref.at[:, y_peer], left_recv.at[len(left_units)])
    finish(0)

    def x_swap(yy):
        ref = x_ref.at[:, yy]
        return remote(ref, ref, x_send.at[0], x_recv.at[0], dev(plane, z, y_peer, core))

    def base_swap(yy, quarter):
        ref = base_ref.at[:, yy, :, cols(quarter)]
        return remote(ref, ref, x_send.at[1], x_recv.at[1], dev(plane, z, y_peer, core))

    def coup_copy(yy, k, quarter):
        p, to_y = others[k]
        ref = coup_ref.at[yy].at[:, cols(quarter)]
        return remote(ref, ref, c_send.at[0], c_recv.at[yy], dev(p, z, to_y, core))

    for yy in range(Y):
        re, im = complex_rows_here(left_ref[:, yy].reshape(2 * depth, width), 0)
        for u in range(yy * per, (yy + 1) * per):
            here = slice(u % per * rows, (u % per + 1) * rows)
            coup_ref[u, 0:rows, cols(q)] = re[here].astype(bf16)
            coup_ref[u, rows:, cols(q)] = im[here].astype(bf16)
            for k in range(len(others)):
                coup_copy(u, k, q).start()


    for yy in order:
        for d in range(2, outer):
            hop(1, yy, d)
    collect(1)
    trio = len(others) * part_width
    for u in parts:
        got(coup_ref.at[u, :, 0:trio], c_recv.at[u])
        re, im = complex_rows_here(coup_ref[u], 1)
        here = slice(u % per * rows, (u % per + 1) * rows)
        for part, value in ((0, re), (1, im)):
            start = g_ref[1, part, z * Y + u // per, core, here]
            g_ref[2, part, z * Y + u // per, core, here] = (value + start.astype(f32)).astype(bf16)
        near(2, u, outward)
    x_swap(y).start()
    base_swap(y, plane * Y + y_peer).start()
    share(2, 0)
    for u in parts[:len(parts) // 2]:
        near(2, u, inner)
    for u in parts:
        for d in range(2, outer):
            hop(2, u, d)
        if u >= len(parts) // 2:
            near(2, u, inner)
    for d in range(1, outer):
        rest(2, d)
    x_swap(y_peer).wait_recv()
    base_swap(y_peer, q).wait_recv()
    finish(2)

    re, im = complex_rows_here(x_ref[...].reshape(2 * Y * sources, width), 2)
    for part, value in ((0, re), (1, im)):
        start = base_ref[part, :, :, cols(q)].astype(f32)
        f_ref[part] = (value.reshape(Y, sources, part_width) + start).astype(bf16)

    lhs = f_ref[...].reshape(2 * Y * sources, part_width)
    n = Y * sources
    tile = Y * CORE * depth

    def d_copy(k, yy, j):
        spots = slice(j * tile, (j + 1) * tile)
        return remote(d_ref.at[:, yy, :, spots], far_ref.at[k].at[:, :, spots],
                      d_send.at[0], d_recv.at[j], dev(0, z, yy, core))

    def f_copy(yy):
        return remote(f_ref.at[:, yy], whole_ref.at[:, :, cols(q)], f_send.at[0],
                      f_recv.at[0], dev(last, z, yy, core))

    handed, direct = range(outer // 2), range(outer // 2, outer)

    def hand_copy(j):
        spots = slice(j * tile, (j + 1) * tile)
        return remote(d_ref.at[:, y_peer, :, spots], hand_ref.at[:, :, spots], d_send.at[0], hand_recv.at[j],
                      dev(plane, z, y_peer, core))

    for j in (direct[0], *handed, *direct[1:]):
        spots = slice(j * tile, (j + 1) * tile)
        dims = (((1,), (1,)), ((), ()))
        right = [g_ref[2, part, j * Y:(j + 1) * Y].reshape(tile, part_width) for part in range(2)]
        pr = lax.dot_general(lhs, right[0], dims, preferred_element_type=f32)
        pi = lax.dot_general(lhs, right[1], dims, preferred_element_type=f32)
        d_ref[0, :, :, spots] = (pr[:n] - pi[n:]).astype(bf16).reshape(Y, sources, tile)
        d_ref[1, :, :, spots] = (pi[:n] + pr[n:]).astype(bf16).reshape(Y, sources, tile)

        @pl.when(plane == last)
        def _():
            if j in handed:
                hand_copy(j).start()
            else:
                d_copy(2, y_peer, j).start()
                d_copy(0, y, j).start()

        @pl.when(plane != last)
        def _():
            d_copy(1, y_peer, j).start()

    @pl.when(plane == last)
    def _():
        f_copy(y_peer).start()
        for j in handed:
            spots = slice(j * tile, (j + 1) * tile)
            got(hand_ref.at[:, :, spots], hand_recv.at[j])
            for part in range(2):
                d_ref[part, y, :, spots] = (d_ref[part, y, :, spots].astype(f32)
                                            + hand_ref[part, :, spots].astype(f32)).astype(bf16)
            d_copy(0, y, j).start()

    @pl.when(plane != last)
    def _():
        f_copy(y_peer).start()
        f_copy(y).start()

    @pl.when(plane == last)
    def _():
        sent(r_hbm.at[0, :, :, 0:6 * part_width], in_send.at[0])
        sent(left_ref, left_send.at[0])

    @pl.when(plane != last)
    def _():
        sent(left_ref.at[:, 0], left_send.at[0])

    x_swap(y).wait_send()
    base_swap(y, plane * Y + y_peer).wait_send()
    sent(coup_ref.at[:, :, 0:trio], c_send.at[0])
    sent(g_ref.at[:, :, :, 0], core_send.at[0])
    for zz in range(outer):
        count = sum(0 <= zz + s < outer for s in reach)
        hops = (max(zz - 1, 0) + max(outer - 2 - zz, 0)) * (0 < zz < outer - 1)

        @pl.when(z == zz)
        def _():
            sent(g_ref.at[:, :, 0:Y * count, 0], z_send.at[0])
            if hops:
                sent(g_ref.at[:, :, 0:Y * hops, 0], relay_send.at[0])

    @pl.when(plane == last)
    def _():
        whole_ref[:, :, cols(q)] = f_ref[:, y]
        got(whole_ref.at[:, :, 0:trio], f_recv.at[0])
        for part in range(2):
            out_ref[:, part * width:(part + 1) * width] = whole_ref[part].astype(f32)
        sent(d_ref, d_send.at[0])
        sent(f_ref.at[:, 0], f_send.at[0])

    @pl.when(plane != last)
    def _():
        for j in (*direct, *handed):
            spots = slice(j * tile, (j + 1) * tile)
            count = len(others) - (j in handed)
            got(far_ref.at[0:count, :, :, spots], d_recv.at[j])
            for part in range(2):
                total = d_ref.at[part][y, :, spots].astype(f32)
                for k in range(count):
                    total = total + far_ref[k, part, :, spots].astype(f32)
                out_ref[:, part * width + j * tile:part * width + (j + 1) * tile] = (
                    x_ref.at[part][y, :, spots].astype(f32) + total.astype(bf16).astype(f32))
        sent(d_ref.at[:, 0], d_send.at[0])
        sent(f_ref, f_send.at[0])


def pair_body(transmit, reflect, source_amp, source_cell, source_slab):
    outer = lax.axis_size("blk") // (Y * CORE)
    sources, double = source_amp.shape
    depth = transmit.shape[1]
    width = double // 2
    quarter = width // (PLANES * Y)
    bf16 = jnp.bfloat16
    hbm = pl.BlockSpec(memory_space=pltpu.HBM)
    sem = pltpu.SemaphoreType.DMA
    out = pl.pallas_call(
        functools.partial(pair_kernel, outer),
        out_shape=pltpu.VMEM((sources, double), jnp.float32),
        in_specs=[hbm] * 5,
        out_specs=pl.BlockSpec(memory_space=pltpu.VMEM),
        scratch_shapes=[
            pltpu.VMEM((sources, double), bf16),
            pltpu.VMEM((1, sources), jnp.int32),
            pltpu.VMEM((1, sources), jnp.int32),
            pltpu.VMEM((3, 2, outer * Y, CORE, depth, quarter), bf16),
            pltpu.VMEM((2, Y, depth, width), bf16),
            pltpu.VMEM((SPLIT, 2 * Y * depth // SPLIT, width), bf16),
            pltpu.VMEM((2, Y, sources, width), bf16),
            pltpu.VMEM((2, Y, sources, width), bf16),
            pltpu.VMEM((2, Y, sources, quarter), bf16),
            pltpu.VMEM((2, sources, width), bf16),
            pltpu.VMEM((2, Y, sources, width), bf16),
            pltpu.VMEM((PLANES * Y - 1, 2, sources, width), bf16),
            pltpu.VMEM((2, sources, width), bf16),
            pltpu.SemaphoreType.REGULAR((2,)),
            sem((3,)),
            sem((1,)),
            sem((2 * Y + 1,)),
            sem((1,)),
            sem((9,)),
            sem((1,)),
            sem(((outer - 1) * (2 * Y + SPLIT),)),
            sem((1,)),
            sem((1,)),
            sem((3,)),
            sem((1,)),
            sem((SPLIT,)),
            sem((2,)),
            sem((2,)),
            sem((1,)),
            sem((1,)),
            sem((1,)),
            sem((outer,)),
            sem((outer // 2,)),
        ],
        compiler_params=pltpu.CompilerParams(
            collective_id=0, has_side_effects=True, vmem_limit_bytes=32 << 20),
    )(*(pltpu.with_memory_space_constraint(a, pltpu.HBM) for a in (
        transmit, reflect, source_amp, source_cell[None], source_slab[None])))
    return out[None]


def solution(mesh):
    pair = mesh.shape["slab"] == PLANES and mesh.shape["blk"] % (Y * CORE) == 0 and mesh.shape["blk"] > 2 * Y * CORE
    return jax.shard_map(
        pair_body if pair else body,
        mesh=mesh,
        in_specs=(
            P("slab", "blk", None),
            P("slab", None, "blk", None),
            P("blk", None),
            P("blk"),
            P("blk"),
        ),
        out_specs=P("slab", "blk", None),
        check_vma=False,
    )
```

```python
import functools

import jax
import jax.numpy as jnp
from jax import lax
from jax.experimental import pallas as pl
from jax.experimental.pallas import tpu as pltpu
from jax.sharding import PartitionSpec as P


def shifted(block, axis, distance):
    devices = range(lax.axis_size(axis))
    route = [(i - distance, i) for i in devices if i - distance in devices]
    return lax.ppermute(block, axis, route)


def transposed(matrix):
    half_width = matrix.shape[0]
    return jnp.concatenate([matrix[:, :half_width].T, matrix[:, half_width:].T], 1)


def complex_rows(left_rows, right_matrix):
    inner_width = right_matrix.shape[0]
    outer_width = right_matrix.shape[1] // 2
    row_count = left_rows.shape[0]
    stacked = jnp.concatenate([left_rows[:, :inner_width], left_rows[:, inner_width:]], 0)
    product = jnp.dot(stacked, right_matrix, preferred_element_type=jnp.float32)
    real_out = product[:row_count, :outer_width] - product[row_count:, outer_width:]
    imag_out = product[:row_count, outer_width:] + product[row_count:, :outer_width]
    return jnp.concatenate([real_out, imag_out], 1)


def body(transmit, reflect, source_amp, source_cell, source_slab):
    trans_local = transmit[0]
    refl_local = reflect[0]
    half_width = source_amp.shape[1] // 2
    refl_second = lax.all_gather(refl_local[1], "blk", axis=0, tiled=True)
    coupling = complex_rows(refl_local[0], refl_second).astype(jnp.bfloat16)
    start_rows = trans_local.astype(jnp.float32)
    piece_rows = lax.all_gather(trans_local, "blk", axis=0, tiled=True)
    piece_count = piece_rows.shape[0]
    real_cols = lax.slice_in_dim(coupling, 0, piece_count, axis=1)
    imag_cols = lax.dynamic_slice_in_dim(coupling, half_width, piece_count, 1)
    left_rows = jnp.concatenate([real_cols, imag_cols], 1)
    joined = (start_rows + complex_rows(left_rows, piece_rows)).astype(jnp.bfloat16)
    slab_matrix = lax.all_gather(joined, "blk", axis=0, tiled=True)
    back_matrix = transposed(slab_matrix)
    cell_index = lax.iota(jnp.int32, half_width)
    offset = (cell_index[None, :] - source_cell[:, None]) % half_width
    inside = offset < half_width // 4
    here = source_slab == lax.axis_index("slab")
    keep = inside & here[:, None]
    keep = jnp.concatenate([keep, keep], 1)
    forcing = jnp.where(keep, source_amp, jnp.zeros_like(source_amp))
    chain_length = lax.axis_size("slab")
    carried = forcing
    for sweep_step in range(chain_length - 1):
        arrived = shifted(carried, "slab", 1)
        carried = (forcing.astype(jnp.float32) + complex_rows(arrived, slab_matrix)).astype(
            jnp.bfloat16
        )
    current = carried.astype(jnp.float32)
    for sweep_step in range(chain_length - 1):
        message = complex_rows(current.astype(jnp.bfloat16), back_matrix).astype(jnp.bfloat16)
        arrived = shifted(message, "slab", -1)
        current = carried.astype(jnp.float32) + arrived.astype(jnp.float32)
    return current[None]


MESH = pl.DeviceIdType.MESH
Y = 2
CORE = 2
PLANES = 2
SPLIT = 4


def pair_kernel(
    outer, t_hbm, r_hbm, amp_hbm, cell_hbm, slab_hbm, out_ref,
    amp_ref, cell_ref, slab_ref, g_ref, left_ref, coup_ref, x_ref, base_ref,
    f_ref, whole_ref, d_ref, far_ref, hand_ref,
    ready, arg_sem, in_send, in_recv, left_send, left_recv, z_send, z_recv, relay_send,
    core_send, core_recv, c_send, c_recv, x_send, x_recv, f_send, f_recv, d_send, d_recv, hand_recv,
):
    plane = lax.axis_index("slab")
    me = lax.axis_index("blk")
    z, y, core = me // (Y * CORE), (me // CORE) % Y, me % CORE
    last = PLANES - 1
    depth = t_hbm.shape[1]
    half = depth // 2
    width = t_hbm.shape[2] // 2
    part_width = width // (PLANES * Y)
    sources = amp_hbm.shape[0]
    y_peer, c_peer, x_peer = 1 - y, 1 - core, 1 - plane
    q = plane * Y + y
    f32, bf16 = jnp.float32, jnp.bfloat16
    others = ((x_peer, y), (plane, y_peer), (x_peer, y_peer))
    order = (y, y_peer)
    rows = coup_ref.shape[1] // 2
    per = depth // rows
    parts = range(Y * per)

    def dev(p, zz, yy, cc):
        return (p, (zz * Y + yy) * CORE + cc)

    def cols(quarter, base=0):
        return pl.ds(pl.multiple_of(base + quarter * part_width, part_width), part_width)

    def remote(s, d, ss, rs, to):
        return pltpu.make_async_remote_copy(
            src_ref=s, dst_ref=d, send_sem=ss, recv_sem=rs, device_id=to, device_id_type=MESH)

    def got(ref, sem):
        pltpu.make_async_copy(ref, ref, sem).wait()

    def sent(ref, sem):
        remote(ref, ref, sem, sem, dev(plane, z, y, c_peer)).wait_send()

    def valid(zz):
        return (zz >= 0) & (zz < outer)

    def unit(m, zz, u):
        if m < 2:
            return g_ref.at[m].at[:, zz * Y + u, core]
        return g_ref.at[m].at[:, zz * Y + u // per, core, u % per * rows:(u % per + 1) * rows]

    def piece(m, part, p, yy):
        s = r_hbm.at[0, 1] if m == 0 else t_hbm.at[0]
        return s.at[:, cols(p * Y + yy, part * width)]

    def slot(m, part):
        return g_ref.at[m, part].at[z * Y + y, core]

    def piece_local(m, part):
        return pltpu.make_async_copy(piece(m, part, last, y), slot(m, part), in_recv.at[m * Y + y])

    def piece_send(m, part, p, yy):
        split = m == 0 and part == 1 and p != last and yy is y
        return remote(piece(m, part, p, yy), slot(m, part), in_send.at[0],
                      in_recv.at[2 * Y] if split else in_recv.at[m * Y + y], dev(p, z, yy, core))

    def piece_wait(m, yy):
        got(unit(m, z, yy), in_recv.at[m * Y + yy])

    left_units = [(part, h) for part in range(2) for h in range(2)]

    def left_rows(part, h, yy):
        return left_ref.at[part].at[yy, h * half:(h + 1) * half]

    def left_src(part, h):
        return r_hbm.at[0, 0, h * half:(h + 1) * half, part * width:(part + 1) * width]

    def left_local(part):
        return pltpu.make_async_copy(
            r_hbm.at[0, 0, :, part * width:(part + 1) * width], left_ref.at[part].at[y], left_recv.at[0])

    def left_push(u, part, h, k):
        to = dev(0, z, y, core) if k == 0 else dev(last, z, y_peer, core)
        return remote(left_src(part, h), left_rows(part, h, y), left_send.at[0],
                      left_recv.at[u if k == 0 else len(left_units)], to)

    def left_relay(u, part, h):
        ref = left_rows(part, h, y)
        return remote(ref, ref, left_send.at[0], left_recv.at[len(left_units)], dev(plane, z, y_peer, core))

    args = [pltpu.make_async_copy(a, b, arg_sem.at[i]) for i, (a, b) in enumerate(
        ((amp_hbm, amp_ref), (cell_hbm, cell_ref), (slab_hbm, slab_ref)))]

    barrier = pltpu.get_barrier_semaphore()

    def tell(sem, to, when=None):
        def send():
            pl.semaphore_signal(sem, inc=1, device_id=to, device_id_type=MESH)
        send() if when is None else pl.when(when)(send)

    for p, yy, cc in ((plane, y, c_peer), (plane, y_peer, core), (x_peer, y, core), (x_peer, y_peer, core)):
        tell(barrier, dev(p, z, yy, cc))
    for s in (1, 2):
        tell(barrier, dev(plane, z + s, y, core), valid(z + s))

    @pl.when(plane == last)
    def _():
        for m in range(2):
            for part in range(2):
                piece_local(m, part).start()
        for part in range(2):
            left_local(part).start()

    for copy in args:
        copy.start()
    pl.semaphore_wait(barrier, 4 + jnp.minimum(z, 2))
    for s in (1, 2):
        tell(ready.at[s - 1], dev(plane, z - s, y, core), valid(z - s))

    @pl.when(plane == last)
    def _():
        for p, yy in ((0, y), (last, y_peer), (0, y_peer)):
            for part in range(2):
                piece_send(0, part, p, yy).start()
        for u, (part, h) in enumerate(left_units):
            for k in range(2):
                left_push(u, part, h, k).start()
        for p, yy in ((0, y), (last, y_peer), (0, y_peer)):
            for part in range(2):
                piece_send(1, part, p, yy).start()

    def z_sem(m, shift, yy):
        k = shift % outer - 1
        return z_recv.at[(m * (outer - 1) + k) * Y + yy if m < 2 else (2 * (outer - 1) + k * per) * Y + yy]

    reach = (-2, 2, -1, 1)

    def near(m, yy, when=lambda s: True, part=None, shifts=reach):
        for s in shifts:
            @pl.when(valid(z + s) & when(s))
            def _():
                ref = unit(m, z, yy) if part is None else slot(m, part)
                remote(ref, ref, z_send.at[0], z_sem(m, -s, yy), dev(plane, z + s, y, core)).start()

    def inner(s):
        return (z + s > 0) & (z + s < outer - 1) if abs(s) == 1 else z < 0

    def outward(s):
        return ~inner(s)

    def ready_wait(s):
        @pl.when(valid(z + s))
        def _():
            pl.semaphore_wait(ready.at[s - 1], 1)

    def relays_to(s):
        return {1: (z >= 2) & valid(z + 1), -1: (z <= outer - 3) & valid(z - 1)}.get(s, z < 0)

    def onward_ok(s):
        return valid(z + s) & valid(z + (-1 if s > 0 else 1)) & (abs(s) > 1)

    def hop(m, yy, d):
        for s in (d, -d) if d > 1 else ():
            @pl.when(onward_ok(s))
            def _():
                onward = -1 if s > 0 else 1
                ref = unit(m, z + s, yy)
                got(ref, z_sem(m, s, yy))
                remote(ref, ref, relay_send.at[0], z_sem(m, s - onward, yy),
                       dev(plane, z + onward, y, core)).start()

    def units(m):
        return order if m < 2 else parts

    def share(m, d, only=None):
        for s in ((d, -d) if d else (0,)):
            @pl.when(valid(z + s))
            def _():
                for u in units(m) if only is None else (only,):
                    ref = unit(m, z + s, u)
                    remote(ref, ref, core_send.at[0], core_recv.at[m], dev(plane, z, y, c_peer)).start()

    def rest(m, d):
        for u in units(m):
            for s in (d, -d):
                @pl.when(valid(z + s) & ~onward_ok(s))
                def _():
                    got(unit(m, z + s, u), z_sem(m, s, u))
            share(m, d, u)

    def finish(m):
        got(g_ref.at[m].at[:, :, c_peer], core_recv.at[m])

    def collect(m):
        for d in range(1, outer):
            rest(m, d)
        finish(m)

    def side(m, part):
        return g_ref[m, part].reshape(width, part_width)

    def complex_rows_here(lhs, m):
        n = lhs.shape[0] // 2
        pr = jnp.dot(lhs, side(m, 0), preferred_element_type=f32)
        pi = jnp.dot(lhs, side(m, 1), preferred_element_type=f32)
        return pr[:n] - pi[n:], pi[:n] + pr[n:]

    @pl.when(plane == last)
    def _():
        piece_wait(0, y)
        near(0, y, shifts=(-2, -1))
        ready_wait(1)
        near(0, y, shifts=(1,))
        ready_wait(2)
        near(0, y, shifts=(2,))
        piece_wait(0, y_peer)
        near(0, y_peer)
        share(0, 0)
        hop(0, y, 2)
        hop(0, y_peer, 2)
        for yy in order:
            for d in range(3, outer):
                hop(0, yy, d)
        piece_wait(1, y)
        near(1, y)
        piece_wait(1, y_peer)
        near(1, y_peer)
        share(1, 0)
        got(left_ref.at[:, y], left_recv.at[0])

    for copy in args:
        copy.wait()
    eye = (lax.broadcasted_iota(jnp.int32, (sources, sources), 0)
           == lax.broadcasted_iota(jnp.int32, (sources, sources), 1))
    cell = jnp.sum(jnp.where(eye, cell_ref[...], 0), axis=1, keepdims=True)
    slab = jnp.sum(jnp.where(eye, slab_ref[...], 0), axis=1, keepdims=True)
    offset = lax.broadcasted_iota(jnp.int32, (sources, width), 1) - cell
    offset = jnp.where(offset < 0, offset + width, offset)
    inside = offset < width // 4
    for part in range(2):
        amp = amp_ref[:, part * width:(part + 1) * width].astype(f32)
        x_ref[part, y] = jnp.where(inside & (slab == 0), amp, 0.0).astype(bf16)
        base_ref[part, y] = jnp.where(inside & (slab == 1), amp, 0.0).astype(bf16)

    @pl.when(plane != last)
    def _():
        ready_wait(1)
        ready_wait(2)
        for part in range(2):
            got(slot(0, part), in_recv.at[y] if part == 0 else in_recv.at[2 * Y])
            near(0, y, part=part)
        piece_wait(0, y_peer)
        near(0, y_peer)
        share(0, 0)
        hops = [(y, 1), (y, 2), (y_peer, 1), (y_peer, 2)]
        for u, (part, h) in enumerate(left_units):
            got(left_rows(part, h, y), left_recv.at[u])
            left_relay(u, part, h).start()
            hop(0, *hops[u])
        for yy in order:
            for d in range(3, outer):
                hop(0, yy, d)
        for yy in order:
            piece_wait(1, yy)
            near(1, yy)
        share(1, 0)

    for d in range(1, outer):
        rest(0, d)
    got(left_ref.at[:, y_peer], left_recv.at[len(left_units)])
    finish(0)

    def x_swap(yy):
        ref = x_ref.at[:, yy]
        return remote(ref, ref, x_send.at[0], x_recv.at[0], dev(plane, z, y_peer, core))

    def base_swap(yy, quarter):
        ref = base_ref.at[:, yy, :, cols(quarter)]
        return remote(ref, ref, x_send.at[1], x_recv.at[1], dev(plane, z, y_peer, core))

    def coup_copy(yy, k, quarter):
        p, to_y = others[k]
        ref = coup_ref.at[yy].at[:, cols(quarter)]
        return remote(ref, ref, c_send.at[0], c_recv.at[yy], dev(p, z, to_y, core))

    for yy in range(Y):
        re, im = complex_rows_here(left_ref[:, yy].reshape(2 * depth, width), 0)
        for u in range(yy * per, (yy + 1) * per):
            here = slice(u % per * rows, (u % per + 1) * rows)
            coup_ref[u, 0:rows, cols(q)] = re[here].astype(bf16)
            coup_ref[u, rows:, cols(q)] = im[here].astype(bf16)
            for k in range(len(others)):
                coup_copy(u, k, q).start()


    for yy in order:
        for d in range(2, outer):
            hop(1, yy, d)
    collect(1)
    trio = len(others) * part_width
    for u in parts:
        got(coup_ref.at[u, :, 0:trio], c_recv.at[u])
        re, im = complex_rows_here(coup_ref[u], 1)
        here = slice(u % per * rows, (u % per + 1) * rows)
        for part, value in ((0, re), (1, im)):
            start = g_ref[1, part, z * Y + u // per, core, here]
            g_ref[2, part, z * Y + u // per, core, here] = (value + start.astype(f32)).astype(bf16)
        near(2, u, outward)
    x_swap(y).start()
    base_swap(y, plane * Y + y_peer).start()
    share(2, 0)
    for u in parts[:len(parts) // 2]:
        near(2, u, inner)
    for u in parts:
        for d in range(2, outer):
            hop(2, u, d)
        if u >= len(parts) // 2:
            near(2, u, inner)
    for d in range(1, outer):
        rest(2, d)
    x_swap(y_peer).wait_recv()
    base_swap(y_peer, q).wait_recv()
    finish(2)

    re, im = complex_rows_here(x_ref[...].reshape(2 * Y * sources, width), 2)
    for part, value in ((0, re), (1, im)):
        start = base_ref[part, :, :, cols(q)].astype(f32)
        f_ref[part] = (value.reshape(Y, sources, part_width) + start).astype(bf16)

    lhs = f_ref[...].reshape(2 * Y * sources, part_width)
    n = Y * sources
    tile = Y * CORE * depth

    def d_copy(k, yy, j):
        spots = slice(j * tile, (j + 1) * tile)
        return remote(d_ref.at[:, yy, :, spots], far_ref.at[k].at[:, :, spots],
                      d_send.at[0], d_recv.at[j], dev(0, z, yy, core))

    def f_copy(yy):
        return remote(f_ref.at[:, yy], whole_ref.at[:, :, cols(q)], f_send.at[0],
                      f_recv.at[0], dev(last, z, yy, core))

    handed, direct = range(outer // 2), range(outer // 2, outer)

    def hand_copy(j):
        spots = slice(j * tile, (j + 1) * tile)
        return remote(d_ref.at[:, y_peer, :, spots], hand_ref.at[:, :, spots], d_send.at[0], hand_recv.at[j],
                      dev(plane, z, y_peer, core))

    for j in (direct[0], *handed, *direct[1:]):
        spots = slice(j * tile, (j + 1) * tile)
        dims = (((1,), (1,)), ((), ()))
        right = [g_ref[2, part, j * Y:(j + 1) * Y].reshape(tile, part_width) for part in range(2)]
        pr = lax.dot_general(lhs, right[0], dims, preferred_element_type=f32)
        pi = lax.dot_general(lhs, right[1], dims, preferred_element_type=f32)
        d_ref[0, :, :, spots] = (pr[:n] - pi[n:]).astype(bf16).reshape(Y, sources, tile)
        d_ref[1, :, :, spots] = (pi[:n] + pr[n:]).astype(bf16).reshape(Y, sources, tile)

        @pl.when(plane == last)
        def _():
            if j in handed:
                hand_copy(j).start()
            else:
                d_copy(2, y_peer, j).start()
                d_copy(0, y, j).start()

        @pl.when(plane != last)
        def _():
            d_copy(1, y_peer, j).start()

    @pl.when(plane == last)
    def _():
        f_copy(y_peer).start()
        for j in handed:
            spots = slice(j * tile, (j + 1) * tile)
            got(hand_ref.at[:, :, spots], hand_recv.at[j])
            for part in range(2):
                d_ref[part, y, :, spots] = (d_ref[part, y, :, spots].astype(f32)
                                            + hand_ref[part, :, spots].astype(f32)).astype(bf16)
            d_copy(0, y, j).start()

    @pl.when(plane != last)
    def _():
        f_copy(y_peer).start()
        f_copy(y).start()

    @pl.when(plane == last)
    def _():
        sent(r_hbm.at[0, :, :, 0:6 * part_width], in_send.at[0])
        sent(left_ref, left_send.at[0])

    @pl.when(plane != last)
    def _():
        sent(left_ref.at[:, 0], left_send.at[0])

    x_swap(y).wait_send()
    base_swap(y, plane * Y + y_peer).wait_send()
    sent(coup_ref.at[:, :, 0:trio], c_send.at[0])
    sent(g_ref.at[:, :, :, 0], core_send.at[0])
    for zz in range(outer):
        count = sum(0 <= zz + s < outer for s in reach)
        hops = (max(zz - 1, 0) + max(outer - 2 - zz, 0)) * (0 < zz < outer - 1)

        @pl.when(z == zz)
        def _():
            sent(g_ref.at[:, :, 0:Y * count, 0], z_send.at[0])
            if hops:
                sent(g_ref.at[:, :, 0:Y * hops, 0], relay_send.at[0])

    @pl.when(plane == last)
    def _():
        whole_ref[:, :, cols(q)] = f_ref[:, y]
        got(whole_ref.at[:, :, 0:trio], f_recv.at[0])
        for part in range(2):
            out_ref[:, part * width:(part + 1) * width] = whole_ref[part].astype(f32)
        sent(d_ref, d_send.at[0])
        sent(f_ref.at[:, 0], f_send.at[0])

    @pl.when(plane != last)
    def _():
        for j in (*direct, *handed):
            spots = slice(j * tile, (j + 1) * tile)
            count = len(others) - (j in handed)
            got(far_ref.at[0:count, :, :, spots], d_recv.at[j])
            for part in range(2):
                total = d_ref.at[part][y, :, spots].astype(f32)
                for k in range(count):
                    total = total + far_ref[k, part, :, spots].astype(f32)
                out_ref[:, part * width + j * tile:part * width + (j + 1) * tile] = (
                    x_ref.at[part][y, :, spots].astype(f32) + total.astype(bf16).astype(f32))
        sent(d_ref.at[:, 0], d_send.at[0])
        sent(f_ref, f_send.at[0])


def pair_body(transmit, reflect, source_amp, source_cell, source_slab):
    outer = lax.axis_size("blk") // (Y * CORE)
    sources, double = source_amp.shape
    depth = transmit.shape[1]
    width = double // 2
    quarter = width // (PLANES * Y)
    bf16 = jnp.bfloat16
    hbm = pl.BlockSpec(memory_space=pltpu.HBM)
    sem = pltpu.SemaphoreType.DMA
    out = pl.pallas_call(
        functools.partial(pair_kernel, outer),
        out_shape=pltpu.VMEM((sources, double), jnp.float32),
        in_specs=[hbm] * 5,
        out_specs=pl.BlockSpec(memory_space=pltpu.VMEM),
        scratch_shapes=[
            pltpu.VMEM((sources, double), bf16),
            pltpu.VMEM((1, sources), jnp.int32),
            pltpu.VMEM((1, sources), jnp.int32),
            pltpu.VMEM((3, 2, outer * Y, CORE, depth, quarter), bf16),
            pltpu.VMEM((2, Y, depth, width), bf16),
            pltpu.VMEM((SPLIT, 2 * Y * depth // SPLIT, width), bf16),
            pltpu.VMEM((2, Y, sources, width), bf16),
            pltpu.VMEM((2, Y, sources, width), bf16),
            pltpu.VMEM((2, Y, sources, quarter), bf16),
            pltpu.VMEM((2, sources, width), bf16),
            pltpu.VMEM((2, Y, sources, width), bf16),
            pltpu.VMEM((PLANES * Y - 1, 2, sources, width), bf16),
            pltpu.VMEM((2, sources, width), bf16),
            pltpu.SemaphoreType.REGULAR((2,)),
            sem((3,)),
            sem((1,)),
            sem((2 * Y + 1,)),
            sem((1,)),
            sem((5,)),
            sem((1,)),
            sem(((outer - 1) * (2 * Y + SPLIT),)),
            sem((1,)),
            sem((1,)),
            sem((3,)),
            sem((1,)),
            sem((SPLIT,)),
            sem((2,)),
            sem((2,)),
            sem((1,)),
            sem((1,)),
            sem((1,)),
            sem((outer,)),
            sem((outer // 2,)),
        ],
        compiler_params=pltpu.CompilerParams(
            collective_id=0, has_side_effects=True, vmem_limit_bytes=32 << 20),
    )(*(pltpu.with_memory_space_constraint(a, pltpu.HBM) for a in (
        transmit, reflect, source_amp, source_cell[None], source_slab[None])))
    return out[None]


def solution(mesh):
    pair = mesh.shape["slab"] == PLANES and mesh.shape["blk"] % (Y * CORE) == 0 and mesh.shape["blk"] > 2 * Y * CORE
    return jax.shard_map(
        pair_body if pair else body,
        mesh=mesh,
        in_specs=(
            P("slab", "blk", None),
            P("slab", None, "blk", None),
            P("blk", None),
            P("blk"),
            P("blk"),
        ),
        out_specs=P("slab", "blk", None),
        check_vma=False,
    )
```
